128 devices in a mesh: tm: 16 (over x, y), bl: 8 (over z, core).
Axes of the slice: x: 4, y: 4, z: 4, core: 2. Of those that a mesh axis runs over, the one named last changes fastest.
Arguments:
- visibilities: bfloat16 [65536, 2, 240], P(('tm', 'bl')), may hold values from -12 to 12
- noise_weight: float32 [65536], P(('tm', 'bl')), may hold values from 0.005 to 0.05
- keep_flag: int32 [65536], P(('tm', 'bl')), may hold values 0 or 1
- station_pairs: int32 [2, 65536], P(None, ('tm', 'bl')), may hold values from 0 to 63, as said below
- tile_owner: int32 [65536, 1], P(('tm', 'bl')), may hold values from 0 to 127; in each aligned block of 512 rows (0 to 511, 512 to 1023, ...) at most 8 rows name the same one
- tile_offset: int32 [65536], P(('tm', 'bl')), may hold values from 0 to 32760
- kernel_taps: float32 [8, 65536], P(None, ('tm', 'bl')), may hold values from 0.1 to 1
- gain_field: float32 [16, 64, 8, 2, 240], P('tm', 'bl'), may hold values from 0.25 to 1.75
- sky_grid: float32 [2, 8, 2, 4194304], P(None, None, None, ('tm', 'bl')), may hold values from -4 to 4
Outputs:
- gain_gradient: float32 [16, 64, 8, 2, 240], P('tm', 'bl')
- grid_gradient: float32 [2, 8, 2, 4194304], P(None, None, None, ('tm', 'bl'))
The draws below stay inside these ranges and needn't reach their ends.
Inputs may be any that keep to these rules, and one draw needn't show every extreme that they name: `station_pairs`: the two stations of a row differ. `tile_owner`: among the rows of one device no value appears more than 8 times, and in some device one appears exactly 8 times.
All inputs are finite; a program needn't handle non-finite values. No bound on the sum of `keep_flag` on one device may be relied on, other than what follows from the above.
Results may differ from the reference program's by a relative error of at most 0.0003.
Values sent between devices are 32-bit elements; how exact they have to be, the bound alone decides.
A program may use at most 128 MiB of HBM per device.

```python
import math
import jax
import jax.numpy as jnp
import numpy as np
from jax import lax

S = 64
F = 8
C = 240
NT = 2
KT = 8
GRID = 4194304
ROWS_DEV = 512
NSOL = 16
ROWS_SOL = 4096
ROWS = 65536
GRID_DEV = 32768
CAP = 8
N_TM = 16
DEVICES = 128


def draw_station_pairs(key, part):
    first_key, second_key = jax.random.split(jax.random.fold_in(key, 11))
    first_station = jax.random.randint(first_key, (ROWS,), 0, S)
    offset = jax.random.randint(second_key, (ROWS,), 1, S)
    second_station = (first_station + offset) % S
    return jnp.stack([first_station, second_station]).astype(jnp.int32)


def plant(drawn, key, least, top_value):
    shape = drawn.shape
    spot = [jax.random.randint(jax.random.fold_in(key, axis), (), 0, shape[axis]) for axis in range(len(shape))]
    drawn = drawn.at[tuple(spot)].set(least)
    longest = shape.index(max(shape))
    spot[longest] = (spot[longest] + 1) % shape[longest]
    return drawn.at[tuple(spot)].set(top_value)


def level_of(own_key, shape, pieces, low, top_value):
    def one(dim, parts):
        steps = jax.random.uniform(jax.random.fold_in(jax.random.fold_in(own_key, 6), dim), (parts,), jnp.float32, low / len(pieces), top_value / len(pieces))
        return jnp.repeat(jnp.exp(steps), shape[dim] // parts).reshape((-1,) + (1,) * (len(shape) - dim - 1))

    factor_of = one(*pieces[0])
    for cut in pieces[1:]:
        factor_of = factor_of * one(*cut)
    return factor_of


def deal_out(key, own, number, rows, amount, top, most, skew):
    sequence = jax.random.permutation(key, amount)
    packed, usual = load_shares(amount, rows * top, most, skew, True), load_shares(amount, rows * top, most, skew, False)
    places = jnp.arange(amount)

    def named(sizes, turn):
        used = int((sizes > 0).sum())
        fixed = max(1, used // 4)
        passed = fixed + (places - fixed + turn * (used - fixed)) % max(1, amount - fixed)
        return jnp.zeros((amount,), jnp.int32).at[sequence[jnp.where(places < fixed, places, passed)]].set(jnp.asarray(sizes, jnp.int32))

    sizes = jnp.where(number % 4 == 0, named(packed, number // 4), named(usual, number - number // 4 - 1))
    mixed = jax.random.permutation(jax.random.fold_in(own, 3), amount)
    source_of, taker = mixed[0:amount // 2 * 2:2], mixed[1:amount // 2 * 2:2]
    slack = jnp.minimum(sizes[source_of] - 1, most - sizes[taker]) // 2
    slack = jnp.where((source_of == sequence[0]) | (taker == sequence[0]) | (sizes[taker] == 0), 0, jnp.maximum(slack, 0))
    passed = jax.random.randint(jax.random.fold_in(own, 4), (amount // 2,), 0, 1 << 20) % (slack + 1)
    sizes = sizes.at[source_of].add(-passed).at[taker].add(passed)
    items = jnp.searchsorted(jnp.cumsum(sizes), jnp.arange(rows * top), side="right").astype(jnp.int32)
    table = items.reshape(top, rows).T
    table = table[jax.random.permutation(jax.random.fold_in(own, 1), rows)]
    turn = jax.random.randint(jax.random.fold_in(own, 2), (rows, 1), 0, top)
    return jnp.take_along_axis(table, (jnp.arange(top)[None, :] + turn) % top, axis=1)


def load_shares(number_of, total, limit, lean, full):
    portions = [(1 << 20) // math.isqrt(rank ** lean) + 1 for rank in range(1, number_of + 1)]
    largest = limit if full else min(limit, max(-(-total // number_of), total * portions[0] // sum(portions)))
    least = 1 if total - largest >= number_of - 1 else 0
    counts, surplus = [largest] + [least] * (number_of - 1), total - largest - least * (number_of - 1)
    while surplus > 0:
        free = [i for i in range(1, number_of) if counts[i] < largest] or [i for i in range(1, number_of) if counts[i] < limit]
        pool, left = sum([portions[i] for i in free]), surplus
        for i in free:
            addition = min(limit - counts[i], max(1, left * portions[i] // pool), surplus)
            counts[i] = counts[i] + addition
            surplus = surplus - addition
    return np.array(counts)


def bell_draw(own_key, shape, width, bound, cuts=(), held_as=jnp.bfloat16):
    values = jax.random.normal(own_key, shape, jnp.float32) * width
    if len(cuts) > 0:
        values = level_of(own_key, shape, cuts, -0.22, 0.18) * values
    return jnp.clip(values, min=-bound, max=bound).astype(held_as)


def setup_inputs(seed: int = 0) -> dict:
    key_of = jax.random.split(jax.random.key(seed), 10)
    visibilities = bell_draw(key_of[0], (ROWS, 2, C), 2.0, 12.0, ((0, 128),))
    noise_weight = jnp.clip(jnp.exp(math.log(0.05) - 2.3025851 * jax.random.uniform(key_of[1], (ROWS,), jnp.float32) ** level_of(key_of[1], (ROWS,), ((0, 128),), -0.2, 0.2)), 0.005, 0.05)
    keep_flag = plant((jax.random.randint(key_of[2], (ROWS,), 0, 10) < 9).astype(jnp.int32), jax.random.fold_in(key_of[2], 1), 0, 1)
    station_pairs = draw_station_pairs(jax.random.fold_in(key_of[9], 71), 0)
    tile_owner_keys = jax.random.split(jax.random.fold_in(key_of[4], 1), ROWS // ROWS_DEV)
    tile_owner_turns = jax.random.permutation(jax.random.fold_in(key_of[4], 3), ROWS // ROWS_DEV)
    tile_owner = jax.vmap(lambda own, number: deal_out(jax.random.fold_in(key_of[4], 2), own, number, ROWS_DEV, DEVICES, 1, CAP, 2))(tile_owner_keys, tile_owner_turns).reshape((ROWS, 1))
    tile_offset = plant(jax.random.randint(key_of[5], (ROWS,), 0, GRID_DEV - KT + 1), jax.random.fold_in(key_of[5], 1), 0, GRID_DEV - KT).astype(jnp.int32)
    kernel_taps = jnp.clip(0.1 + 0.9 * jax.random.uniform(key_of[6], (KT, ROWS), jnp.float32) ** level_of(key_of[6], (KT, ROWS), ((1, 128),), -0.2, 0.2), 0.1, 1.0)
    gain_field = jnp.clip(1.0 + 0.15 * jax.random.normal(key_of[7], (NSOL, S, F, 2, C), jnp.float32), 0.25, 1.75)
    sky_grid = bell_draw(key_of[8], (2, F, NT, GRID), 0.5, 4.0, ((3, 128),), jnp.float32)
    return dict(visibilities=visibilities, noise_weight=noise_weight, keep_flag=keep_flag, station_pairs=station_pairs, tile_owner=tile_owner, tile_offset=tile_offset, kernel_taps=kernel_taps, gain_field=gain_field, sky_grid=sky_grid)


smoothness = 4.0

def spectral_table(channels, spectral_terms):
    channel_ramp = 2.0 * jnp.arange(channels, dtype=jnp.float32) / (channels - 1) - 1.0
    powers = jnp.arange(spectral_terms, dtype=jnp.float32)
    return channel_ramp[None, :] ** powers[:, None]

def complex_mul(x_re, x_im, y_re, y_im):
    return (x_re * y_re - x_im * y_im, x_re * y_im + x_im * y_re)

def row_grads(visibilities, noise_weight, keep_flag, station_pairs, gains_all, degrid):
    row_count = visibilities.shape[0]
    stations = gains_all.shape[0]
    facets = gains_all.shape[1]
    channels = gains_all.shape[3]
    spectral_terms = degrid.shape[2]
    spectrum = spectral_table(channels, spectral_terms)
    first_station = station_pairs[0]
    second_station = station_pairs[1]
    observed = visibilities.astype(jnp.float32)
    scaling = (noise_weight * keep_flag.astype(jnp.float32))[:, None, None]
    onehot_first = (jnp.arange(stations, dtype=jnp.int32)[:, None] == first_station[None, :]).astype(jnp.float32)
    onehot_second = (jnp.arange(stations, dtype=jnp.int32)[:, None] == second_station[None, :]).astype(jnp.float32)

    def facet_parts(facet_index):
        gain_slab = lax.dynamic_index_in_dim(gains_all, facet_index, 1, keepdims=False)
        left_gain = jnp.take(gain_slab, first_station, axis=0)
        right_gain = jnp.take(gain_slab, second_station, axis=0)
        degrid_slab = lax.dynamic_index_in_dim(degrid, facet_index, 1, keepdims=False)
        facet_model = jnp.einsum('xtr,tc->xrc', degrid_slab, spectrum, precision=lax.Precision.HIGHEST)
        return (left_gain, right_gain, facet_model)

    def add_model(facet_index, running):
        left_gain, right_gain, facet_model = facet_parts(facet_index)
        pair_re, pair_im = complex_mul(left_gain[:, 0], left_gain[:, 1], right_gain[:, 0], -right_gain[:, 1])
        vis_re, vis_im = complex_mul(pair_re, pair_im, facet_model[0], facet_model[1])
        return running + jnp.stack([vis_re, vis_im], axis=1)
    predicted = lax.fori_loop(0, facets, add_model, jnp.zeros((row_count, 2, channels), jnp.float32))
    error = scaling * (observed - predicted)
    err_re = error[:, 0]
    err_im = error[:, 1]

    def add_grads(facet_index, accums):
        gain_acc, degrid_acc = accums
        left_gain, right_gain, facet_model = facet_parts(facet_index)
        left_re, left_im = (left_gain[:, 0], left_gain[:, 1])
        right_re, right_im = (right_gain[:, 0], right_gain[:, 1])
        model_re, model_im = (facet_model[0], facet_model[1])
        first_re, first_im = complex_mul(err_re, err_im, right_re, right_im)
        grad_are, grad_aim = complex_mul(first_re, first_im, model_re, -model_im)
        second_re, second_im = complex_mul(err_re, -err_im, left_re, left_im)
        grad_bre, grad_bim = complex_mul(second_re, second_im, model_re, model_im)
        third_re, third_im = complex_mul(err_re, err_im, left_re, -left_im)
        grad_mre, grad_mim = complex_mul(third_re, third_im, right_re, right_im)
        grad_left = -jnp.stack([grad_are, grad_aim], axis=1).reshape(row_count, 2 * channels)
        grad_right = -jnp.stack([grad_bre, grad_bim], axis=1).reshape(row_count, 2 * channels)
        per_station = jnp.dot(onehot_first, grad_left, precision=lax.Precision.HIGHEST)
        per_station = per_station + jnp.dot(onehot_second, grad_right, precision=lax.Precision.HIGHEST)
        gain_acc = lax.dynamic_update_index_in_dim(gain_acc, per_station.reshape(stations, 2, channels), facet_index, 1)
        grad_model = -jnp.stack([grad_mre, grad_mim], axis=0)
        grad_degrid = jnp.einsum('xrc,tc->xtr', grad_model, spectrum, precision=lax.Precision.HIGHEST)
        degrid_acc = lax.dynamic_update_index_in_dim(degrid_acc, grad_degrid, facet_index, 1)
        return (gain_acc, degrid_acc)
    initial = (jnp.zeros((stations, facets, 2, channels), jnp.float32), jnp.zeros((2, facets, spectral_terms, row_count), jnp.float32))
    return lax.fori_loop(0, facets, add_grads, initial)

def smooth_grad(gain_block):
    step_diff = gain_block[1:] - gain_block[:-1]
    from_below = jnp.pad(step_diff, ((1, 0), (0, 0), (0, 0), (0, 0), (0, 0)))
    from_above = jnp.pad(step_diff, ((0, 1), (0, 0), (0, 0), (0, 0), (0, 0)))
    return smoothness * (from_below - from_above)

def reference(visibilities, noise_weight, keep_flag, station_pairs, tile_owner, tile_offset, kernel_taps, gain_field, sky_grid):
    rows_block = ROWS_SOL
    taps_count = kernel_taps.shape[0]
    tile_start = (tile_owner[:, 0] * GRID_DEV + tile_offset).astype(jnp.int32)

    def per_time(grid_sum, block_index):
        begin = (block_index * rows_block).astype(jnp.int32)
        vis_rows = lax.dynamic_slice_in_dim(visibilities, begin, rows_block, 0)
        weight_rows = lax.dynamic_slice_in_dim(noise_weight, begin, rows_block, 0)
        keep_rows = lax.dynamic_slice_in_dim(keep_flag, begin, rows_block, 0)
        pair_rows = lax.dynamic_slice_in_dim(station_pairs, begin, rows_block, 1)
        start_rows = lax.dynamic_slice_in_dim(tile_start, begin, rows_block, 0)
        tap_rows = lax.dynamic_slice_in_dim(kernel_taps, begin, rows_block, 1).T
        gains_here = lax.dynamic_index_in_dim(gain_field, block_index, 0, keepdims=False)
        cell_index = start_rows[:, None] + jnp.arange(taps_count, dtype=jnp.int32)[None, :]
        tiles = sky_grid[:, :, :, cell_index]
        degrid = lax.optimization_barrier(jnp.sum(tiles * tap_rows[None, None, None], axis=4))
        gain_part, grad_degrid = row_grads(vis_rows, weight_rows, keep_rows, pair_rows, gains_here, degrid)
        spread = grad_degrid[..., None] * tap_rows[None, None, None]
        grid_sum = grid_sum.at[:, :, :, cell_index].add(spread)
        return (grid_sum, gain_part)
    grid_gradient, data_gain = lax.scan(per_time, jnp.zeros(sky_grid.shape, jnp.float32), jnp.arange(N_TM, dtype=jnp.int32))
    gain_gradient = data_gain + smooth_grad(gain_field)
    return (gain_gradient, grid_gradient)
```

```python
import functools

import jax
import jax.numpy as jnp
from jax import lax
from jax.experimental import pallas as pl
from jax.experimental.pallas import tpu as pltpu
from jax.sharding import PartitionSpec as P

smoothness = 4.0
F32, BF16, I32 = jnp.float32, jnp.bfloat16, jnp.int32
LANES = 128
WORDS = 16
BLOCK = 512
STRIDE = LANES + 8
CHUNK = 16
VMEM_LIMIT = 56 << 20
NT = (((1,), (1,)), ((), ()))


def iota(shape, axis):
    return lax.broadcasted_iota(I32, shape, axis)


def halves(x):
    hi = x.astype(BF16)
    return hi, (x - hi.astype(F32)).astype(BF16)


def dot(x, y):
    return jnp.dot(x, y, preferred_element_type=F32)


def dot_nt(x, y):
    return lax.dot_general(x, y, NT, preferred_element_type=F32)


def ones_where(mask):
    return jnp.where(mask, 1.0, 0.0).astype(BF16)


def form_slots(owner_ref, offset_ref, taps_ref, place_ref, store_message):
    devices, rows = place_ref.shape[1:]
    hits = iota((devices, rows), 0) == owner_ref[...]
    earlier = ones_where(iota((rows, rows), 0) < iota((rows, rows), 1))
    counts = dot(ones_where(hits), earlier)
    rank = jnp.sum(jnp.where(hits, counts, 0.0), axis=0, keepdims=True)
    words = jnp.concatenate(
        [taps_ref[...], jnp.broadcast_to(offset_ref[...].astype(F32), (WORDS - 8, rows))], axis=0
    )
    hi, lo = halves(jnp.concatenate([words] * 8, axis=0))
    group = iota((devices, LANES), 1) // WORDS
    message = jnp.zeros((devices, LANES), F32)
    for j in range(8):
        place = ones_where(jnp.where(hits, rank, -1.0) == float(j))
        place_ref[j] = place
        message = jnp.where(group == j, dot_nt(place, hi) + dot_nt(place, lo), message)
    store_message(message)


def transpose_grid(stage_ref, cells_ref):
    blocks = stage_ref.shape[1] // 8

    @pl.loop(0, blocks)
    def _(b):
        tile = stage_ref[:, pl.ds(pl.multiple_of(b * 8, 8), 8), :].reshape(LANES, LANES)
        cells_ref[pl.ds(pl.multiple_of(b * STRIDE, 8), LANES), :] = tile.T

    quarter = (iota((8, LANES), 1) >> 1) & 3

    @pl.loop(0, blocks)
    def _(b):
        here = cells_ref[pl.ds(pl.multiple_of(b * STRIDE, 8), 8), :]
        after = cells_ref[pl.ds(pl.multiple_of(jnp.minimum(b + 1, blocks - 1) * STRIDE, 8), 8), :]
        pad = jnp.where(
            quarter < 3, pltpu.roll(here, LANES - 2, 1), pltpu.roll(after, 6, 1)
        )
        cells_ref[pl.ds(pl.multiple_of(b * STRIDE + LANES, 8), 8), :] = pad


def fold_table():
    a, b = iota((2 * LANES, LANES), 0) & (LANES - 1), iota((2 * LANES, LANES), 1)
    return ones_where(((a >> 3) == (b >> 3)) & ((a & 1) == (b & 1)))


def degrid_slots(offset_ref, words_ref, cells_ref, weight_ref, product_ref, store_value):
    sources = words_ref.shape[1]
    step = 4
    quarter = (iota((8, LANES), 1) >> 1) & 3

    @pl.loop(0, sources // step)
    def _(s0):
        first = s0 * step
        for j in range(8):
            taps = pltpu.roll(words_ref[j * WORDS : j * WORDS + 8, :], sources - first, 1)
            for i in range(step):
                offset = offset_ref[j, first + i]
                row = (offset >> 9) * STRIDE + (offset & (LANES - 1))
                lane = (offset >> 7) & 3
                weight = jnp.where(
                    quarter == lane, jnp.broadcast_to(taps[:, i : i + 1], (8, LANES)), 0.0
                )
                at = pl.ds(pl.multiple_of((first + i) * 64 + j * 8, 8), 8)
                weight_ref[at, :] = weight
                product_ref[at, :] = weight * cells_ref[pl.ds(row, 8), :]

    fold = fold_table()
    group = (iota((sources, LANES), 1) >> 1) & 3
    for h in range(2):
        value = jnp.zeros((sources, LANES), F32)
        for g in range(4):
            j = 4 * h + g
            total = product_ref[pl.ds(j * 8, sources, stride=64), :]
            for k in range(1, 8):
                total = total + product_ref[pl.ds(j * 8 + k, sources, stride=64), :]
            value = jnp.where(group == g, dot(jnp.concatenate(halves(total), axis=1), fold), value)
        store_value(h, value)


def gather_degrid(load_value, place_ref, part_ref, degrid_ref):
    sources = place_ref.shape[1]
    quarter = (iota((LANES, sources), 0) >> 1) & 3
    total = None
    for h in range(2):
        turned = load_value(h).T
        for pair in range(2):
            parts = [halves(jnp.where(quarter == g, turned, 0.0)) for g in (2 * pair, 2 * pair + 1)]
            j = 4 * h + 2 * pair
            place = place_ref[j : j + 2].reshape(2 * sources, place_ref.shape[2])
            for n in range(2):
                term = dot(jnp.concatenate([parts[0][n], parts[1][n]], axis=1), place)
                total = term if total is None else total + term
    for n in range(part_ref.shape[0]):
        tile = slice(n * LANES, (n + 1) * LANES)
        part_ref[n] = total[:, tile]
        for t in range(2):
            degrid_ref[t, :, tile] = sum(part_ref[n, pl.ds(2 * g + t, 16, stride=8), :] for g in range(4))


def station_tables(pairs_ref, gather_ref, sum_ref):
    rows = pairs_ref.shape[1]
    for side in range(2):
        hits = ((iota((LANES, rows), 0) & 63) == pairs_ref[side : side + 1, :]) * 1.0
        gather_ref[side] = hits.astype(BF16)
        turned = jnp.where(iota((rows, LANES), 1) < 64, hits.T, 0.0).astype(BF16)
        sum_ref[pl.ds(2 * side * rows, rows), :] = turned
        sum_ref[pl.ds((2 * side + 1) * rows, rows), :] = turned


def turn_gains(gains_ref, turned_ref):
    chunks = turned_ref.shape[0]
    for fc in range(16):
        tiles = []
        for lt in range(2):
            block = gains_ref[:, 2 * fc + lt, :]
            hi = block.astype(BF16).astype(F32)
            tiles.append(jnp.concatenate([hi, block - hi], axis=0).T)
        full = jnp.concatenate(tiles, axis=0)[: chunks * CHUNK].astype(BF16)
        turned_ref[:, fc // 2, fc % 2] = full.reshape(chunks, CHUNK, LANES)


def row_step(
    chunk, channels, vis_ref, scale_ref, degrid_ref, turned_ref, gather_ref, sum_ref,
    left_ref, right_ref, grads_ref, grad_degrid_ref, station_ref,
):
    facets = turned_ref.shape[1]
    rows = vis_ref.shape[2]
    gains = turned_ref[chunk].reshape(facets * 2 * CHUNK, LANES)
    left_ref[...] = dot(gains, gather_ref[0])
    right_ref[...] = dot(gains, gather_ref[1])
    channel = (iota((CHUNK, rows), 0) + chunk * CHUNK).astype(F32)
    ramp = 2.0 * channel / (channels - 1) - 1.0

    def parts(f):
        base = f * 2 * CHUNK
        re, im = slice(base, base + CHUNK), slice(base + CHUNK, base + 2 * CHUNK)
        model_re = degrid_ref[0, f : f + 1, :] + degrid_ref[1, f : f + 1, :] * ramp
        model_im = degrid_ref[0, facets + f : facets + f + 1, :] + degrid_ref[1, facets + f : facets + f + 1, :] * ramp
        return left_ref[re, :], left_ref[im, :], right_ref[re, :], right_ref[im, :], model_re, model_im

    pred_re = pred_im = None
    for f in range(facets):
        are, aim, bre, bim, mre, mim = parts(f)
        pre, pim = are * bre + aim * bim, aim * bre - are * bim
        vre, vim = pre * mre - pim * mim, pre * mim + pim * mre
        pred_re = vre if pred_re is None else pred_re + vre
        pred_im = vim if pred_im is None else pred_im + vim
    at = pl.ds(pl.multiple_of(chunk * CHUNK, CHUNK), CHUNK)
    ere = scale_ref[...] * (pred_re - vis_ref[0, at, :].astype(F32))
    eim = scale_ref[...] * (pred_im - vis_ref[1, at, :].astype(F32))
    for f in range(facets):
        are, aim, bre, bim, mre, mim = parts(f)
        base = f * 2 * CHUNK
        qre, qim = ere * mre + eim * mim, eim * mre - ere * mim
        values = (
            (qre * bre - qim * bim, qre * bim + qim * bre),
            (qre * are + qim * aim, qre * aim - qim * are),
        )
        for side in range(2):
            for c in range(2):
                hi, lo = halves(values[side][c])
                to = slice(base + c * CHUNK, base + (c + 1) * CHUNK)
                grads_ref[to, pl.ds(2 * side * rows, rows)] = hi
                grads_ref[to, pl.ds((2 * side + 1) * rows, rows)] = lo
        pre, pim = are * bre + aim * bim, aim * bre - are * bim
        models = (ere * pre + eim * pim, eim * pre - ere * pim)
        for c in range(2):
            n = c * facets + f
            slope = models[c] * ramp
            grad_degrid_ref[0, n] += models[c][:8] + models[c][8:]
            grad_degrid_ref[1, n] += slope[:8] + slope[8:]
    station_ref[chunk] = dot(grads_ref[...], sum_ref[...])


def place_grads(grad_degrid_ref, place_ref, store_value):
    planes = grad_degrid_ref.shape[1]
    rows = grad_degrid_ref.shape[3]
    devices = place_ref.shape[1]
    odd = (iota((8, rows), 0) & 1) == 1
    full = []
    for n in range(planes):
        level = jnp.sum(grad_degrid_ref[0, n], axis=0, keepdims=True)
        slope = jnp.sum(grad_degrid_ref[1, n], axis=0, keepdims=True)
        full.append(jnp.where(odd, slope, level))
    hi, lo = halves(jnp.concatenate(full, axis=0))
    group = (iota((devices, LANES), 1) >> 1) & 3
    for h in range(2):
        value = jnp.zeros((devices, LANES), F32)
        for g in range(4):
            place = place_ref[4 * h + g]
            value = jnp.where(group == g, dot_nt(place, hi) + dot_nt(place, lo), value)
        store_value(h, value)


def split_stations(station_ref, out_ref):
    chunks = station_ref.shape[0]
    for fc in range(16):
        block = station_ref[:, fc * CHUNK : (fc + 1) * CHUNK, :].reshape(chunks * CHUNK, LANES)
        block = jnp.concatenate([block, jnp.zeros((2 * LANES - chunks * CHUNK, LANES), F32)], axis=0)
        for lt in range(2):
            turned = block[lt * LANES : (lt + 1) * LANES].T
            out_ref[:, fc, :, pl.ds(lt * LANES, LANES)] = turned[:64].reshape(8, 8, LANES)


def form_kernel(owner_ref, offset_ref, taps_ref, place_ref, message_ref):
    def store(message):
        message_ref[...] = message

    form_slots(owner_ref, offset_ref, taps_ref, place_ref, store)


def degrid_kernel(offset_ref, message_ref, sky_ref, weight_ref, value_ref, stage, words, cells, product, sem):
    copy = pltpu.make_async_copy(sky_ref, stage, sem)
    copy.start()
    words[...] = message_ref[...].T
    copy.wait()
    transpose_grid(stage, cells)

    def store(h, value):
        value_ref[:, h, :] = value

    degrid_slots(offset_ref, words, cells, weight_ref, product, store)


def rows_kernel(
    value_ref, place_ref, gains_ref, vis_ref, noise_ref, keep_ref, pairs_ref,
    grad_ref, out_ref,
    part, degrid, turned, gather, sums, scale, left, right, grads, grad_degrid, station,
    channels,
):
    scale[...] = noise_ref[...] * keep_ref[...].astype(F32)
    station_tables(pairs_ref, gather, sums)
    turn_gains(gains_ref, turned)
    gather_degrid(lambda h: value_ref[:, h, :], place_ref, part, degrid)
    grad_degrid[...] = jnp.zeros_like(grad_degrid)

    @pl.loop(0, turned.shape[0])
    def _(chunk):
        row_step(
            chunk, channels, vis_ref, scale, degrid, turned, gather, sums,
            left, right, grads, grad_degrid, station,
        )

    def store(h, value):
        grad_ref[:, h, :] = value

    place_grads(grad_degrid, place_ref, store)
    split_stations(station, out_ref)


def scatter_kernel(offset_ref, weight_ref, grad_ref, sky_ref, spread, cells, stage, sem):
    sources = grad_ref.shape[0]
    blocks = stage.shape[1] // 8
    fold = fold_table()
    group = (iota((sources, LANES), 1) >> 1) & 3
    for h in range(2):
        block = grad_ref[:, h, :]
        for g in range(4):
            part = jnp.concatenate(halves(jnp.where(group == g, block, 0.0)), axis=1)
            spread[pl.ds(4 * h + g, sources, stride=8), :] = dot(part, fold)

    @pl.loop(0, blocks)
    def _(b):
        at = pl.ds(pl.multiple_of(b * STRIDE, 8), STRIDE)
        for n in range(2):
            cells[n, at, :] = jnp.zeros((STRIDE, LANES), F32)

    @pl.loop(0, sources)
    def _(s):
        for j in range(8):
            offset = offset_ref[j, s]
            row = (offset >> 9) * STRIDE + (offset & (LANES - 1))
            at = pl.ds(pl.multiple_of(s * 64 + j * 8, 8), 8)
            term = weight_ref[at, :] * spread[pl.ds(s * 8 + j, 1), :]
            cells[j % 2, pl.ds(row, 8), :] += term

    quarter = (iota((8, LANES), 1) >> 1) & 3

    @pl.loop(0, blocks)
    def _(b):
        at = pl.ds(pl.multiple_of(b * STRIDE, 8), LANES)
        tile = cells[0, at, :] + cells[1, at, :]
        pads = pl.ds(pl.multiple_of(b * STRIDE + LANES, 8), 8)
        before = pl.ds(pl.multiple_of(jnp.maximum(b - 1, 0) * STRIDE + LANES, 8), 8)
        here = pltpu.roll(cells[0, pads, :] + cells[1, pads, :], 2, 1)
        last = pltpu.roll(cells[0, before, :] + cells[1, before, :], LANES - 6, 1)
        last = jnp.where(b > 0, last, 0.0)
        head = tile[:8] + jnp.where(quarter > 0, here, last)
        turned = jnp.concatenate([head, tile[8:]], axis=0).T
        stage[:, pl.ds(pl.multiple_of(b * 8, 8), 8), :] = turned.reshape(16, 8, LANES)

    copy = pltpu.make_async_copy(stage, sky_ref, sem)
    copy.start()
    copy.wait()


def vmem(count):
    return [pl.BlockSpec(memory_space=pltpu.VMEM)] * count


def shape(dims, dtype=F32):
    return jax.ShapeDtypeStruct(dims, dtype)


def params():
    return pltpu.CompilerParams(vmem_limit_bytes=VMEM_LIMIT)


def body(
    visibilities, noise_weight, keep_flag, station_pairs, tile_owner, tile_offset, kernel_taps, gain_field, sky_grid
):
    rows = visibilities.shape[0]
    channels = visibilities.shape[2]
    devices = lax.axis_size("tm") * lax.axis_size("bl")
    chunks = channels // CHUNK
    parts, facets, terms, cells = sky_grid.shape
    lines = cells // LANES
    sky = sky_grid.reshape(parts, facets, terms, lines, LANES).transpose(0, 1, 3, 2, 4)
    sky = sky.reshape(parts * facets, lines * terms, LANES)

    place, message = pl.pallas_call(
        form_kernel,
        out_shape=(shape((8, devices, rows), BF16), shape((devices, LANES))),
        in_specs=vmem(3),
        out_specs=tuple(vmem(2)),
        compiler_params=params(),
        name="form",
    )(tile_owner.reshape(1, rows), tile_offset.reshape(1, rows), kernel_taps)
    got = lax.all_to_all(message, ("tm", "bl"), split_axis=0, concat_axis=0, tiled=True)
    offsets = got.reshape(devices, 8, WORDS)[:, :, 8].T.astype(I32)

    weight, value = pl.pallas_call(
        degrid_kernel,
        out_shape=(shape((devices * 64, LANES)), shape((devices, 2, LANES))),
        in_specs=[pl.BlockSpec(memory_space=pltpu.SMEM)] + vmem(1) + [pl.BlockSpec(memory_space=pl.ANY)],
        out_specs=tuple(vmem(2)),
        scratch_shapes=[
            pltpu.VMEM(sky.shape, F32),
            pltpu.VMEM((LANES, devices), F32),
            pltpu.VMEM((cells // BLOCK * STRIDE, LANES), F32),
            pltpu.VMEM((devices * 64, LANES), F32),
            pltpu.SemaphoreType.DMA,
        ],
        compiler_params=params(),
        name="degrid",
    )(offsets, got, sky)
    value = lax.all_to_all(value, ("tm", "bl"), split_axis=0, concat_axis=0, tiled=True)

    own = jnp.pad(gain_field[0], ((0, 0), (0, 0), (0, 0), (0, 2 * LANES - channels)))
    own = own.reshape(-1, facets * 4, LANES)
    gains = lax.all_gather(own, "bl", axis=0, tiled=True)
    grad, partial = pl.pallas_call(
        functools.partial(rows_kernel, channels=channels),
        out_shape=(shape((devices, 2, LANES)), shape((8, 16, 8, 2 * LANES))),
        in_specs=vmem(7),
        out_specs=tuple(vmem(2)),
        scratch_shapes=[
            pltpu.VMEM((rows // LANES, LANES, LANES), F32),
            pltpu.VMEM((2, 16, rows), F32),
            pltpu.VMEM((chunks, facets, 2, CHUNK, LANES), BF16),
            pltpu.VMEM((2, LANES, rows), BF16),
            pltpu.VMEM((4 * rows, LANES), BF16),
            pltpu.VMEM((1, rows), F32),
            pltpu.VMEM((facets * 2 * CHUNK, rows), F32),
            pltpu.VMEM((facets * 2 * CHUNK, rows), F32),
            pltpu.VMEM((facets * 2 * CHUNK, 4 * rows), BF16),
            pltpu.VMEM((2, 2 * facets, 8, rows), F32),
            pltpu.VMEM((chunks, facets * 2 * CHUNK, LANES), F32),
        ],
        compiler_params=params(),
        name="rows",
    )(
        value, place, gains, visibilities.transpose(1, 2, 0), noise_weight.reshape(1, rows),
        keep_flag.reshape(1, rows), station_pairs,
    )
    grad = lax.all_to_all(grad, ("tm", "bl"), split_axis=0, concat_axis=0, tiled=True)
    data = lax.psum_scatter(partial, "bl", scatter_dimension=0, tiled=False)

    out_grid = pl.pallas_call(
        scatter_kernel,
        out_shape=shape(sky.shape),
        in_specs=[pl.BlockSpec(memory_space=pltpu.SMEM)] + vmem(2),
        out_specs=pl.BlockSpec(memory_space=pl.ANY),
        scratch_shapes=[
            pltpu.VMEM((devices * 8, LANES), F32),
            pltpu.VMEM((2, cells // BLOCK * STRIDE, LANES), F32),
            pltpu.VMEM(sky.shape, F32),
            pltpu.SemaphoreType.DMA,
        ],
        compiler_params=params(),
        name="scatter",
    )(offsets, weight, grad)
    grid_gradient = out_grid.reshape(parts, facets, lines, terms, LANES).transpose(0, 1, 3, 2, 4)
    grid_gradient = grid_gradient.reshape(sky_grid.shape)

    times = lax.axis_size("tm")
    below = lax.ppermute(gain_field, "tm", [(i, i + 1) for i in range(times - 1)])
    above = lax.ppermute(gain_field, "tm", [(i + 1, i) for i in range(times - 1)])
    here = lax.axis_index("tm")
    smooth = jnp.where(here > 0, gain_field - below, 0.0) - jnp.where(here < times - 1, above - gain_field, 0.0)
    data = data.reshape(facets, 2, 8, 2 * LANES).transpose(2, 0, 1, 3)[None, :, :, :, :channels]
    return (data + smoothness * smooth, grid_gradient)


def solution(mesh):
    split = ("tm", "bl")
    return jax.shard_map(
        body,
        mesh=mesh,
        in_specs=(
            P(split, None, None),
            P(split),
            P(split),
            P(None, split),
            P(split, None),
            P(split),
            P(None, split),
            P("tm", "bl", None, None, None),
            P(None, None, None, split),
        ),
        out_specs=(P("tm", "bl", None, None, None), P(None, None, None, split)),
        check_vma=False,
    )
```

```python
import functools

import jax
import jax.numpy as jnp
from jax import lax
from jax.experimental import pallas as pl
from jax.experimental.pallas import tpu as pltpu
from jax.sharding import PartitionSpec as P

smoothness = 4.0
F32, BF16, I32 = jnp.float32, jnp.bfloat16, jnp.int32
LANES = 128
WORDS = 16
BLOCK = 512
STRIDE = LANES + 8
CHUNK = 16
VMEM_LIMIT = 56 << 20
NT = (((1,), (1,)), ((), ()))


def iota(shape, axis):
    return lax.broadcasted_iota(I32, shape, axis)


def halves(x):
    hi = x.astype(BF16)
    return hi, (x - hi.astype(F32)).astype(BF16)


def dot(x, y):
    return jnp.dot(x, y, preferred_element_type=F32)


def dot_nt(x, y):
    return lax.dot_general(x, y, NT, preferred_element_type=F32)


def ones_where(mask):
    return jnp.where(mask, 1.0, 0.0).astype(BF16)


def form_slots(owner_ref, offset_ref, taps_ref, place_ref, store_message):
    devices, rows = place_ref.shape[1:]
    hits = iota((devices, rows), 0) == owner_ref[...]
    earlier = ones_where(iota((rows, rows), 0) < iota((rows, rows), 1))
    counts = dot(ones_where(hits), earlier)
    rank = jnp.sum(jnp.where(hits, counts, 0.0), axis=0, keepdims=True)
    offset = offset_ref[...]
    row = (offset >> 9) * STRIDE + (offset & (LANES - 1))
    tail = jnp.where(iota((WORDS - 8, rows), 0) == 0, row, (offset >> 7) & 3).astype(F32)
    words = jnp.concatenate([taps_ref[...], tail], axis=0)
    hi, lo = halves(jnp.concatenate([words] * 8, axis=0))
    group = iota((devices, LANES), 1) // WORDS
    message = jnp.zeros((devices, LANES), F32)
    for j in range(8):
        place = ones_where(jnp.where(hits, rank, -1.0) == float(j))
        place_ref[j] = place
        message = jnp.where(group == j, dot_nt(place, hi) + dot_nt(place, lo), message)
    store_message(message)


def transpose_grid(stage_ref, cells_ref):
    blocks = stage_ref.shape[1] // 8

    @pl.loop(0, blocks, unroll=8)
    def _(b):
        tile = stage_ref[:, pl.ds(pl.multiple_of(b * 8, 8), 8), :].reshape(LANES, LANES)
        cells_ref[pl.ds(pl.multiple_of(b * STRIDE, 8), LANES), :] = tile.T

    quarter = (iota((8, LANES), 1) >> 1) & 3
    for b in range(blocks):
        here = cells_ref[b * STRIDE : b * STRIDE + 8, :]
        next_block = min(b + 1, blocks - 1) * STRIDE
        after = cells_ref[next_block : next_block + 8, :]
        pad = jnp.where(quarter < 3, pltpu.roll(here, LANES - 2, 1), pltpu.roll(after, 6, 1))
        cells_ref[b * STRIDE + LANES : (b + 1) * STRIDE, :] = pad


def spread_taps(words_ref, weight_ref):
    sources = words_ref.shape[0]
    tall = jnp.broadcast_to(words_ref[...].reshape(sources, 1, LANES), (sources, 8, LANES)).reshape(8 * sources, LANES)
    tall = jnp.where((iota(tall.shape, 1) & (WORDS - 1)) == (iota(tall.shape, 0) & 7), tall, 0.0)
    both = jnp.concatenate(halves(tall), axis=1)
    for pair in range(4):
        a, b = iota((2 * LANES, 2 * LANES), 0) & (LANES - 1), iota((2 * LANES, 2 * LANES), 1)
        weight = dot(both, ones_where(a // WORDS == 2 * pair + b // LANES))
        for n in range(2):
            weight_ref[2 * pair + n] = weight[:, n * LANES : (n + 1) * LANES]


def slot_quarter(words_ref, j):
    return jnp.broadcast_to(words_ref[:, j * WORDS + 9 : j * WORDS + 10], (words_ref.shape[0], LANES))


def fold_table():
    a, b = iota((2 * LANES, LANES), 0) & (LANES - 1), iota((2 * LANES, LANES), 1)
    return ones_where(((a >> 3) == (b >> 3)) & ((a & 1) == (b & 1)))


def degrid_slots(first_ref, words_ref, cells_ref, weight_ref, product_ref, store_value):
    sources = words_ref.shape[0]

    @pl.loop(0, sources, unroll=2)
    def _(s):
        at = pl.ds(pl.multiple_of(s * 8, 8), 8)
        for j in range(8):
            product_ref[j, at, :] = weight_ref[j, at, :] * cells_ref[pl.ds(first_ref[j, s], 8), :]

    fold = fold_table()
    lane_quarter = (iota((sources, LANES), 1) >> 1) & 3
    for h in range(2):
        value = jnp.zeros((sources, LANES), F32)
        for g in range(4):
            j = 4 * h + g
            total = product_ref[j, pl.ds(0, sources, stride=8), :]
            for k in range(1, 8):
                total = total + product_ref[j, pl.ds(k, sources, stride=8), :]
            total = jnp.where(slot_quarter(words_ref, j) == lane_quarter.astype(F32), total, 0.0)
            value = jnp.where(lane_quarter == g, dot(jnp.concatenate(halves(total), axis=1), fold), value)
        store_value(h, value)


def gather_degrid(load_value, place_ref, part_ref, degrid_ref):
    sources = place_ref.shape[1]
    quarter = (iota((LANES, sources), 0) >> 1) & 3
    total = None
    for h in range(2):
        turned = load_value(h).T
        for pair in range(2):
            parts = [halves(jnp.where(quarter == g, turned, 0.0)) for g in (2 * pair, 2 * pair + 1)]
            j = 4 * h + 2 * pair
            place = place_ref[j : j + 2].reshape(2 * sources, place_ref.shape[2])
            for n in range(2):
                term = dot(jnp.concatenate([parts[0][n], parts[1][n]], axis=1), place)
                total = term if total is None else total + term
    for n in range(part_ref.shape[0]):
        tile = slice(n * LANES, (n + 1) * LANES)
        part_ref[n] = total[:, tile]
        for t in range(2):
            degrid_ref[t, :, tile] = sum(part_ref[n, pl.ds(2 * g + t, 16, stride=8), :] for g in range(4))


def station_tables(pairs_ref, gather_ref, sum_ref):
    rows = pairs_ref.shape[1]
    for side in range(2):
        hits = ones_where((iota((LANES, rows), 0) & 63) == pairs_ref[side : side + 1, :])
        gather_ref[side] = hits
        for n in range(2):
            sum_ref[:, (2 * side + n) * rows : (2 * side + n + 1) * rows] = hits[:64]


def turn_gains(gains_ref, turned_ref, channels):
    for fc in range(16):
        tiles = []
        for lt in range(2):
            block = gains_ref[:, 2 * fc + lt, :]
            hi = block.astype(BF16).astype(F32)
            tiles.append(jnp.concatenate([hi, block - hi], axis=0).T)
        turned_ref[fc * channels : (fc + 1) * channels] = jnp.concatenate(tiles, axis=0)[:channels].astype(BF16)


def gather_gains(turned_ref, gather_ref, left_ref, right_ref):
    size = turned_ref.shape[0] // 3

    @pl.loop(0, 3)
    def _(n):
        at = pl.ds(pl.multiple_of(n * size, CHUNK), size)
        gains = turned_ref[at, :]
        left_ref[at, :] = dot(gains, gather_ref[0])
        right_ref[at, :] = dot(gains, gather_ref[1])


def row_step(chunk, channels, vis_ref, scale_ref, degrid_ref, left_ref, right_ref, grads_ref, grad_degrid_ref):
    rows = vis_ref.shape[2]
    facets = left_ref.shape[0] // channels // 2
    width = 2 * LANES

    def rows_of(n):
        return pl.ds(pl.multiple_of(n * channels + chunk * CHUNK, CHUNK), CHUNK)

    at = rows_of(0)
    channel = (iota((CHUNK, width), 0) + chunk * CHUNK).astype(F32)
    ramp = 2.0 * channel / (channels - 1) - 1.0
    for lanes in range(rows // width):
        ln = slice(lanes * width, (lanes + 1) * width)

        def parts(f):
            re, im = rows_of(2 * f), rows_of(2 * f + 1)
            g = facets + f
            mre = degrid_ref[0, f : f + 1, ln] + degrid_ref[1, f : f + 1, ln] * ramp
            mim = degrid_ref[0, g : g + 1, ln] + degrid_ref[1, g : g + 1, ln] * ramp
            return left_ref[re, ln], left_ref[im, ln], right_ref[re, ln], right_ref[im, ln], mre, mim

        pred_re = pred_im = None
        for f in range(facets):
            are, aim, bre, bim, mre, mim = parts(f)
            pre, pim = are * bre + aim * bim, aim * bre - are * bim
            vre, vim = pre * mre - pim * mim, pre * mim + pim * mre
            pred_re = vre if pred_re is None else pred_re + vre
            pred_im = vim if pred_im is None else pred_im + vim
        ere = scale_ref[:, ln] * (pred_re - vis_ref[0, at, ln].astype(F32))
        eim = scale_ref[:, ln] * (pred_im - vis_ref[1, at, ln].astype(F32))
        for f in range(facets):
            are, aim, bre, bim, mre, mim = parts(f)
            qre, qim = ere * mre + eim * mim, eim * mre - ere * mim
            values = (
                (qre * bre - qim * bim, qre * bim + qim * bre),
                (qre * are + qim * aim, qre * aim - qim * are),
            )
            for side in range(2):
                for c in range(2):
                    hi, lo = halves(values[side][c])
                    first = 2 * side * rows + lanes * width
                    grads_ref[rows_of(2 * f + c), first : first + width] = hi
                    grads_ref[rows_of(2 * f + c), first + rows : first + rows + width] = lo
            pre, pim = are * bre + aim * bim, aim * bre - are * bim
            models = (ere * pre + eim * pim, eim * pre - ere * pim)
            for c in range(2):
                n = c * facets + f
                slope = models[c] * ramp
                grad_degrid_ref[0, n, :, ln] += models[c][:8] + models[c][8:]
                grad_degrid_ref[1, n, :, ln] += slope[:8] + slope[8:]


def place_grads(grad_degrid_ref, place_ref, store_value):
    planes = grad_degrid_ref.shape[1]
    rows = grad_degrid_ref.shape[3]
    devices = place_ref.shape[1]
    odd = (iota((8, rows), 0) & 1) == 1
    full = []
    for n in range(planes):
        level = jnp.sum(grad_degrid_ref[0, n], axis=0, keepdims=True)
        slope = jnp.sum(grad_degrid_ref[1, n], axis=0, keepdims=True)
        full.append(jnp.where(odd, slope, level))
    hi, lo = halves(jnp.concatenate(full, axis=0))
    group = (iota((devices, LANES), 1) >> 1) & 3
    for h in range(2):
        value = jnp.zeros((devices, LANES), F32)
        for g in range(4):
            place = place_ref[4 * h + g]
            value = jnp.where(group == g, dot_nt(place, hi) + dot_nt(place, lo), value)
        store_value(h, value)


class Exchange:
    def __init__(self, send_ref, receive_ref, sems):
        self.send_ref, self.receive_ref, self.sems = send_ref, receive_ref, sems

    def own(self, me):
        return pltpu.make_async_copy(self.send_ref.at[me], self.receive_ref.at[me], self.sems.at[1])

    def start(self, me, groups):
        devices = self.send_ref.shape[0]
        self.own(me).start()

        @pl.loop(1, devices)
        def _(n):
            to = lax.rem(me + n, devices)
            pltpu.make_async_remote_copy(
                src_ref=self.send_ref.at[to],
                dst_ref=self.receive_ref.at[me],
                send_sem=self.sems.at[0],
                recv_sem=self.sems.at[1],
                device_id=(to // groups, lax.rem(to, groups)),
                device_id_type=pl.DeviceIdType.MESH,
            ).start()

    def wait_receive(self):
        pltpu.make_async_copy(self.receive_ref, self.receive_ref, self.sems.at[1]).wait()

    def wait_send(self):
        others = pl.ds(0, self.send_ref.shape[0] - 1)
        pltpu.make_async_copy(self.send_ref.at[others], self.send_ref.at[others], self.sems.at[0]).wait()


def main_kernel(
    owner_ref, offset_ref, taps_ref, own_ref, vis_ref, noise_ref, keep_ref, pairs_ref, sky_ref,
    words_ref, firsts_ref, grad_ref, data_ref,
    send_a, got_a, send_c, got_c, send_e, got_e, gains, send_g, got_g, near,
    place, stage, cells, weight, product, slots, part, degrid, turned, gather, sums, scale,
    left, right, grads, grad_degrid,
    sky_sem, slot_sem, sem_a, sem_c, sem_e, gain_sem, near_sem, sum_sem,
    channels, times, groups,
):
    time, group = lax.axis_index("tm"), lax.axis_index("bl")
    devices = times * groups
    me = time * groups + group
    barrier = pltpu.get_barrier_semaphore()

    @pl.loop(1, devices)
    def _(n):
        to = lax.rem(me + n, devices)
        pl.semaphore_signal(
            barrier, inc=1, device_id=(to // groups, lax.rem(to, groups)), device_id_type=pl.DeviceIdType.MESH
        )

    sky_copy = pltpu.make_async_copy(sky_ref, stage, sky_sem)
    sky_copy.start()

    def store_message(message):
        for t in range(devices):
            send_a[t] = message[t : t + 1, :]

    form_slots(owner_ref, offset_ref, taps_ref, place, store_message)
    pl.semaphore_wait(barrier, devices - 1)

    first = Exchange(send_a, got_a, sem_a)
    first.start(me, groups)

    mine = gains.at[pl.ds(group * 8, 8)]
    pltpu.make_async_copy(own_ref, mine, gain_sem.at[1]).start()

    @pl.loop(1, groups)
    def _(n):
        pltpu.make_async_remote_copy(
            src_ref=own_ref, dst_ref=mine, send_sem=gain_sem.at[0], recv_sem=gain_sem.at[1],
            device_id=(time, lax.rem(group + n, groups)), device_id_type=pl.DeviceIdType.MESH,
        ).start()

    def pass_on(n, step):
        return pltpu.make_async_remote_copy(
            src_ref=own_ref, dst_ref=near.at[n], send_sem=near_sem.at[2 * n], recv_sem=near_sem.at[2 * n + 1],
            device_id=(lax.rem(time + step, times), group), device_id_type=pl.DeviceIdType.MESH,
        )

    below, above = pass_on(0, 1), pass_on(1, times - 1)
    below.start()
    above.start()

    sky_copy.wait()
    transpose_grid(stage, cells)
    scale[...] = noise_ref[...] * keep_ref[...].astype(F32)
    station_tables(pairs_ref, gather, sums)
    grad_degrid[...] = jnp.zeros_like(grad_degrid)

    first.wait_receive()
    words_ref[...] = got_a[...].reshape(devices, LANES)
    turned_words = words_ref[...].T
    firsts = jnp.concatenate([turned_words[j * WORDS + 8 : j * WORDS + 9, :] for j in range(8)], axis=0)
    firsts_ref[...] = jnp.clip(firsts.astype(I32), 0, cells.shape[0] - 8)
    slot_copy = pltpu.make_async_copy(firsts_ref, slots, slot_sem)
    slot_copy.start()
    spread_taps(words_ref, weight)
    slot_copy.wait()

    def store_value(h, value):
        send_c[:, h, :] = value

    degrid_slots(slots, words_ref, cells, weight, product, store_value)
    second = Exchange(send_c, got_c, sem_c)
    second.start(me, groups)

    pltpu.make_async_copy(gains, gains, gain_sem.at[1]).wait()
    turn_gains(gains, turned, channels)
    gather_gains(turned, gather, left, right)

    second.wait_receive()
    gather_degrid(lambda h: got_c[:, h, :], place, part, degrid)

    @pl.loop(0, channels // CHUNK)
    def _(chunk):
        row_step(chunk, channels, vis_ref, scale, degrid, left, right, grads, grad_degrid)

    def store_grad(h, value):
        send_e[:, h, :] = value

    place_grads(grad_degrid, place, store_grad)
    third = Exchange(send_e, got_e, sem_e)
    third.start(me, groups)

    def to_peer(n, fc):
        to = lax.rem(group + n, groups)
        return pltpu.make_async_remote_copy(
            src_ref=send_g.at[fc, pl.ds(to * 8, 8)], dst_ref=got_g.at[group, fc],
            send_sem=sum_sem.at[0], recv_sem=sum_sem.at[1],
            device_id=(time, to), device_id_type=pl.DeviceIdType.MESH,
        )

    @pl.loop(0, 16)
    def _(fc):
        sums_here = dot_nt(sums[...], grads[pl.ds(pl.multiple_of(fc * channels, CHUNK), channels), :])
        send_g[fc] = jnp.concatenate([sums_here, jnp.zeros((64, 2 * LANES - channels), F32)], axis=1)
        pltpu.make_async_copy(send_g.at[fc, pl.ds(group * 8, 8)], got_g.at[group, fc], sum_sem.at[1]).start()

        @pl.loop(1, groups)
        def _(n):
            to_peer(n, fc).start()

    third.wait_receive()
    grad_ref[...] = got_e[...]
    below.wait()
    above.wait()
    pltpu.make_async_copy(got_g, got_g, sum_sem.at[1]).wait()
    for fc in range(16):
        total = got_g[0, fc]
        for n in range(1, groups):
            total = total + got_g[n, fc]
        for lt in range(2):
            here = own_ref[:, 2 * fc + lt, :]
            down = jnp.where(time > 0, here - near[0, :, 2 * fc + lt, :], 0.0)
            up = jnp.where(time < times - 1, near[1, :, 2 * fc + lt, :] - here, 0.0)
            data_ref[fc, :, lt * LANES : (lt + 1) * LANES] = (
                total[:, lt * LANES : (lt + 1) * LANES] + smoothness * (down - up)
            )

    first.wait_send()
    second.wait_send()
    third.wait_send()
    others = gains.at[pl.ds(0, 8 * (groups - 1))]
    pltpu.make_async_copy(others, others, gain_sem.at[0]).wait()
    sent = got_g.at[pl.ds(0, groups - 1)]
    pltpu.make_async_copy(sent, sent, sum_sem.at[0]).wait()


def scatter_kernel(first_ref, words_ref, grad_ref, sky_ref, weight_ref, spread, cells, stage, sem):
    sources = grad_ref.shape[0]
    blocks = stage.shape[1] // 8
    for b in range(blocks):
        cells[b * STRIDE : (b + 1) * STRIDE, :] = jnp.zeros((STRIDE, LANES), F32)
    spread_taps(words_ref, weight_ref)
    fold = fold_table()
    lane_quarter = (iota((sources, LANES), 1) >> 1) & 3
    for h in range(2):
        block = grad_ref[:, h, :]
        for g in range(4):
            j = 4 * h + g
            part = jnp.concatenate(halves(jnp.where(lane_quarter == g, block, 0.0)), axis=1)
            spread[j] = jnp.where(slot_quarter(words_ref, j) == lane_quarter.astype(F32), dot(part, fold), 0.0)

    @pl.loop(0, sources, unroll=2)
    def _(s):
        at = pl.ds(pl.multiple_of(s * 8, 8), 8)
        for j in range(8):
            cells[pl.ds(first_ref[j, s], 8), :] += weight_ref[j, at, :] * spread[j, pl.ds(s, 1), :]

    quarter = (iota((8, LANES), 1) >> 1) & 3
    last = jnp.zeros((8, LANES), F32)
    for b in range(blocks):
        pads = cells[b * STRIDE + LANES : (b + 1) * STRIDE, :]
        head = slice(b * STRIDE, b * STRIDE + 8)
        cells[head, :] = cells[head, :] + jnp.where(quarter > 0, pltpu.roll(pads, 2, 1), last)
        last = pltpu.roll(pads, LANES - 6, 1)

    pieces = 4
    length = blocks // pieces

    def copy(n):
        at = pl.ds(n * length * 8, length * 8)
        return pltpu.make_async_copy(stage.at[:, at, :], sky_ref.at[:, at, :], sem.at[n])

    for n in range(pieces):

        @pl.loop(n * length, (n + 1) * length, unroll=8)
        def _(b):
            turned = cells[pl.ds(pl.multiple_of(b * STRIDE, 8), LANES), :].T
            stage[:, pl.ds(pl.multiple_of(b * 8, 8), 8), :] = turned.reshape(16, 8, LANES)

        copy(n).start()
    for n in range(pieces):
        copy(n).wait()


def vmem(count):
    return [pl.BlockSpec(memory_space=pltpu.VMEM)] * count


def shape(dims, dtype=F32):
    return jax.ShapeDtypeStruct(dims, dtype)


def params():
    return pltpu.CompilerParams(vmem_limit_bytes=VMEM_LIMIT)


def body(
    visibilities, noise_weight, keep_flag, station_pairs, tile_owner, tile_offset, kernel_taps, gain_field, sky_grid
):
    rows = visibilities.shape[0]
    channels = visibilities.shape[2]
    devices = lax.axis_size("tm") * lax.axis_size("bl")
    parts, facets, terms, cells = sky_grid.shape
    lines = cells // LANES
    sky = sky_grid.reshape(parts, facets, terms, lines, LANES).transpose(0, 1, 3, 2, 4)
    sky = sky.reshape(parts * facets, lines * terms, LANES)

    own = jnp.pad(gain_field[0], ((0, 0), (0, 0), (0, 0), (0, 2 * LANES - channels)))
    own = own.reshape(-1, facets * 4, LANES)
    pieces = pltpu.VMEM((devices, 2, LANES), F32)
    words, firsts, grad, data = pl.pallas_call(
        functools.partial(
            main_kernel, channels=channels, times=lax.axis_size("tm"), groups=lax.axis_size("bl")
        ),
        out_shape=(
            shape((devices, LANES)), shape((8, devices), I32), shape((devices, 2, LANES)),
            shape((2 * facets, 8, 2 * LANES)),
        ),
        in_specs=vmem(8) + [pl.BlockSpec(memory_space=pl.ANY)],
        out_specs=tuple(vmem(4)),
        scratch_shapes=[
            pltpu.VMEM((devices, 1, LANES), F32),
            pltpu.VMEM((devices, 1, LANES), F32),
            pieces,
            pieces,
            pieces,
            pieces,
            pltpu.VMEM((64, facets * 4, LANES), F32),
            pltpu.VMEM((2 * facets, 64, 2 * LANES), F32),
            pltpu.VMEM((8, 2 * facets, 8, 2 * LANES), F32),
            pltpu.VMEM((2, 8, facets * 4, LANES), F32),
            pltpu.VMEM((8, devices, rows), BF16),
            pltpu.VMEM(sky.shape, F32),
            pltpu.VMEM((cells // BLOCK * STRIDE, LANES), F32),
            pltpu.VMEM((8, devices * 8, LANES), F32),
            pltpu.VMEM((8, devices * 8, LANES), F32),
            pltpu.SMEM((8, devices), I32),
            pltpu.VMEM((rows // LANES, LANES, LANES), F32),
            pltpu.VMEM((2, 16, rows), F32),
            pltpu.VMEM((2 * facets * channels, LANES), BF16),
            pltpu.VMEM((2, LANES, rows), BF16),
            pltpu.VMEM((64, 4 * rows), BF16),
            pltpu.VMEM((1, rows), F32),
            pltpu.VMEM((2 * facets * channels, rows), F32),
            pltpu.VMEM((2 * facets * channels, rows), F32),
            pltpu.VMEM((2 * facets * channels, 4 * rows), BF16),
            pltpu.VMEM((2, 2 * facets, 8, rows), F32),
            pltpu.SemaphoreType.DMA,
            pltpu.SemaphoreType.DMA,
            pltpu.SemaphoreType.DMA((2,)),
            pltpu.SemaphoreType.DMA((2,)),
            pltpu.SemaphoreType.DMA((2,)),
            pltpu.SemaphoreType.DMA((2,)),
            pltpu.SemaphoreType.DMA((4,)),
            pltpu.SemaphoreType.DMA((2,)),
        ],
        compiler_params=pltpu.CompilerParams(
            vmem_limit_bytes=62 << 20, collective_id=0, has_side_effects=True
        ),
        name="main",
    )(
        tile_owner.reshape(1, rows), tile_offset.reshape(1, rows), kernel_taps, own,
        visibilities.transpose(1, 2, 0), noise_weight.reshape(1, rows), keep_flag.reshape(1, rows),
        station_pairs, sky,
    )

    out_grid = pl.pallas_call(
        scatter_kernel,
        out_shape=shape(sky.shape),
        in_specs=[pl.BlockSpec(memory_space=pltpu.SMEM)] + vmem(2),
        out_specs=pl.BlockSpec(memory_space=pl.ANY),
        scratch_shapes=[
            pltpu.VMEM((8, devices * 8, LANES), F32),
            pltpu.VMEM((8, devices, LANES), F32),
            pltpu.VMEM((cells // BLOCK * STRIDE, LANES), F32),
            pltpu.VMEM(sky.shape, F32),
            pltpu.SemaphoreType.DMA((4,)),
        ],
        compiler_params=params(),
        name="scatter",
    )(firsts, words, grad)
    grid_gradient = out_grid.reshape(parts, facets, lines, terms, LANES).transpose(0, 1, 3, 2, 4)
    grid_gradient = grid_gradient.reshape(sky_grid.shape)

    data = data.reshape(facets, 2, 8, 2 * LANES).transpose(2, 0, 1, 3)[None, :, :, :, :channels]
    return (data, grid_gradient)


def solution(mesh):
    split = ("tm", "bl")
    return jax.shard_map(
        body,
        mesh=mesh,
        in_specs=(
            P(split, None, None),
            P(split),
            P(split),
            P(None, split),
            P(split, None),
            P(split),
            P(None, split),
            P("tm", "bl", None, None, None),
            P(None, None, None, split),
        ),
        out_specs=(P("tm", "bl", None, None, None), P(None, None, None, split)),
        check_vma=False,
    )
```

```python
import functools

import jax
import jax.numpy as jnp
from jax import lax
from jax.experimental import pallas as pl
from jax.experimental.pallas import tpu as pltpu
from jax.sharding import PartitionSpec as P

smoothness = 4.0
F32, BF16, I32 = jnp.float32, jnp.bfloat16, jnp.int32
LANES = 128
WORDS = 16
BLOCK = 512
STRIDE = LANES + 8
CHUNK = 16
VMEM_LIMIT = 56 << 20
NT = (((1,), (1,)), ((), ()))


def iota(shape, axis):
    return lax.broadcasted_iota(I32, shape, axis)


def halves(x):
    hi = x.astype(BF16)
    return hi, (x - hi.astype(F32)).astype(BF16)


def dot(x, y):
    return jnp.dot(x, y, preferred_element_type=F32)


def dot_nt(x, y):
    return lax.dot_general(x, y, NT, preferred_element_type=F32)


def ones_where(mask):
    return jnp.where(mask, 1.0, 0.0).astype(BF16)


def form_slots(owner_ref, offset_ref, taps_ref, place_ref, store_message):
    devices, rows = place_ref.shape[1:]
    hits = iota((devices, rows), 0) == owner_ref[...]
    earlier = ones_where(iota((rows, rows), 0) < iota((rows, rows), 1))
    counts = dot(ones_where(hits), earlier)
    rank = jnp.sum(jnp.where(hits, counts, 0.0), axis=0, keepdims=True)
    offset = offset_ref[...]
    row = (offset >> 9) * STRIDE + (offset & (LANES - 1))
    tail = jnp.where(iota((WORDS - 8, rows), 0) == 0, row, (offset >> 7) & 3).astype(F32)
    words = jnp.concatenate([taps_ref[...], tail], axis=0)
    hi, lo = halves(jnp.concatenate([words] * 8, axis=0))
    group = iota((devices, LANES), 1) // WORDS
    message = jnp.zeros((devices, LANES), F32)
    for j in range(8):
        place = ones_where(jnp.where(hits, rank, -1.0) == float(j))
        place_ref[j] = place
        message = jnp.where(group == j, dot_nt(place, hi) + dot_nt(place, lo), message)
    store_message(message)


def transpose_grid(stage_ref, cells_ref):
    blocks = stage_ref.shape[1] // 8

    @pl.loop(0, blocks, unroll=8)
    def _(b):
        tile = stage_ref[:, pl.ds(pl.multiple_of(b * 8, 8), 8), :].reshape(LANES, LANES)
        cells_ref[pl.ds(pl.multiple_of(b * STRIDE, 8), LANES), :] = tile.T

    quarter = (iota((8, LANES), 1) >> 1) & 3
    for b in range(blocks):
        here = cells_ref[b * STRIDE : b * STRIDE + 8, :]
        next_block = min(b + 1, blocks - 1) * STRIDE
        after = cells_ref[next_block : next_block + 8, :]
        pad = jnp.where(quarter < 3, pltpu.roll(here, LANES - 2, 1), pltpu.roll(after, 6, 1))
        cells_ref[b * STRIDE + LANES : (b + 1) * STRIDE, :] = pad


def spread_taps(words_ref, weight_ref):
    sources = words_ref.shape[0]
    tall = jnp.broadcast_to(words_ref[...].reshape(sources, 1, LANES), (sources, 8, LANES)).reshape(8 * sources, LANES)
    tall = jnp.where((iota(tall.shape, 1) & (WORDS - 1)) == (iota(tall.shape, 0) & 7), tall, 0.0)
    both = jnp.concatenate(halves(tall), axis=1)
    for pair in range(4):
        a, b = iota((2 * LANES, 2 * LANES), 0) & (LANES - 1), iota((2 * LANES, 2 * LANES), 1)
        weight = dot(both, ones_where(a // WORDS == 2 * pair + b // LANES))
        for n in range(2):
            weight_ref[2 * pair + n] = weight[:, n * LANES : (n + 1) * LANES]


def slot_quarter(words_ref, j):
    return jnp.broadcast_to(words_ref[:, j * WORDS + 9 : j * WORDS + 10], (words_ref.shape[0], LANES))


def fold_table():
    a, b = iota((2 * LANES, LANES), 0) & (LANES - 1), iota((2 * LANES, LANES), 1)
    return ones_where(((a >> 3) == (b >> 3)) & ((a & 1) == (b & 1)))


def degrid_slots(first_ref, words_ref, cells_ref, weight_ref, product_ref, store_value):
    sources = words_ref.shape[0]

    @pl.loop(0, sources, unroll=2)
    def _(s):
        at = pl.ds(pl.multiple_of(s * 8, 8), 8)
        for j in range(8):
            product_ref[j, at, :] = weight_ref[j, at, :] * cells_ref[pl.ds(first_ref[j, s], 8), :]

    fold = fold_table()
    lane_quarter = (iota((sources, LANES), 1) >> 1) & 3
    for h in range(2):
        value = jnp.zeros((sources, LANES), F32)
        for g in range(4):
            j = 4 * h + g
            total = product_ref[j, pl.ds(0, sources, stride=8), :]
            for k in range(1, 8):
                total = total + product_ref[j, pl.ds(k, sources, stride=8), :]
            total = jnp.where(slot_quarter(words_ref, j) == lane_quarter.astype(F32), total, 0.0)
            value = jnp.where(lane_quarter == g, dot(jnp.concatenate(halves(total), axis=1), fold), value)
        store_value(h, value)


def gather_degrid(load_value, place_ref, part_ref, degrid_ref):
    sources = place_ref.shape[1]
    quarter = (iota((LANES, sources), 0) >> 1) & 3
    total = None
    for h in range(2):
        turned = load_value(h).T
        for pair in range(2):
            parts = [halves(jnp.where(quarter == g, turned, 0.0)) for g in (2 * pair, 2 * pair + 1)]
            j = 4 * h + 2 * pair
            place = place_ref[j : j + 2].reshape(2 * sources, place_ref.shape[2])
            for n in range(2):
                term = dot(jnp.concatenate([parts[0][n], parts[1][n]], axis=1), place)
                total = term if total is None else total + term
    for n in range(part_ref.shape[0]):
        tile = slice(n * LANES, (n + 1) * LANES)
        part_ref[n] = total[:, tile]
        for t in range(2):
            degrid_ref[t, :, tile] = sum(part_ref[n, pl.ds(2 * g + t, 16, stride=8), :] for g in range(4))


def station_tables(pairs_ref, gather_ref, sum_ref):
    rows = pairs_ref.shape[1]
    for side in range(2):
        hits = ones_where((iota((LANES, rows), 0) & 63) == pairs_ref[side : side + 1, :])
        gather_ref[side] = hits
        for n in range(2):
            sum_ref[:, (2 * side + n) * rows : (2 * side + n + 1) * rows] = hits[:64]


def turn_gains(gains_ref, turned_ref, channels):
    for fc in range(16):
        tiles = []
        for lt in range(2):
            block = gains_ref[:, :, :, 2 * fc + lt, :].reshape(64, LANES)
            hi = block.astype(BF16).astype(F32)
            tiles.append(jnp.concatenate([hi, block - hi], axis=0).T)
        turned_ref[fc * channels : (fc + 1) * channels] = jnp.concatenate(tiles, axis=0)[:channels].astype(BF16)


def gather_gains(turned_ref, gather_ref, left_ref, right_ref):
    size = turned_ref.shape[0] // 3

    @pl.loop(0, 3)
    def _(n):
        at = pl.ds(pl.multiple_of(n * size, CHUNK), size)
        gains = turned_ref[at, :]
        left_ref[at, :] = dot(gains, gather_ref[0])
        right_ref[at, :] = dot(gains, gather_ref[1])


def row_step(chunk, channels, vis_ref, scale_ref, degrid_ref, left_ref, right_ref, grads_ref, grad_degrid_ref):
    rows = vis_ref.shape[2]
    facets = left_ref.shape[0] // channels // 2
    width = 2 * LANES

    def rows_of(n):
        return pl.ds(pl.multiple_of(n * channels + chunk * CHUNK, CHUNK), CHUNK)

    at = rows_of(0)
    channel = (iota((CHUNK, width), 0) + chunk * CHUNK).astype(F32)
    ramp = 2.0 * channel / (channels - 1) - 1.0
    for lanes in range(rows // width):
        ln = slice(lanes * width, (lanes + 1) * width)

        def parts(f):
            re, im = rows_of(2 * f), rows_of(2 * f + 1)
            g = facets + f
            mre = degrid_ref[0, f : f + 1, ln] + degrid_ref[1, f : f + 1, ln] * ramp
            mim = degrid_ref[0, g : g + 1, ln] + degrid_ref[1, g : g + 1, ln] * ramp
            return left_ref[re, ln], left_ref[im, ln], right_ref[re, ln], right_ref[im, ln], mre, mim

        pred_re = pred_im = None
        for f in range(facets):
            are, aim, bre, bim, mre, mim = parts(f)
            pre, pim = are * bre + aim * bim, aim * bre - are * bim
            vre, vim = pre * mre - pim * mim, pre * mim + pim * mre
            pred_re = vre if pred_re is None else pred_re + vre
            pred_im = vim if pred_im is None else pred_im + vim
        ere = scale_ref[:, ln] * (pred_re - vis_ref[0, at, ln].astype(F32))
        eim = scale_ref[:, ln] * (pred_im - vis_ref[1, at, ln].astype(F32))
        for f in range(facets):
            are, aim, bre, bim, mre, mim = parts(f)
            qre, qim = ere * mre + eim * mim, eim * mre - ere * mim
            values = (
                (qre * bre - qim * bim, qre * bim + qim * bre),
                (qre * are + qim * aim, qre * aim - qim * are),
            )
            for side in range(2):
                for c in range(2):
                    hi, lo = halves(values[side][c])
                    first = 2 * side * rows + lanes * width
                    grads_ref[rows_of(2 * f + c), first : first + width] = hi
                    grads_ref[rows_of(2 * f + c), first + rows : first + rows + width] = lo
            pre, pim = are * bre + aim * bim, aim * bre - are * bim
            models = (ere * pre + eim * pim, eim * pre - ere * pim)
            for c in range(2):
                n = c * facets + f
                slope = models[c] * ramp
                grad_degrid_ref[0, n, :, ln] += models[c][:8] + models[c][8:]
                grad_degrid_ref[1, n, :, ln] += slope[:8] + slope[8:]


def place_grads(grad_degrid_ref, place_ref, store_value):
    planes = grad_degrid_ref.shape[1]
    rows = grad_degrid_ref.shape[3]
    devices = place_ref.shape[1]
    odd = (iota((8, rows), 0) & 1) == 1
    full = []
    for n in range(planes):
        level = jnp.sum(grad_degrid_ref[0, n], axis=0, keepdims=True)
        slope = jnp.sum(grad_degrid_ref[1, n], axis=0, keepdims=True)
        full.append(jnp.where(odd, slope, level))
    hi, lo = halves(jnp.concatenate(full, axis=0))
    group = (iota((devices, LANES), 1) >> 1) & 3
    for h in range(2):
        value = jnp.zeros((devices, LANES), F32)
        for g in range(4):
            place = place_ref[4 * h + g]
            value = jnp.where(group == g, dot_nt(place, hi) + dot_nt(place, lo), value)
        store_value(h, value)


class Exchange:
    def __init__(self, send_ref, middle_ref, receive_ref, sems, time, group):
        self.send_ref, self.middle_ref, self.receive_ref, self.sems = send_ref, middle_ref, receive_ref, sems
        self.time, self.group = time, group
        self.times, self.groups = send_ref.shape[:2]

    def start(self):
        to_middle = self.middle_ref.at[:, self.time]
        pltpu.make_async_copy(self.send_ref.at[self.time], to_middle, self.sems.at[1]).start()

        @pl.loop(1, self.times)
        def _(n):
            to = lax.rem(self.time + n, self.times)
            remote(self.send_ref.at[to], to_middle, self.sems.at[0], self.sems.at[1], (to, self.group)).start()

    def pass_on(self):
        wait_bytes(self.middle_ref, self.sems.at[1])
        to_end = self.receive_ref.at[:, self.group]
        pltpu.make_async_copy(self.middle_ref.at[self.group], to_end, self.sems.at[3]).start()

        @pl.loop(1, self.groups)
        def _(n):
            to = lax.rem(self.group + n, self.groups)
            remote(self.middle_ref.at[to], to_end, self.sems.at[2], self.sems.at[3], (self.time, to)).start()

    def wait_receive(self):
        wait_bytes(self.receive_ref, self.sems.at[3])

    def wait_send(self):
        wait_bytes(self.send_ref.at[pl.ds(0, self.times - 1)], self.sems.at[0])
        wait_bytes(self.middle_ref.at[pl.ds(0, self.groups - 1)], self.sems.at[2])


def remote(source, target, send_sem, receive_sem, device):
    return pltpu.make_async_remote_copy(
        src_ref=source, dst_ref=target, send_sem=send_sem, recv_sem=receive_sem,
        device_id=device, device_id_type=pl.DeviceIdType.MESH,
    )


def wait_bytes(ref, sem):
    pltpu.make_async_copy(ref, ref, sem).wait()


def main_kernel(
    owner_ref, offset_ref, taps_ref, gain_ref, vis_ref, noise_ref, keep_ref, pairs_ref, sky_ref,
    words_ref, firsts_ref, grad_ref, data_ref,
    send_a, mid_a, got_a, send_c, mid_c, got_c, send_e, mid_e, got_e, own, gains, send_g, got_g, near,
    place, stage, cells, weight, product, slots, part, degrid, turned, gather, sums, scale,
    left, right, grads, grad_degrid,
    sky_sem, slot_sem, sem_a, sem_c, sem_e, gain_sem, pair_sem, near_sem, sum_sem,
    channels, times, groups,
):
    time, group = lax.axis_index("tm"), lax.axis_index("bl")
    devices = times * groups
    level, core = group // 2, lax.rem(group, 2)
    facets = gain_ref.shape[1]
    barrier = pltpu.get_barrier_semaphore()

    @pl.loop(1, times)
    def _(n):
        to = (lax.rem(time + n, times), group)
        pl.semaphore_signal(barrier, inc=1, device_id=to, device_id_type=pl.DeviceIdType.MESH)

    @pl.loop(1, groups)
    def _(n):
        to = (time, lax.rem(group + n, groups))
        pl.semaphore_signal(barrier, inc=1, device_id=to, device_id_type=pl.DeviceIdType.MESH)

    sky_copy = pltpu.make_async_copy(sky_ref, stage, sky_sem)
    sky_copy.start()

    def store_message(message):
        for t in range(devices):
            send_a[t // groups, t % groups] = message[t : t + 1, :]

    form_slots(owner_ref, offset_ref, taps_ref, place, store_message)
    pl.semaphore_wait(barrier, times + groups - 2)

    first = Exchange(send_a, mid_a, got_a, sem_a, time, group)
    second = Exchange(send_c, mid_c, got_c, sem_c, time, group)
    third = Exchange(send_e, mid_e, got_e, sem_e, time, group)
    first.start()

    for f in range(facets):
        for c in range(2):
            for lt in range(2):
                wide = min(LANES, channels - lt * LANES)
                block = gain_ref[:, f, c, lt * LANES : lt * LANES + wide]
                if wide < LANES:
                    block = jnp.concatenate([block, jnp.zeros((block.shape[0], LANES - wide), F32)], axis=1)
                own[:, 4 * f + 2 * c + lt, :] = block
    mine = gains.at[level, core]
    pltpu.make_async_copy(own, mine, gain_sem.at[1]).start()

    @pl.loop(1, groups // 2)
    def _(n):
        to = lax.rem(group + 2 * n, groups)
        remote(own, mine, gain_sem.at[0], gain_sem.at[1], (time, to)).start()

    def next_interval(n, step):
        to = lax.rem(time + step, times)
        return remote(own, near.at[n], near_sem.at[2 * n], near_sem.at[2 * n + 1], (to, group))

    below, above = next_interval(0, 1), next_interval(1, times - 1)
    below.start()
    above.start()

    sky_copy.wait()
    transpose_grid(stage, cells)
    first.pass_on()
    scale[...] = noise_ref[...] * keep_ref[...].astype(F32)
    station_tables(pairs_ref, gather, sums)
    grad_degrid[...] = jnp.zeros_like(grad_degrid)

    first.wait_receive()
    words_ref[...] = got_a[...].reshape(devices, LANES)
    turned_words = words_ref[...].T
    firsts = jnp.concatenate([turned_words[j * WORDS + 8 : j * WORDS + 9, :] for j in range(8)], axis=0)
    firsts_ref[...] = jnp.clip(firsts.astype(I32), 0, cells.shape[0] - 8)
    slot_copy = pltpu.make_async_copy(firsts_ref, slots, slot_sem)
    slot_copy.start()
    spread_taps(words_ref, weight)
    slot_copy.wait()

    def store_value(h, value):
        send_c[:, :, h, :] = value.reshape(times, groups, LANES)

    degrid_slots(slots, words_ref, cells, weight, product, store_value)
    second.start()

    column = gains.at[:, core]
    wait_bytes(column, gain_sem.at[1])
    to_pair = remote(column, column, pair_sem.at[0], pair_sem.at[1], (time, group + 1 - 2 * core))
    to_pair.start()
    second.pass_on()
    wait_bytes(column, pair_sem.at[1])
    turn_gains(gains, turned, channels)
    gather_gains(turned, gather, left, right)

    second.wait_receive()
    gather_degrid(lambda h: got_c[:, :, h, :].reshape(devices, LANES), place, part, degrid)

    @pl.loop(0, channels // CHUNK)
    def _(chunk):
        row_step(chunk, channels, vis_ref, scale, degrid, left, right, grads, grad_degrid)

    def store_grad(h, value):
        send_e[:, :, h, :] = value.reshape(times, groups, LANES)

    place_grads(grad_degrid, place, store_grad)
    third.start()

    batch = 4

    def sum_batch(b):
        for i in range(batch):
            fc = b * batch + i
            value = dot_nt(sums[...], grads[fc * channels : (fc + 1) * channels, :])
            send_g[fc] = jnp.concatenate([value, jnp.zeros((64, 2 * LANES - channels), F32)], axis=1)
        these = pl.ds(b * batch, batch)
        to_end = got_g.at[group, these]
        pltpu.make_async_copy(send_g.at[these, pl.ds(group * 8, 8)], to_end, sum_sem.at[1]).start()

        @pl.loop(1, groups)
        def _(n):
            to = lax.rem(group + n, groups)
            remote(send_g.at[these, pl.ds(to * 8, 8)], to_end, sum_sem.at[0], sum_sem.at[1], (time, to)).start()

    sum_batch(0)
    third.pass_on()
    for b in range(1, 2 * facets // batch):
        sum_batch(b)

    third.wait_receive()
    grad_ref[...] = got_e[...].reshape(devices, 2, LANES)
    below.wait()
    above.wait()
    wait_bytes(got_g, sum_sem.at[1])
    for f in range(facets):
        for c in range(2):
            fc = 2 * f + c
            total = got_g[0, fc]
            for n in range(1, groups):
                total = total + got_g[n, fc]
            smooth = []
            for lt in range(2):
                here = own[:, 2 * fc + lt, :]
                down = jnp.where(time > 0, here - near[0, :, 2 * fc + lt, :], 0.0)
                up = jnp.where(time < times - 1, near[1, :, 2 * fc + lt, :] - here, 0.0)
                smooth.append(down - up)
            total = total + smoothness * jnp.concatenate(smooth, axis=1)
            data_ref[:, f, c, :] = total[:, :channels]

    first.wait_send()
    second.wait_send()
    third.wait_send()
    wait_bytes(gains.at[pl.ds(0, groups // 2 - 1), 0], gain_sem.at[0])
    wait_bytes(column, pair_sem.at[0])
    wait_bytes(got_g.at[pl.ds(0, groups - 1)], sum_sem.at[0])


def scatter_kernel(first_ref, words_ref, grad_ref, sky_ref, weight_ref, spread, cells, stage, sem):
    sources = grad_ref.shape[0]
    blocks = stage.shape[1] // 8
    for b in range(blocks):
        cells[b * STRIDE : (b + 1) * STRIDE, :] = jnp.zeros((STRIDE, LANES), F32)
    spread_taps(words_ref, weight_ref)
    fold = fold_table()
    lane_quarter = (iota((sources, LANES), 1) >> 1) & 3
    for h in range(2):
        block = grad_ref[:, h, :]
        for g in range(4):
            j = 4 * h + g
            part = jnp.concatenate(halves(jnp.where(lane_quarter == g, block, 0.0)), axis=1)
            spread[j] = jnp.where(slot_quarter(words_ref, j) == lane_quarter.astype(F32), dot(part, fold), 0.0)

    @pl.loop(0, sources, unroll=2)
    def _(s):
        at = pl.ds(pl.multiple_of(s * 8, 8), 8)
        for j in range(8):
            cells[pl.ds(first_ref[j, s], 8), :] += weight_ref[j, at, :] * spread[j, pl.ds(s, 1), :]

    quarter = (iota((8, LANES), 1) >> 1) & 3
    last = jnp.zeros((8, LANES), F32)
    for b in range(blocks):
        pads = cells[b * STRIDE + LANES : (b + 1) * STRIDE, :]
        head = slice(b * STRIDE, b * STRIDE + 8)
        cells[head, :] = cells[head, :] + jnp.where(quarter > 0, pltpu.roll(pads, 2, 1), last)
        last = pltpu.roll(pads, LANES - 6, 1)

    pieces = 4
    length = blocks // pieces

    def copy(n):
        at = pl.ds(n * length * 8, length * 8)
        return pltpu.make_async_copy(stage.at[:, at, :], sky_ref.at[:, at, :], sem.at[n])

    for n in range(pieces):

        @pl.loop(n * length, (n + 1) * length, unroll=8)
        def _(b):
            turned = cells[pl.ds(pl.multiple_of(b * STRIDE, 8), LANES), :].T
            stage[:, pl.ds(pl.multiple_of(b * 8, 8), 8), :] = turned.reshape(16, 8, LANES)

        copy(n).start()
    for n in range(pieces):
        copy(n).wait()


def vmem(count):
    return [pl.BlockSpec(memory_space=pltpu.VMEM)] * count


def shape(dims, dtype=F32):
    return jax.ShapeDtypeStruct(dims, dtype)


def params():
    return pltpu.CompilerParams(vmem_limit_bytes=VMEM_LIMIT)


def body(
    visibilities, noise_weight, keep_flag, station_pairs, tile_owner, tile_offset, kernel_taps, gain_field, sky_grid
):
    rows = visibilities.shape[0]
    channels = visibilities.shape[2]
    devices = lax.axis_size("tm") * lax.axis_size("bl")
    parts, facets, terms, cells = sky_grid.shape
    lines = cells // LANES
    sky = sky_grid.reshape(parts, facets, terms, lines, LANES).transpose(0, 1, 3, 2, 4)
    sky = sky.reshape(parts * facets, lines * terms, LANES)

    times, groups = lax.axis_size("tm"), lax.axis_size("bl")
    singles, pairs = pltpu.VMEM((times, groups, 1, LANES), F32), pltpu.VMEM((times, groups, 2, LANES), F32)
    middle_singles = pltpu.VMEM((groups, times, 1, LANES), F32)
    middle_pairs = pltpu.VMEM((groups, times, 2, LANES), F32)
    tiles = facets * 4
    words, firsts, grad, data = pl.pallas_call(
        functools.partial(
            main_kernel, channels=channels, times=times, groups=groups
        ),
        out_shape=(
            shape((devices, LANES)), shape((8, devices), I32), shape((devices, 2, LANES)),
            shape(gain_field.shape[1:]),
        ),
        in_specs=vmem(8) + [pl.BlockSpec(memory_space=pl.ANY)],
        out_specs=tuple(vmem(4)),
        scratch_shapes=[
            singles, middle_singles, singles,
            pairs, middle_pairs, pairs,
            pairs, middle_pairs, pairs,
            pltpu.VMEM((8, tiles, LANES), F32),
            pltpu.VMEM((groups // 2, 2, 8, tiles, LANES), F32),
            pltpu.VMEM((2 * facets, 64, 2 * LANES), F32),
            pltpu.VMEM((groups, 2 * facets, 8, 2 * LANES), F32),
            pltpu.VMEM((2, 8, tiles, LANES), F32),
            pltpu.VMEM((8, devices, rows), BF16),
            pltpu.VMEM(sky.shape, F32),
            pltpu.VMEM((cells // BLOCK * STRIDE, LANES), F32),
            pltpu.VMEM((8, devices * 8, LANES), F32),
            pltpu.VMEM((8, devices * 8, LANES), F32),
            pltpu.SMEM((8, devices), I32),
            pltpu.VMEM((rows // LANES, LANES, LANES), F32),
            pltpu.VMEM((2, 16, rows), F32),
            pltpu.VMEM((2 * facets * channels, LANES), BF16),
            pltpu.VMEM((2, LANES, rows), BF16),
            pltpu.VMEM((64, 4 * rows), BF16),
            pltpu.VMEM((1, rows), F32),
            pltpu.VMEM((2 * facets * channels, rows), F32),
            pltpu.VMEM((2 * facets * channels, rows), F32),
            pltpu.VMEM((2 * facets * channels, 4 * rows), BF16),
            pltpu.VMEM((2, 2 * facets, 8, rows), F32),
            pltpu.SemaphoreType.DMA,
            pltpu.SemaphoreType.DMA,
            pltpu.SemaphoreType.DMA((4,)),
            pltpu.SemaphoreType.DMA((4,)),
            pltpu.SemaphoreType.DMA((4,)),
            pltpu.SemaphoreType.DMA((2,)),
            pltpu.SemaphoreType.DMA((2,)),
            pltpu.SemaphoreType.DMA((4,)),
            pltpu.SemaphoreType.DMA((2,)),
        ],
        compiler_params=pltpu.CompilerParams(
            vmem_limit_bytes=62 << 20, collective_id=0, has_side_effects=True
        ),
        name="main",
    )(
        tile_owner.reshape(1, rows), tile_offset.reshape(1, rows), kernel_taps, gain_field[0],
        visibilities.transpose(1, 2, 0), noise_weight.reshape(1, rows), keep_flag.reshape(1, rows),
        station_pairs, sky,
    )

    out_grid = pl.pallas_call(
        scatter_kernel,
        out_shape=shape(sky.shape),
        in_specs=[pl.BlockSpec(memory_space=pltpu.SMEM)] + vmem(2),
        out_specs=pl.BlockSpec(memory_space=pl.ANY),
        scratch_shapes=[
            pltpu.VMEM((8, devices * 8, LANES), F32),
            pltpu.VMEM((8, devices, LANES), F32),
            pltpu.VMEM((cells // BLOCK * STRIDE, LANES), F32),
            pltpu.VMEM(sky.shape, F32),
            pltpu.SemaphoreType.DMA((4,)),
        ],
        compiler_params=params(),
        name="scatter",
    )(firsts, words, grad)
    grid_gradient = out_grid.reshape(parts, facets, lines, terms, LANES).transpose(0, 1, 3, 2, 4)
    grid_gradient = grid_gradient.reshape(sky_grid.shape)

    return (data[None], grid_gradient)


def solution(mesh):
    split = ("tm", "bl")
    return jax.shard_map(
        body,
        mesh=mesh,
        in_specs=(
            P(split, None, None),
            P(split),
            P(split),
            P(None, split),
            P(split, None),
            P(split),
            P(None, split),
            P("tm", "bl", None, None, None),
            P(None, None, None, split),
        ),
        out_specs=(P("tm", "bl", None, None, None), P(None, None, None, split)),
        check_vma=False,
    )
```

```python
import functools

import jax
import jax.numpy as jnp
from jax import lax
from jax.experimental import pallas as pl
from jax.experimental.pallas import tpu as pltpu
from jax.sharding import PartitionSpec as P

smoothness = 4.0
F32, BF16, I32 = jnp.float32, jnp.bfloat16, jnp.int32
LANES = 128
WORDS = 16
BLOCK = 512
STRIDE = LANES + 8
CHUNK = 16
VMEM_LIMIT = 56 << 20
NT = (((1,), (1,)), ((), ()))


def iota(shape, axis):
    return lax.broadcasted_iota(I32, shape, axis)


def halves(x):
    hi = x.astype(BF16)
    return hi, (x - hi.astype(F32)).astype(BF16)


def dot(x, y):
    return jnp.dot(x, y, preferred_element_type=F32)


def dot_nt(x, y):
    return lax.dot_general(x, y, NT, preferred_element_type=F32)


def ones_where(mask):
    return jnp.where(mask, 1.0, 0.0).astype(BF16)


def form_slots(owner_ref, offset_ref, taps_ref, place_ref, store_message):
    devices, rows = place_ref.shape[1:]
    hits = iota((devices, rows), 0) == owner_ref[...]
    earlier = ones_where(iota((rows, rows), 0) < iota((rows, rows), 1))
    counts = dot(ones_where(hits), earlier)
    rank = jnp.sum(jnp.where(hits, counts, 0.0), axis=0, keepdims=True)
    offset = offset_ref[...]
    row = (offset >> 9) * STRIDE + (offset & (LANES - 1))
    tail = jnp.where(iota((WORDS - 8, rows), 0) == 0, row, (offset >> 7) & 3).astype(F32)
    words = jnp.concatenate([taps_ref[...], tail], axis=0)
    hi, lo = halves(jnp.concatenate([words] * 8, axis=0))
    group = iota((devices, LANES), 1) // WORDS
    message = jnp.zeros((devices, LANES), F32)
    for j in range(8):
        place = ones_where(jnp.where(hits, rank, -1.0) == float(j))
        place_ref[j] = place
        message = jnp.where(group == j, dot_nt(place, hi) + dot_nt(place, lo), message)
    store_message(message)


def transpose_grid(stage_ref, cells_ref):
    blocks = stage_ref.shape[1] // 8

    @pl.loop(0, blocks, unroll=8)
    def _(b):
        tile = stage_ref[:, pl.ds(pl.multiple_of(b * 8, 8), 8), :].reshape(LANES, LANES)
        cells_ref[pl.ds(pl.multiple_of(b * STRIDE, 8), LANES), :] = tile.T

    quarter = (iota((8, LANES), 1) >> 1) & 3
    for b in range(blocks):
        here = cells_ref[b * STRIDE : b * STRIDE + 8, :]
        next_block = min(b + 1, blocks - 1) * STRIDE
        after = cells_ref[next_block : next_block + 8, :]
        pad = jnp.where(quarter < 3, pltpu.roll(here, LANES - 2, 1), pltpu.roll(after, 6, 1))
        cells_ref[b * STRIDE + LANES : (b + 1) * STRIDE, :] = pad


def spread_taps(words_ref, weight_ref):
    sources = words_ref.shape[0]
    tall = jnp.broadcast_to(words_ref[...].reshape(sources, 1, LANES), (sources, 8, LANES)).reshape(8 * sources, LANES)
    tall = jnp.where((iota(tall.shape, 1) & (WORDS - 1)) == (iota(tall.shape, 0) & 7), tall, 0.0)
    both = jnp.concatenate(halves(tall), axis=1)
    for pair in range(4):
        a, b = iota((2 * LANES, 2 * LANES), 0) & (LANES - 1), iota((2 * LANES, 2 * LANES), 1)
        weight = dot(both, ones_where(a // WORDS == 2 * pair + b // LANES))
        for n in range(2):
            weight_ref[2 * pair + n] = weight[:, n * LANES : (n + 1) * LANES]


def slot_quarter(words_ref, j):
    return jnp.broadcast_to(words_ref[:, j * WORDS + 9 : j * WORDS + 10], (words_ref.shape[0], LANES))


def fold_table():
    a, b = iota((2 * LANES, LANES), 0) & (LANES - 1), iota((2 * LANES, LANES), 1)
    return ones_where(((a >> 3) == (b >> 3)) & ((a & 1) == (b & 1)))


def degrid_slots(first_ref, words_ref, cells_ref, weight_ref, product_ref, store_value):
    sources = words_ref.shape[0]

    @pl.loop(0, sources, unroll=2)
    def _(s):
        at = pl.ds(pl.multiple_of(s * 8, 8), 8)
        for j in range(8):
            product_ref[j, at, :] = weight_ref[j, at, :] * cells_ref[pl.ds(first_ref[j, s], 8), :]

    fold = fold_table()
    lane_quarter = (iota((sources, LANES), 1) >> 1) & 3
    for h in range(2):
        value = jnp.zeros((sources, LANES), F32)
        for g in range(4):
            j = 4 * h + g
            total = product_ref[j, pl.ds(0, sources, stride=8), :]
            for k in range(1, 8):
                total = total + product_ref[j, pl.ds(k, sources, stride=8), :]
            total = jnp.where(slot_quarter(words_ref, j) == lane_quarter.astype(F32), total, 0.0)
            value = jnp.where(lane_quarter == g, dot(jnp.concatenate(halves(total), axis=1), fold), value)
        store_value(h, value)


def gather_degrid(load_value, place_ref, part_ref, degrid_ref):
    sources = place_ref.shape[1]
    quarter = (iota((LANES, sources), 0) >> 1) & 3
    total = None
    for h in range(2):
        turned = load_value(h).T
        for pair in range(2):
            parts = [halves(jnp.where(quarter == g, turned, 0.0)) for g in (2 * pair, 2 * pair + 1)]
            j = 4 * h + 2 * pair
            place = place_ref[j : j + 2].reshape(2 * sources, place_ref.shape[2])
            for n in range(2):
                term = dot(jnp.concatenate([parts[0][n], parts[1][n]], axis=1), place)
                total = term if total is None else total + term
    for n in range(part_ref.shape[0]):
        tile = slice(n * LANES, (n + 1) * LANES)
        part_ref[n] = total[:, tile]
        for t in range(2):
            degrid_ref[t, :, tile] = sum(part_ref[n, pl.ds(2 * g + t, 16, stride=8), :] for g in range(4))


def station_tables(pairs_ref, gather_ref, sum_ref):
    rows = pairs_ref.shape[1]
    for side in range(2):
        hits = ones_where((iota((LANES, rows), 0) & 63) == pairs_ref[side : side + 1, :])
        gather_ref[side] = hits
        for n in range(2):
            sum_ref[:, (2 * side + n) * rows : (2 * side + n + 1) * rows] = hits[:64]


def turn_gains(gains_ref, turned_ref, channels):
    for fc in range(16):
        tiles = []
        for lt in range(2):
            block = gains_ref[:, :, :, 2 * fc + lt, :].reshape(64, LANES)
            hi = block.astype(BF16).astype(F32)
            tiles.append(jnp.concatenate([hi, block - hi], axis=0).T)
        turned_ref[fc * channels : (fc + 1) * channels] = jnp.concatenate(tiles, axis=0)[:channels].astype(BF16)


def gather_gains(turned_ref, gather_ref, left_ref, right_ref, first, last):
    size = turned_ref.shape[0] // 3

    @pl.loop(first, last)
    def _(n):
        at = pl.ds(pl.multiple_of(n * size, CHUNK), size)
        gains = turned_ref[at, :]
        left_ref[at, :] = dot(gains, gather_ref[0])
        right_ref[at, :] = dot(gains, gather_ref[1])


def chunk_rows(plane, channels, chunk):
    return pl.ds(pl.multiple_of(plane * channels + chunk * CHUNK, CHUNK), CHUNK)


def channel_ramp(channels, chunk, width):
    channel = (iota((CHUNK, width), 0) + chunk * CHUNK).astype(F32)
    return 2.0 * channel / (channels - 1) - 1.0


def facet_model(degrid_ref, f, lanes, ramp):
    g = degrid_ref.shape[1] // 2 + f
    return tuple(degrid_ref[0, n : n + 1, lanes] + degrid_ref[1, n : n + 1, lanes] * ramp for n in (f, g))


def error_step(
    chunk, channels, vis_ref, scale_ref, degrid_ref, left_ref, right_ref, error_ref, grad_degrid_ref, width=LANES
):
    rows = vis_ref.shape[2]
    facets = degrid_ref.shape[1] // 2
    at = chunk_rows(0, channels, chunk)
    ramp = channel_ramp(channels, chunk, width)
    for first in range(0, rows, width):
        lanes = slice(first, first + width)
        products, pred_re, pred_im = [], None, None
        for f in range(facets):
            re, im = chunk_rows(2 * f, channels, chunk), chunk_rows(2 * f + 1, channels, chunk)
            are, aim, bre, bim = left_ref[re, lanes], left_ref[im, lanes], right_ref[re, lanes], right_ref[im, lanes]
            mre, mim = facet_model(degrid_ref, f, lanes, ramp)
            pre, pim = are * bre + aim * bim, aim * bre - are * bim
            vre, vim = pre * mre - pim * mim, pre * mim + pim * mre
            pred_re = vre if pred_re is None else pred_re + vre
            pred_im = vim if pred_im is None else pred_im + vim
            products.append((pre, pim))
        ere = scale_ref[:, lanes] * (pred_re - vis_ref[0, at, lanes].astype(F32))
        eim = scale_ref[:, lanes] * (pred_im - vis_ref[1, at, lanes].astype(F32))
        error_ref[0, at, lanes] = ere
        error_ref[1, at, lanes] = eim
        for f in range(facets):
            pre, pim = products[f]
            models = (ere * pre + eim * pim, eim * pre - ere * pim)
            for c in range(2):
                n = c * facets + f
                slope = models[c] * ramp
                grad_degrid_ref[0, n, :, lanes] += models[c][:8] + models[c][8:]
                grad_degrid_ref[1, n, :, lanes] += slope[:8] + slope[8:]


def gain_step(f, chunk, channels, degrid_ref, left_ref, right_ref, error_ref, grads_ref, width=LANES):
    rows = error_ref.shape[2]
    at = chunk_rows(0, channels, chunk)
    ramp = channel_ramp(channels, chunk, width)
    re, im = chunk_rows(2 * f, channels, chunk), chunk_rows(2 * f + 1, channels, chunk)
    for first in range(0, rows, width):
        lanes = slice(first, first + width)
        are, aim, bre, bim = left_ref[re, lanes], left_ref[im, lanes], right_ref[re, lanes], right_ref[im, lanes]
        mre, mim = facet_model(degrid_ref, f, lanes, ramp)
        ere, eim = error_ref[0, at, lanes], error_ref[1, at, lanes]
        qre, qim = ere * mre + eim * mim, eim * mre - ere * mim
        values = (
            (qre * bre - qim * bim, qre * bim + qim * bre),
            (qre * are + qim * aim, qre * aim - qim * are),
        )
        for side in range(2):
            for c in range(2):
                hi, lo = halves(values[side][c])
                start = 2 * side * rows + first
                grads_ref[chunk_rows(c, channels, chunk), start : start + width] = hi
                grads_ref[chunk_rows(c, channels, chunk), start + rows : start + rows + width] = lo


def place_grads(grad_degrid_ref, place_ref, store_value):
    planes = grad_degrid_ref.shape[1]
    rows = grad_degrid_ref.shape[3]
    devices = place_ref.shape[1]
    odd = (iota((8, rows), 0) & 1) == 1
    full = []
    for n in range(planes):
        level = jnp.sum(grad_degrid_ref[0, n], axis=0, keepdims=True)
        slope = jnp.sum(grad_degrid_ref[1, n], axis=0, keepdims=True)
        full.append(jnp.where(odd, slope, level))
    hi, lo = halves(jnp.concatenate(full, axis=0))
    group = (iota((devices, LANES), 1) >> 1) & 3
    for h in range(2):
        value = jnp.zeros((devices, LANES), F32)
        for g in range(4):
            place = place_ref[4 * h + g]
            value = jnp.where(group == g, dot_nt(place, hi) + dot_nt(place, lo), value)
        store_value(h, value)


class Exchange:
    def __init__(self, send_ref, middle_ref, receive_ref, sems, time, group):
        self.send_ref, self.middle_ref, self.receive_ref, self.sems = send_ref, middle_ref, receive_ref, sems
        self.time, self.group = time, group
        self.times, self.groups = send_ref.shape[:2]

    def start(self):
        to_middle = self.middle_ref.at[:, self.time]
        pltpu.make_async_copy(self.send_ref.at[self.time], to_middle, self.sems.at[1]).start()

        @pl.loop(1, self.times)
        def _(n):
            to = lax.rem(self.time + n, self.times)
            remote(self.send_ref.at[to], to_middle, self.sems.at[0], self.sems.at[1], (to, self.group)).start()

    def pass_on(self):
        wait_bytes(self.middle_ref, self.sems.at[1])
        to_end = self.receive_ref.at[:, self.group]
        pltpu.make_async_copy(self.middle_ref.at[self.group], to_end, self.sems.at[3]).start()

        @pl.loop(1, self.groups)
        def _(n):
            to = lax.rem(self.group + n, self.groups)
            remote(self.middle_ref.at[to], to_end, self.sems.at[2], self.sems.at[3], (self.time, to)).start()

    def wait_receive(self):
        wait_bytes(self.receive_ref, self.sems.at[3])

    def wait_send(self):
        wait_bytes(self.send_ref.at[pl.ds(0, self.times - 1)], self.sems.at[0])
        wait_bytes(self.middle_ref.at[pl.ds(0, self.groups - 1)], self.sems.at[2])


def remote(source, target, send_sem, receive_sem, device):
    return pltpu.make_async_remote_copy(
        src_ref=source, dst_ref=target, send_sem=send_sem, recv_sem=receive_sem,
        device_id=device, device_id_type=pl.DeviceIdType.MESH,
    )


def wait_bytes(ref, sem):
    pltpu.make_async_copy(ref, ref, sem).wait()


def main_kernel(
    owner_ref, offset_ref, taps_ref, gain_ref, vis_ref, noise_ref, keep_ref, pairs_ref, sky_ref,
    words_ref, firsts_ref, grad_ref, data_ref,
    send_a, mid_a, got_a, send_c, mid_c, got_c, send_e, mid_e, got_e, own, gains, send_g, pair_g, sum_g, got_g, near,
    place, stage, cells, weight, product, slots, part, degrid, turned, gather, sums, scale,
    left, right, error, grads_even, grads_odd, grad_degrid,
    sky_sem, slot_sem, sem_a, sem_c, sem_e, gain_sem, pair_sem, near_sem, sum_sem,
    channels, times, groups,
):
    time, group = lax.axis_index("tm"), lax.axis_index("bl")
    devices = times * groups
    level, core = group // 2, lax.rem(group, 2)
    facets = gain_ref.shape[1]
    barrier = pltpu.get_barrier_semaphore()

    @pl.loop(1, times)
    def _(n):
        to = (lax.rem(time + n, times), group)
        pl.semaphore_signal(barrier, inc=1, device_id=to, device_id_type=pl.DeviceIdType.MESH)

    @pl.loop(1, groups)
    def _(n):
        to = (time, lax.rem(group + n, groups))
        pl.semaphore_signal(barrier, inc=1, device_id=to, device_id_type=pl.DeviceIdType.MESH)

    sky_copy = pltpu.make_async_copy(sky_ref, stage, sky_sem)
    sky_copy.start()

    def store_message(message):
        for t in range(devices):
            send_a[t // groups, t % groups] = message[t : t + 1, :]

    form_slots(owner_ref, offset_ref, taps_ref, place, store_message)
    pl.semaphore_wait(barrier, times + groups - 2)

    first = Exchange(send_a, mid_a, got_a, sem_a, time, group)
    second = Exchange(send_c, mid_c, got_c, sem_c, time, group)
    third = Exchange(send_e, mid_e, got_e, sem_e, time, group)
    first.start()

    for f in range(facets):
        for c in range(2):
            for lt in range(2):
                wide = min(LANES, channels - lt * LANES)
                block = gain_ref[:, f, c, lt * LANES : lt * LANES + wide]
                if wide < LANES:
                    block = jnp.concatenate([block, jnp.zeros((block.shape[0], LANES - wide), F32)], axis=1)
                own[:, 4 * f + 2 * c + lt, :] = block
    mine = gains.at[level, core]
    pltpu.make_async_copy(own, mine, gain_sem.at[1]).start()

    @pl.loop(1, groups // 2)
    def _(n):
        to = lax.rem(group + 2 * n, groups)
        remote(own, mine, gain_sem.at[0], gain_sem.at[1], (time, to)).start()

    def next_interval(n, step):
        to = lax.rem(time + step, times)
        return remote(own, near.at[n], near_sem.at[2 * n], near_sem.at[2 * n + 1], (to, group))

    below, above = next_interval(0, 1), next_interval(1, times - 1)
    below.start()
    above.start()

    sky_copy.wait()
    transpose_grid(stage, cells)
    first.pass_on()
    scale[...] = noise_ref[...] * keep_ref[...].astype(F32)
    station_tables(pairs_ref, gather, sums)
    grad_degrid[...] = jnp.zeros_like(grad_degrid)

    first.wait_receive()
    words_ref[...] = got_a[...].reshape(devices, LANES)
    turned_words = words_ref[...].T
    firsts = jnp.concatenate([turned_words[j * WORDS + 8 : j * WORDS + 9, :] for j in range(8)], axis=0)
    firsts_ref[...] = jnp.clip(firsts.astype(I32), 0, cells.shape[0] - 8)
    slot_copy = pltpu.make_async_copy(firsts_ref, slots, slot_sem)
    slot_copy.start()
    spread_taps(words_ref, weight)
    column = gains.at[:, core]
    pair = (time, group + 1 - 2 * core)
    wait_bytes(column, gain_sem.at[1])
    remote(column, column, pair_sem.at[0], pair_sem.at[1], pair).start()
    slot_copy.wait()

    def store_value(h, value):
        send_c[:, :, h, :] = value.reshape(times, groups, LANES)

    degrid_slots(slots, words_ref, cells, weight, product, store_value)
    second.start()
    wait_bytes(column, pair_sem.at[1])
    turn_gains(gains, turned, channels)
    gather_gains(turned, gather, left, right, 0, 2)
    second.pass_on()
    gather_gains(turned, gather, left, right, 2, 3)

    second.wait_receive()
    gather_degrid(lambda h: got_c[:, :, h, :].reshape(devices, LANES), place, part, degrid)

    @pl.loop(0, channels // CHUNK)
    def _(chunk):
        error_step(chunk, channels, vis_ref, scale, degrid, left, right, error, grad_degrid, 2 * LANES)

    def store_grad(h, value):
        send_e[:, :, h, :] = value.reshape(times, groups, LANES)

    place_grads(grad_degrid, place, store_grad)
    third.start()

    batch = 4

    def these(b):
        return pl.ds(b * batch, batch)

    def combine(b):
        wait_bytes(pair_g.at[these(b)], sum_sem.at[3 + b])
        for fc in range(b * batch, (b + 1) * batch):
            sum_g[:, fc] = send_g[core, fc] + pair_g[fc]
        to_end = got_g.at[level, these(b)]
        pltpu.make_async_copy(sum_g.at[level, these(b)], to_end, sum_sem.at[2]).start()

        @pl.loop(1, groups // 2)
        def _(n):
            to = lax.rem(level + n, groups // 2)
            remote(sum_g.at[to, these(b)], to_end, sum_sem.at[1], sum_sem.at[2], (time, 2 * to + core)).start()

    for f in range(facets):
        grads = grads_even if f % 2 == 0 else grads_odd

        @pl.loop(0, channels // CHUNK, unroll=5)
        def _(chunk):
            gain_step(f, chunk, channels, degrid, left, right, error, grads, 2 * LANES)

        for c in range(2):
            value = dot_nt(sums[...], grads[c * channels : (c + 1) * channels, :])
            value = jnp.concatenate([value, jnp.zeros((64, 2 * LANES - channels), F32)], axis=1)
            value = value.reshape(groups // 2, 2, 8, 2 * LANES)
            for k in range(2):
                send_g[k, 2 * f + c] = value[:, k]
        b = (2 * f + 1) // batch
        if (2 * f + 2) % batch == 0:
            remote(
                send_g.at[1 - core, these(b)], pair_g.at[these(b)], sum_sem.at[0], sum_sem.at[3 + b], pair
            ).start()
            if b > 0:
                combine(b - 1)
            if b == 1:
                third.pass_on()
    combine(2 * facets // batch - 1)

    third.wait_receive()
    grad_ref[...] = got_e[...].reshape(devices, 2, LANES)
    below.wait()
    above.wait()
    wait_bytes(got_g, sum_sem.at[2])
    for f in range(facets):
        for c in range(2):
            fc = 2 * f + c
            total = got_g[0, fc]
            for n in range(1, groups // 2):
                total = total + got_g[n, fc]
            smooth = []
            for lt in range(2):
                here = own[:, 2 * fc + lt, :]
                down = jnp.where(time > 0, here - near[0, :, 2 * fc + lt, :], 0.0)
                up = jnp.where(time < times - 1, near[1, :, 2 * fc + lt, :] - here, 0.0)
                smooth.append(down - up)
            total = total + smoothness * jnp.concatenate(smooth, axis=1)
            data_ref[:, f, c, :] = total[:, :channels]

    first.wait_send()
    second.wait_send()
    third.wait_send()
    wait_bytes(gains.at[pl.ds(0, groups // 2 - 1), 0], gain_sem.at[0])
    wait_bytes(column, pair_sem.at[0])
    wait_bytes(pair_g, sum_sem.at[0])
    wait_bytes(got_g.at[pl.ds(0, groups // 2 - 1)], sum_sem.at[1])


def scatter_kernel(first_ref, words_ref, grad_ref, sky_ref, weight_ref, spread, cells, stage, sem):
    sources = grad_ref.shape[0]
    blocks = stage.shape[1] // 8
    for b in range(blocks):
        cells[b * STRIDE : (b + 1) * STRIDE, :] = jnp.zeros((STRIDE, LANES), F32)
    spread_taps(words_ref, weight_ref)
    fold = fold_table()
    lane_quarter = (iota((sources, LANES), 1) >> 1) & 3
    for h in range(2):
        block = grad_ref[:, h, :]
        for g in range(4):
            j = 4 * h + g
            part = jnp.concatenate(halves(jnp.where(lane_quarter == g, block, 0.0)), axis=1)
            spread[j] = jnp.where(slot_quarter(words_ref, j) == lane_quarter.astype(F32), dot(part, fold), 0.0)

    @pl.loop(0, sources, unroll=2)
    def _(s):
        at = pl.ds(pl.multiple_of(s * 8, 8), 8)
        for j in range(8):
            cells[pl.ds(first_ref[j, s], 8), :] += weight_ref[j, at, :] * spread[j, pl.ds(s, 1), :]

    quarter = (iota((8, LANES), 1) >> 1) & 3
    last = jnp.zeros((8, LANES), F32)
    for b in range(blocks):
        pads = cells[b * STRIDE + LANES : (b + 1) * STRIDE, :]
        head = slice(b * STRIDE, b * STRIDE + 8)
        cells[head, :] = cells[head, :] + jnp.where(quarter > 0, pltpu.roll(pads, 2, 1), last)
        last = pltpu.roll(pads, LANES - 6, 1)

    pieces = 4
    length = blocks // pieces

    def copy(n):
        at = pl.ds(n * length * 8, length * 8)
        return pltpu.make_async_copy(stage.at[:, at, :], sky_ref.at[:, at, :], sem.at[n])

    for n in range(pieces):

        @pl.loop(n * length, (n + 1) * length, unroll=8)
        def _(b):
            turned = cells[pl.ds(pl.multiple_of(b * STRIDE, 8), LANES), :].T
            stage[:, pl.ds(pl.multiple_of(b * 8, 8), 8), :] = turned.reshape(16, 8, LANES)

        copy(n).start()
    for n in range(pieces):
        copy(n).wait()


def vmem(count):
    return [pl.BlockSpec(memory_space=pltpu.VMEM)] * count


def shape(dims, dtype=F32):
    return jax.ShapeDtypeStruct(dims, dtype)


def params():
    return pltpu.CompilerParams(vmem_limit_bytes=VMEM_LIMIT)


def body(
    visibilities, noise_weight, keep_flag, station_pairs, tile_owner, tile_offset, kernel_taps, gain_field, sky_grid
):
    rows = visibilities.shape[0]
    channels = visibilities.shape[2]
    devices = lax.axis_size("tm") * lax.axis_size("bl")
    parts, facets, terms, cells = sky_grid.shape
    lines = cells // LANES
    sky = sky_grid.reshape(parts, facets, terms, lines, LANES).transpose(0, 1, 3, 2, 4)
    sky = sky.reshape(parts * facets, lines * terms, LANES)

    times, groups = lax.axis_size("tm"), lax.axis_size("bl")
    singles, pairs = pltpu.VMEM((times, groups, 1, LANES), F32), pltpu.VMEM((times, groups, 2, LANES), F32)
    middle_singles = pltpu.VMEM((groups, times, 1, LANES), F32)
    middle_pairs = pltpu.VMEM((groups, times, 2, LANES), F32)
    tiles = facets * 4
    words, firsts, grad, data = pl.pallas_call(
        functools.partial(
            main_kernel, channels=channels, times=times, groups=groups
        ),
        out_shape=(
            shape((devices, LANES)), shape((8, devices), I32), shape((devices, 2, LANES)),
            shape(gain_field.shape[1:]),
        ),
        in_specs=vmem(8) + [pl.BlockSpec(memory_space=pl.ANY)],
        out_specs=tuple(vmem(4)),
        scratch_shapes=[
            singles, middle_singles, singles,
            pairs, middle_pairs, pairs,
            pairs, middle_pairs, pairs,
            pltpu.VMEM((8, tiles, LANES), F32),
            pltpu.VMEM((groups // 2, 2, 8, tiles, LANES), F32),
            pltpu.VMEM((2, 2 * facets, groups // 2, 8, 2 * LANES), F32),
            pltpu.VMEM((2 * facets, groups // 2, 8, 2 * LANES), F32),
            pltpu.VMEM((groups // 2, 2 * facets, 8, 2 * LANES), F32),
            pltpu.VMEM((groups // 2, 2 * facets, 8, 2 * LANES), F32),
            pltpu.VMEM((2, 8, tiles, LANES), F32),
            pltpu.VMEM((8, devices, rows), BF16),
            pltpu.VMEM(sky.shape, F32),
            pltpu.VMEM((cells // BLOCK * STRIDE, LANES), F32),
            pltpu.VMEM((8, devices * 8, LANES), F32),
            pltpu.VMEM((8, devices * 8, LANES), F32),
            pltpu.SMEM((8, devices), I32),
            pltpu.VMEM((rows // LANES, LANES, LANES), F32),
            pltpu.VMEM((2, 16, rows), F32),
            pltpu.VMEM((2 * facets * channels, LANES), BF16),
            pltpu.VMEM((2, LANES, rows), BF16),
            pltpu.VMEM((64, 4 * rows), BF16),
            pltpu.VMEM((1, rows), F32),
            pltpu.VMEM((2 * facets * channels, rows), F32),
            pltpu.VMEM((2 * facets * channels, rows), F32),
            pltpu.VMEM((2, channels, rows), F32),
            pltpu.VMEM((2 * channels, 4 * rows), BF16),
            pltpu.VMEM((2 * channels, 4 * rows), BF16),
            pltpu.VMEM((2, 2 * facets, 8, rows), F32),
            pltpu.SemaphoreType.DMA,
            pltpu.SemaphoreType.DMA,
            pltpu.SemaphoreType.DMA((4,)),
            pltpu.SemaphoreType.DMA((4,)),
            pltpu.SemaphoreType.DMA((4,)),
            pltpu.SemaphoreType.DMA((2,)),
            pltpu.SemaphoreType.DMA((2,)),
            pltpu.SemaphoreType.DMA((4,)),
            pltpu.SemaphoreType.DMA((7,)),
        ],
        compiler_params=pltpu.CompilerParams(
            vmem_limit_bytes=62 << 20, collective_id=0, has_side_effects=True
        ),
        name="main",
    )(
        tile_owner.reshape(1, rows), tile_offset.reshape(1, rows), kernel_taps, gain_field[0],
        visibilities.transpose(1, 2, 0), noise_weight.reshape(1, rows), keep_flag.reshape(1, rows),
        station_pairs, sky,
    )

    out_grid = pl.pallas_call(
        scatter_kernel,
        out_shape=shape(sky.shape),
        in_specs=[pl.BlockSpec(memory_space=pltpu.SMEM)] + vmem(2),
        out_specs=pl.BlockSpec(memory_space=pl.ANY),
        scratch_shapes=[
            pltpu.VMEM((8, devices * 8, LANES), F32),
            pltpu.VMEM((8, devices, LANES), F32),
            pltpu.VMEM((cells // BLOCK * STRIDE, LANES), F32),
            pltpu.VMEM(sky.shape, F32),
            pltpu.SemaphoreType.DMA((4,)),
        ],
        compiler_params=params(),
        name="scatter",
    )(firsts, words, grad)
    grid_gradient = out_grid.reshape(parts, facets, lines, terms, LANES).transpose(0, 1, 3, 2, 4)
    grid_gradient = grid_gradient.reshape(sky_grid.shape)

    return (data[None], grid_gradient)


def solution(mesh):
    split = ("tm", "bl")
    return jax.shard_map(
        body,
        mesh=mesh,
        in_specs=(
            P(split, None, None),
            P(split),
            P(split),
            P(None, split),
            P(split, None),
            P(split),
            P(None, split),
            P("tm", "bl", None, None, None),
            P(None, None, None, split),
        ),
        out_specs=(P("tm", "bl", None, None, None), P(None, None, None, split)),
        check_vma=False,
    )
```

```python
import functools
import math

import jax
import jax.numpy as jnp
from jax import lax
from jax.experimental import pallas as pl
from jax.experimental.pallas import tpu as pltpu
from jax.sharding import PartitionSpec as P

smoothness = 4.0
F32, BF16, I32 = jnp.float32, jnp.bfloat16, jnp.int32
LANES = 128
WORDS = 16
BLOCK = 512
STRIDE = LANES + 8
CHUNK = 16
VMEM_LIMIT = 56 << 20
NT = (((1,), (1,)), ((), ()))


def iota(shape, axis):
    return lax.broadcasted_iota(I32, shape, axis)


def halves(x):
    hi = x.astype(BF16)
    return hi, (x - hi.astype(F32)).astype(BF16)


def dot(x, y):
    return jnp.dot(x, y, preferred_element_type=F32)


def dot_nt(x, y):
    return lax.dot_general(x, y, NT, preferred_element_type=F32)


def ones_where(mask):
    return jnp.where(mask, 1.0, 0.0).astype(BF16)


def form_slots(owner_ref, offset_ref, taps_ref, place_ref, store_message):
    devices, rows = place_ref.shape[1:]
    hits = iota((devices, rows), 0) == owner_ref[...]
    earlier = ones_where(iota((rows, rows), 0) < iota((rows, rows), 1))
    counts = dot(ones_where(hits), earlier)
    rank = jnp.sum(jnp.where(hits, counts, 0.0), axis=0, keepdims=True)
    offset = offset_ref[...]
    row = (offset >> 9) * STRIDE + (offset & (LANES - 1))
    tail = jnp.where(iota((WORDS - 8, rows), 0) == 0, row, (offset >> 7) & 3).astype(F32)
    words = jnp.concatenate([taps_ref[...], tail], axis=0)
    hi, lo = halves(jnp.concatenate([words] * 8, axis=0))
    group = iota((devices, LANES), 1) // WORDS
    message = jnp.zeros((devices, LANES), F32)
    for j in range(8):
        place = ones_where(jnp.where(hits, rank, -1.0) == float(j))
        place_ref[j] = place
        message = jnp.where(group == j, dot_nt(place, hi) + dot_nt(place, lo), message)
    store_message(message)


def transpose_grid(stage_ref, cells_ref):
    blocks = stage_ref.shape[1] // 8

    @pl.loop(0, blocks, unroll=8)
    def _(b):
        tile = stage_ref[:, pl.ds(pl.multiple_of(b * 8, 8), 8), :].reshape(LANES, LANES)
        cells_ref[pl.ds(pl.multiple_of(b * STRIDE, 8), LANES), :] = tile.T

    quarter = (iota((8, LANES), 1) >> 1) & 3
    for b in range(blocks):
        here = cells_ref[b * STRIDE : b * STRIDE + 8, :]
        next_block = min(b + 1, blocks - 1) * STRIDE
        after = cells_ref[next_block : next_block + 8, :]
        pad = jnp.where(quarter < 3, pltpu.roll(here, LANES - 2, 1), pltpu.roll(after, 6, 1))
        cells_ref[b * STRIDE + LANES : (b + 1) * STRIDE, :] = pad


def spread_taps(words_ref, weight_ref):
    sources = words_ref.shape[0]
    tall = jnp.broadcast_to(words_ref[...].reshape(sources, 1, LANES), (sources, 8, LANES)).reshape(8 * sources, LANES)
    tall = jnp.where((iota(tall.shape, 1) & (WORDS - 1)) == (iota(tall.shape, 0) & 7), tall, 0.0)
    both = jnp.concatenate(halves(tall), axis=1)
    for pair in range(4):
        a, b = iota((2 * LANES, 2 * LANES), 0) & (LANES - 1), iota((2 * LANES, 2 * LANES), 1)
        weight = dot(both, ones_where(a // WORDS == 2 * pair + b // LANES))
        for n in range(2):
            weight_ref[2 * pair + n] = weight[:, n * LANES : (n + 1) * LANES]


def slot_quarter(words_ref, j):
    return jnp.broadcast_to(words_ref[:, j * WORDS + 9 : j * WORDS + 10], (words_ref.shape[0], LANES))


def fold_table():
    a, b = iota((2 * LANES, LANES), 0) & (LANES - 1), iota((2 * LANES, LANES), 1)
    return ones_where(((a >> 3) == (b >> 3)) & ((a & 1) == (b & 1)))


def degrid_slots(first_ref, words_ref, cells_ref, weight_ref, product_ref, store_value):
    sources = words_ref.shape[0]

    @pl.loop(0, sources, unroll=2)
    def _(s):
        at = pl.ds(pl.multiple_of(s * 8, 8), 8)
        for j in range(8):
            product_ref[j, at, :] = weight_ref[j, at, :] * cells_ref[pl.ds(first_ref[j, s], 8), :]

    fold = fold_table()
    lane_quarter = (iota((sources, LANES), 1) >> 1) & 3
    for h in range(2):
        value = jnp.zeros((sources, LANES), F32)
        for g in range(4):
            j = 4 * h + g
            total = product_ref[j, pl.ds(0, sources, stride=8), :]
            for k in range(1, 8):
                total = total + product_ref[j, pl.ds(k, sources, stride=8), :]
            total = jnp.where(slot_quarter(words_ref, j) == lane_quarter.astype(F32), total, 0.0)
            value = jnp.where(lane_quarter == g, dot(jnp.concatenate(halves(total), axis=1), fold), value)
        store_value(h, value)


def gather_degrid(load_value, place_ref, part_ref, degrid_ref):
    sources = place_ref.shape[1]
    quarter = (iota((LANES, sources), 0) >> 1) & 3
    total = None
    for h in range(2):
        turned = load_value(h).T
        for pair in range(2):
            parts = [halves(jnp.where(quarter == g, turned, 0.0)) for g in (2 * pair, 2 * pair + 1)]
            j = 4 * h + 2 * pair
            place = place_ref[j : j + 2].reshape(2 * sources, place_ref.shape[2])
            for n in range(2):
                term = dot(jnp.concatenate([parts[0][n], parts[1][n]], axis=1), place)
                total = term if total is None else total + term
    for n in range(part_ref.shape[0]):
        tile = slice(n * LANES, (n + 1) * LANES)
        part_ref[n] = total[:, tile]
        for t in range(2):
            degrid_ref[t, :, tile] = sum(part_ref[n, pl.ds(2 * g + t, 16, stride=8), :] for g in range(4))


def station_tables(pairs_ref, gather_ref, sum_ref):
    rows = pairs_ref.shape[1]
    for side in range(2):
        hits = ones_where((iota((LANES, rows), 0) & 63) == pairs_ref[side : side + 1, :])
        gather_ref[side] = hits
        for n in range(2):
            sum_ref[:, (2 * side + n) * rows : (2 * side + n + 1) * rows] = hits[:64]


def turn_gains(gains_ref, turned_ref, channels):
    for fc in range(16):
        tiles = []
        for lt in range(2):
            block = gains_ref[:, :, :, 2 * fc + lt, :].reshape(64, LANES)
            hi = block.astype(BF16).astype(F32)
            tiles.append(jnp.concatenate([hi, block - hi], axis=0).T)
        turned_ref[fc * channels : (fc + 1) * channels] = jnp.concatenate(tiles, axis=0)[:channels].astype(BF16)


def gather_gains(turned_ref, gather_ref, left_ref, right_ref, first, last):
    size = turned_ref.shape[0] // 3

    @pl.loop(first, last)
    def _(n):
        at = pl.ds(pl.multiple_of(n * size, CHUNK), size)
        gains = turned_ref[at, :]
        left_ref[at, :] = dot(gains, gather_ref[0])
        right_ref[at, :] = dot(gains, gather_ref[1])


def chunk_rows(plane, channels, chunk):
    return pl.ds(pl.multiple_of(plane * channels + chunk * CHUNK, CHUNK), CHUNK)


def channel_ramp(channels, chunk, width):
    channel = (iota((CHUNK, width), 0) + chunk * CHUNK).astype(F32)
    return 2.0 * channel / (channels - 1) - 1.0


def facet_model(degrid_ref, f, lanes, ramp):
    g = degrid_ref.shape[1] // 2 + f
    return tuple(degrid_ref[0, n : n + 1, lanes] + degrid_ref[1, n : n + 1, lanes] * ramp for n in (f, g))


def error_step(
    chunk, channels, vis_ref, scale_ref, degrid_ref, left_ref, right_ref, error_ref, grad_degrid_ref, width=LANES
):
    rows = vis_ref.shape[2]
    facets = degrid_ref.shape[1] // 2
    at = chunk_rows(0, channels, chunk)
    ramp = channel_ramp(channels, chunk, width)
    for first in range(0, rows, width):
        lanes = slice(first, first + width)
        products, pred_re, pred_im = [], None, None
        for f in range(facets):
            re, im = chunk_rows(2 * f, channels, chunk), chunk_rows(2 * f + 1, channels, chunk)
            are, aim, bre, bim = left_ref[re, lanes], left_ref[im, lanes], right_ref[re, lanes], right_ref[im, lanes]
            mre, mim = facet_model(degrid_ref, f, lanes, ramp)
            pre, pim = are * bre + aim * bim, aim * bre - are * bim
            vre, vim = pre * mre - pim * mim, pre * mim + pim * mre
            pred_re = vre if pred_re is None else pred_re + vre
            pred_im = vim if pred_im is None else pred_im + vim
            products.append((pre, pim))
        ere = scale_ref[:, lanes] * (pred_re - vis_ref[0, at, lanes].astype(F32))
        eim = scale_ref[:, lanes] * (pred_im - vis_ref[1, at, lanes].astype(F32))
        error_ref[0, at, lanes] = ere
        error_ref[1, at, lanes] = eim
        for f in range(facets):
            pre, pim = products[f]
            models = (ere * pre + eim * pim, eim * pre - ere * pim)
            for c in range(2):
                n = c * facets + f
                slope = models[c] * ramp
                grad_degrid_ref[0, n, :, lanes] += models[c][:8] + models[c][8:]
                grad_degrid_ref[1, n, :, lanes] += slope[:8] + slope[8:]


def gain_step(f, chunk, channels, degrid_ref, left_ref, right_ref, error_ref, grads_ref, width=LANES):
    rows = error_ref.shape[2]
    at = chunk_rows(0, channels, chunk)
    ramp = channel_ramp(channels, chunk, width)
    re, im = chunk_rows(2 * f, channels, chunk), chunk_rows(2 * f + 1, channels, chunk)
    for first in range(0, rows, width):
        lanes = slice(first, first + width)
        are, aim, bre, bim = left_ref[re, lanes], left_ref[im, lanes], right_ref[re, lanes], right_ref[im, lanes]
        mre, mim = facet_model(degrid_ref, f, lanes, ramp)
        ere, eim = error_ref[0, at, lanes], error_ref[1, at, lanes]
        qre, qim = ere * mre + eim * mim, eim * mre - ere * mim
        values = (
            (qre * bre - qim * bim, qre * bim + qim * bre),
            (qre * are + qim * aim, qre * aim - qim * are),
        )
        for side in range(2):
            for c in range(2):
                hi, lo = halves(values[side][c])
                start = 2 * side * rows + first
                grads_ref[chunk_rows(c, channels, chunk), start : start + width] = hi
                grads_ref[chunk_rows(c, channels, chunk), start + rows : start + rows + width] = lo


def place_grads(grad_degrid_ref, place_ref, store_value):
    planes = grad_degrid_ref.shape[1]
    rows = grad_degrid_ref.shape[3]
    devices = place_ref.shape[1]
    odd = (iota((8, rows), 0) & 1) == 1
    full = []
    for n in range(planes):
        level = jnp.sum(grad_degrid_ref[0, n], axis=0, keepdims=True)
        slope = jnp.sum(grad_degrid_ref[1, n], axis=0, keepdims=True)
        full.append(jnp.where(odd, slope, level))
    hi, lo = halves(jnp.concatenate(full, axis=0))
    group = (iota((devices, LANES), 1) >> 1) & 3
    for h in range(2):
        value = jnp.zeros((devices, LANES), F32)
        for g in range(4):
            place = place_ref[4 * h + g]
            value = jnp.where(group == g, dot_nt(place, hi) + dot_nt(place, lo), value)
        store_value(h, value)


class Exchange:
    def __init__(self, send_ref, middle_ref, receive_ref, sems, time, group):
        self.send_ref, self.middle_ref, self.receive_ref, self.sems = send_ref, middle_ref, receive_ref, sems
        self.time, self.group = time, group
        self.times, self.groups = send_ref.shape[:2]

    def start(self):
        to_middle = self.middle_ref.at[:, self.time]
        pltpu.make_async_copy(self.send_ref.at[self.time], to_middle, self.sems.at[1]).start()

        @pl.loop(1, self.times)
        def _(n):
            to = lax.rem(self.time + n, self.times)
            remote(self.send_ref.at[to], to_middle, self.sems.at[0], self.sems.at[1], (to, self.group)).start()

    def pass_on(self):
        wait_bytes(self.middle_ref, self.sems.at[1])
        to_end = self.receive_ref.at[:, self.group]
        pltpu.make_async_copy(self.middle_ref.at[self.group], to_end, self.sems.at[3]).start()

        @pl.loop(1, self.groups)
        def _(n):
            to = lax.rem(self.group + n, self.groups)
            remote(self.middle_ref.at[to], to_end, self.sems.at[2], self.sems.at[3], (self.time, to)).start()

    def wait_receive(self):
        wait_bytes(self.receive_ref, self.sems.at[3])

    def wait_send(self):
        wait_bytes(self.send_ref.at[pl.ds(0, self.times - 1)], self.sems.at[0])
        wait_bytes(self.middle_ref.at[pl.ds(0, self.groups - 1)], self.sems.at[2])


class DirectExchange:
    def __init__(self, send_ref, middle_ref, receive_ref, sems, place, levels):
        self.send_ref, self.middle_ref, self.receive_ref, self.sems = send_ref, middle_ref, receive_ref, sems
        self.time, self.level, self.core = place
        self.levels = levels

    def start(self):
        nodes, levels = self.send_ref.shape[0], self.levels
        me = self.time * levels + self.level
        to_middle = self.middle_ref.at[:, me]
        pltpu.make_async_copy(self.send_ref.at[me], to_middle, self.sems.at[1]).start()

        @pl.loop(0, nodes - 1)
        def _(n):
            to, level = far_first(n, self.time, self.level, nodes // levels, levels)
            device = (to, 2 * level + self.core)
            remote(self.send_ref.at[to * levels + level], to_middle, self.sems.at[0], self.sems.at[1], device).start()

    def pass_on(self):
        wait_bytes(self.middle_ref, self.sems.at[1])
        to_end = self.receive_ref.at[self.core]
        pltpu.make_async_copy(self.middle_ref.at[self.core], to_end, self.sems.at[3]).start()
        pair = (self.time, 2 * self.level + 1 - self.core)
        remote(self.middle_ref.at[1 - self.core], to_end, self.sems.at[2], self.sems.at[3], pair).start()

    def wait_receive(self):
        wait_bytes(self.receive_ref, self.sems.at[3])

    def wait_send(self):
        wait_bytes(self.send_ref.at[pl.ds(0, self.send_ref.shape[0] - 1)], self.sems.at[0])
        wait_bytes(self.middle_ref.at[0], self.sems.at[2])


def far_first(n, time, level, times, levels):
    side = math.isqrt(times)

    def offset(d):
        return 2 + d - (d // 2) * (2 * d - 1)

    x = lax.rem(time // side + offset(n // (side * levels)), side)
    y = lax.rem(lax.rem(time, side) + offset(lax.rem(n // levels, side)), side)
    return x * side + y, lax.rem(level + offset(lax.rem(n, levels)), levels)


def remote(source, target, send_sem, receive_sem, device):
    return pltpu.make_async_remote_copy(
        src_ref=source, dst_ref=target, send_sem=send_sem, recv_sem=receive_sem,
        device_id=device, device_id_type=pl.DeviceIdType.MESH,
    )


def wait_bytes(ref, sem):
    pltpu.make_async_copy(ref, ref, sem).wait()


def main_kernel(
    owner_ref, offset_ref, taps_ref, gain_ref, vis_ref, noise_ref, keep_ref, pairs_ref, sky_ref,
    words_ref, firsts_ref, grad_ref, data_ref,
    send_a, mid_a, got_a, send_c, mid_c, got_c, send_e, mid_e, got_e, own, gains, send_g, pair_g, sum_g, got_g, near, prior,
    place, stage, cells, weight, product, slots, part, degrid, turned, gather, sums, scale,
    left, right, error, grads_even, grads_odd, grad_degrid,
    sky_sem, slot_sem, sem_a, sem_c, sem_e, gain_sem, pair_sem, near_sem, sum_sem,
    channels, times, groups,
):
    time, group = lax.axis_index("tm"), lax.axis_index("bl")
    devices = times * groups
    level, core = group // 2, lax.rem(group, 2)
    facets = gain_ref.shape[1]
    barrier = pltpu.get_barrier_semaphore()

    levels = groups // 2
    pair = (time, group + 1 - 2 * core)

    def greet(device):
        pl.semaphore_signal(barrier, inc=1, device_id=device, device_id_type=pl.DeviceIdType.MESH)

    @pl.loop(0, times * levels - 1)
    def _(n):
        to, at = far_first(n, time, level, times, levels)
        greet((to, 2 * at + core))

    @pl.loop(0, levels)
    def _(n):
        greet((time, 2 * n + 1 - core))

    sky_copy = pltpu.make_async_copy(sky_ref, stage, sky_sem)
    sky_copy.start()

    def store_message(message):
        for t in range(devices):
            send_a[t // 2, t % 2] = message[t : t + 1, :]

    form_slots(owner_ref, offset_ref, taps_ref, place, store_message)
    pl.semaphore_wait(barrier, times * levels - 1 + levels)

    first = DirectExchange(send_a, mid_a, got_a, sem_a, (time, level, core), levels)
    second = DirectExchange(send_c, mid_c, got_c, sem_c, (time, level, core), levels)
    third = Exchange(send_e, mid_e, got_e, sem_e, time, group)
    first.start()

    for f in range(facets):
        for c in range(2):
            for lt in range(2):
                wide = min(LANES, channels - lt * LANES)
                block = gain_ref[:, f, c, lt * LANES : lt * LANES + wide]
                if wide < LANES:
                    block = jnp.concatenate([block, jnp.zeros((block.shape[0], LANES - wide), F32)], axis=1)
                own[:, 4 * f + 2 * c + lt, :] = block
    mine = gains.at[level, core]
    pltpu.make_async_copy(own, mine, gain_sem.at[1]).start()

    @pl.loop(1, groups // 2)
    def _(n):
        to = lax.rem(group + 2 * n, groups)
        remote(own, mine, gain_sem.at[0], gain_sem.at[1], (time, to)).start()

    def next_interval(n, step):
        to = lax.rem(time + step, times)
        return remote(own, near.at[n], near_sem.at[2 * n], near_sem.at[2 * n + 1], (to, group))

    below, above = next_interval(0, 1), next_interval(1, times - 1)
    below.start()
    above.start()

    sky_copy.wait()
    transpose_grid(stage, cells)
    first.pass_on()
    scale[...] = noise_ref[...] * keep_ref[...].astype(F32)
    station_tables(pairs_ref, gather, sums)
    grad_degrid[...] = jnp.zeros_like(grad_degrid)

    first.wait_receive()
    for c in range(2):
        words_ref[pl.ds(c, devices // 2, stride=2), :] = got_a[c, :, 0, :]
    turned_words = words_ref[...].T
    firsts = jnp.concatenate([turned_words[j * WORDS + 8 : j * WORDS + 9, :] for j in range(8)], axis=0)
    firsts_ref[...] = jnp.clip(firsts.astype(I32), 0, cells.shape[0] - 8)
    slot_copy = pltpu.make_async_copy(firsts_ref, slots, slot_sem)
    slot_copy.start()
    spread_taps(words_ref, weight)
    column = gains.at[:, core]
    wait_bytes(column, gain_sem.at[1])
    remote(column, column, pair_sem.at[0], pair_sem.at[1], pair).start()
    slot_copy.wait()

    def store_value(h, value):
        send_c[:, :, h, :] = value.reshape(devices // 2, 2, LANES)

    degrid_slots(slots, words_ref, cells, weight, product, store_value)
    second.start()
    wait_bytes(column, pair_sem.at[1])
    turn_gains(gains, turned, channels)
    gather_gains(turned, gather, left, right, 0, 2)
    second.pass_on()
    gather_gains(turned, gather, left, right, 2, 3)
    below.wait()
    above.wait()
    for f in range(facets):
        for c in range(2):
            smooth = []
            for lt in range(2):
                n = 4 * f + 2 * c + lt
                here = own[:, n, :]
                down = jnp.where(time > 0, here - near[0, :, n, :], 0.0)
                up = jnp.where(time < times - 1, near[1, :, n, :] - here, 0.0)
                smooth.append(smoothness * (down - up))
            prior[2 * f + c] = jnp.concatenate(smooth, axis=1)

    second.wait_receive()
    for h in range(2):
        for c in range(2):
            part[h, pl.ds(c, devices // 2, stride=2), :] = got_c[c, :, h, :]
    gather_degrid(lambda h: part[h], place, part, degrid)

    @pl.loop(0, channels // CHUNK)
    def _(chunk):
        error_step(chunk, channels, vis_ref, scale, degrid, left, right, error, grad_degrid, 2 * LANES)

    def store_grad(h, value):
        send_e[:, :, h, :] = value.reshape(times, groups, LANES)

    place_grads(grad_degrid, place, store_grad)
    third.start()

    batch = 2

    def these(b):
        return pl.ds(b * batch, batch)

    def combine(b):
        wait_bytes(pair_g.at[these(b)], sum_sem.at[3 + b])
        for fc in range(b * batch, (b + 1) * batch):
            sum_g[:, fc] = send_g[core, fc] + pair_g[fc]
        to_end = got_g.at[level, these(b)]
        pltpu.make_async_copy(sum_g.at[level, these(b)], to_end, sum_sem.at[2]).start()

        @pl.loop(1, groups // 2)
        def _(n):
            to = lax.rem(level + n, groups // 2)
            remote(sum_g.at[to, these(b)], to_end, sum_sem.at[1], sum_sem.at[2], (time, 2 * to + core)).start()

    for f in range(facets):
        grads = grads_even if f % 2 == 0 else grads_odd

        @pl.loop(0, channels // CHUNK, unroll=5)
        def _(chunk):
            gain_step(f, chunk, channels, degrid, left, right, error, grads, 2 * LANES)

        for c in range(2):
            value = dot_nt(sums[...], grads[c * channels : (c + 1) * channels, :])
            value = jnp.concatenate([value, jnp.zeros((64, 2 * LANES - channels), F32)], axis=1)
            value = value.reshape(groups // 2, 2, 8, 2 * LANES)
            for k in range(2):
                send_g[k, 2 * f + c] = value[:, k]
        b = (2 * f + 1) // batch
        if (2 * f + 2) % batch == 0:
            remote(
                send_g.at[1 - core, these(b)], pair_g.at[these(b)], sum_sem.at[0], sum_sem.at[3 + b], pair
            ).start()
            if b > 0:
                combine(b - 1)
            if b == 3:
                third.pass_on()
    combine(2 * facets // batch - 1)

    third.wait_receive()
    grad_ref[...] = got_e[...].reshape(devices, 2, LANES)
    wait_bytes(got_g, sum_sem.at[2])
    for f in range(facets):
        for c in range(2):
            fc = 2 * f + c
            total = prior[fc]
            for n in range(levels):
                total = total + got_g[n, fc]
            data_ref[:, f, c, :] = total[:, :channels]

    first.wait_send()
    second.wait_send()
    third.wait_send()
    wait_bytes(gains.at[pl.ds(0, groups // 2 - 1), 0], gain_sem.at[0])
    wait_bytes(column, pair_sem.at[0])
    wait_bytes(pair_g, sum_sem.at[0])
    wait_bytes(got_g.at[pl.ds(0, groups // 2 - 1)], sum_sem.at[1])


def scatter_kernel(first_ref, words_ref, grad_ref, sky_ref, weight_ref, spread, cells, stage, sem):
    sources = grad_ref.shape[0]
    blocks = stage.shape[1] // 8
    for b in range(blocks):
        cells[b * STRIDE : (b + 1) * STRIDE, :] = jnp.zeros((STRIDE, LANES), F32)
    spread_taps(words_ref, weight_ref)
    fold = fold_table()
    lane_quarter = (iota((sources, LANES), 1) >> 1) & 3
    for h in range(2):
        block = grad_ref[:, h, :]
        for g in range(4):
            j = 4 * h + g
            part = jnp.concatenate(halves(jnp.where(lane_quarter == g, block, 0.0)), axis=1)
            spread[j] = jnp.where(slot_quarter(words_ref, j) == lane_quarter.astype(F32), dot(part, fold), 0.0)

    @pl.loop(0, sources)
    def _(s):
        at = pl.ds(pl.multiple_of(s * 8, 8), 8)
        for j in range(8):
            cells[pl.ds(first_ref[j, s], 8), :] += weight_ref[j, at, :] * spread[j, pl.ds(s, 1), :]

    quarter = (iota((8, LANES), 1) >> 1) & 3
    last = jnp.zeros((8, LANES), F32)
    for b in range(blocks):
        pads = cells[b * STRIDE + LANES : (b + 1) * STRIDE, :]
        head = slice(b * STRIDE, b * STRIDE + 8)
        cells[head, :] = cells[head, :] + jnp.where(quarter > 0, pltpu.roll(pads, 2, 1), last)
        last = pltpu.roll(pads, LANES - 6, 1)

    pieces = 4
    length = blocks // pieces

    def copy(n):
        at = pl.ds(n * length * 8, length * 8)
        return pltpu.make_async_copy(stage.at[:, at, :], sky_ref.at[:, at, :], sem.at[n])

    for n in range(pieces):

        @pl.loop(n * length, (n + 1) * length, unroll=8)
        def _(b):
            turned = cells[pl.ds(pl.multiple_of(b * STRIDE, 8), LANES), :].T
            stage[:, pl.ds(pl.multiple_of(b * 8, 8), 8), :] = turned.reshape(16, 8, LANES)

        copy(n).start()
    for n in range(pieces):
        copy(n).wait()


def vmem(count):
    return [pl.BlockSpec(memory_space=pltpu.VMEM)] * count


def shape(dims, dtype=F32):
    return jax.ShapeDtypeStruct(dims, dtype)


def params():
    return pltpu.CompilerParams(vmem_limit_bytes=VMEM_LIMIT)


def body(
    visibilities, noise_weight, keep_flag, station_pairs, tile_owner, tile_offset, kernel_taps, gain_field, sky_grid
):
    rows = visibilities.shape[0]
    channels = visibilities.shape[2]
    devices = lax.axis_size("tm") * lax.axis_size("bl")
    parts, facets, terms, cells = sky_grid.shape
    lines = cells // LANES
    sky = sky_grid.reshape(parts, facets, terms, lines, LANES).transpose(0, 1, 3, 2, 4)
    sky = sky.reshape(parts * facets, lines * terms, LANES)

    times, groups = lax.axis_size("tm"), lax.axis_size("bl")
    pairs = pltpu.VMEM((times, groups, 2, LANES), F32)
    middle_pairs = pltpu.VMEM((groups, times, 2, LANES), F32)
    tiles = facets * 4
    words, firsts, grad, data = pl.pallas_call(
        functools.partial(
            main_kernel, channels=channels, times=times, groups=groups
        ),
        out_shape=(
            shape((devices, LANES)), shape((8, devices), I32), shape((devices, 2, LANES)),
            shape(gain_field.shape[1:]),
        ),
        in_specs=vmem(8) + [pl.BlockSpec(memory_space=pl.ANY)],
        out_specs=tuple(vmem(4)),
        scratch_shapes=[
            pltpu.VMEM((devices // 2, 2, 1, LANES), F32),
            pltpu.VMEM((2, devices // 2, 1, LANES), F32),
            pltpu.VMEM((2, devices // 2, 1, LANES), F32),
            pltpu.VMEM((devices // 2, 2, 2, LANES), F32),
            pltpu.VMEM((2, devices // 2, 2, LANES), F32),
            pltpu.VMEM((2, devices // 2, 2, LANES), F32),
            pairs,
            middle_pairs,
            pairs,
            pltpu.VMEM((8, tiles, LANES), F32),
            pltpu.VMEM((groups // 2, 2, 8, tiles, LANES), F32),
            pltpu.VMEM((2, 2 * facets, groups // 2, 8, 2 * LANES), F32),
            pltpu.VMEM((2 * facets, groups // 2, 8, 2 * LANES), F32),
            pltpu.VMEM((groups // 2, 2 * facets, 8, 2 * LANES), F32),
            pltpu.VMEM((groups // 2, 2 * facets, 8, 2 * LANES), F32),
            pltpu.VMEM((2, 8, tiles, LANES), F32),
            pltpu.VMEM((2 * facets, 8, 2 * LANES), F32),
            pltpu.VMEM((8, devices, rows), BF16),
            pltpu.VMEM(sky.shape, F32),
            pltpu.VMEM((cells // BLOCK * STRIDE, LANES), F32),
            pltpu.VMEM((8, devices * 8, LANES), F32),
            pltpu.VMEM((8, devices * 8, LANES), F32),
            pltpu.SMEM((8, devices), I32),
            pltpu.VMEM((rows // LANES, LANES, LANES), F32),
            pltpu.VMEM((2, 16, rows), F32),
            pltpu.VMEM((2 * facets * channels, LANES), BF16),
            pltpu.VMEM((2, LANES, rows), BF16),
            pltpu.VMEM((64, 4 * rows), BF16),
            pltpu.VMEM((1, rows), F32),
            pltpu.VMEM((2 * facets * channels, rows), F32),
            pltpu.VMEM((2 * facets * channels, rows), F32),
            pltpu.VMEM((2, channels, rows), F32),
            pltpu.VMEM((2 * channels, 4 * rows), BF16),
            pltpu.VMEM((2 * channels, 4 * rows), BF16),
            pltpu.VMEM((2, 2 * facets, 8, rows), F32),
            pltpu.SemaphoreType.DMA,
            pltpu.SemaphoreType.DMA,
            pltpu.SemaphoreType.DMA((4,)),
            pltpu.SemaphoreType.DMA((4,)),
            pltpu.SemaphoreType.DMA((4,)),
            pltpu.SemaphoreType.DMA((2,)),
            pltpu.SemaphoreType.DMA((2,)),
            pltpu.SemaphoreType.DMA((4,)),
            pltpu.SemaphoreType.DMA((3 + facets,)),
        ],
        compiler_params=pltpu.CompilerParams(
            vmem_limit_bytes=62 << 20, collective_id=0, has_side_effects=True
        ),
        name="main",
    )(
        tile_owner.reshape(1, rows), tile_offset.reshape(1, rows), kernel_taps, gain_field[0],
        visibilities.transpose(1, 2, 0), noise_weight.reshape(1, rows), keep_flag.reshape(1, rows),
        station_pairs, sky,
    )

    out_grid = pl.pallas_call(
        scatter_kernel,
        out_shape=shape(sky.shape),
        in_specs=[pl.BlockSpec(memory_space=pltpu.SMEM)] + vmem(2),
        out_specs=pl.BlockSpec(memory_space=pl.ANY),
        scratch_shapes=[
            pltpu.VMEM((8, devices * 8, LANES), F32),
            pltpu.VMEM((8, devices, LANES), F32),
            pltpu.VMEM((cells // BLOCK * STRIDE, LANES), F32),
            pltpu.VMEM(sky.shape, F32),
            pltpu.SemaphoreType.DMA((4,)),
        ],
        compiler_params=params(),
        name="scatter",
    )(firsts, words, grad)
    grid_gradient = out_grid.reshape(parts, facets, lines, terms, LANES).transpose(0, 1, 3, 2, 4)
    grid_gradient = grid_gradient.reshape(sky_grid.shape)

    return (data[None], grid_gradient)


def solution(mesh):
    split = ("tm", "bl")
    return jax.shard_map(
        body,
        mesh=mesh,
        in_specs=(
            P(split, None, None),
            P(split),
            P(split),
            P(None, split),
            P(split, None),
            P(split),
            P(None, split),
            P("tm", "bl", None, None, None),
            P(None, None, None, split),
        ),
        out_specs=(P("tm", "bl", None, None, None), P(None, None, None, split)),
        check_vma=False,
    )
```

```python
import functools

import jax
import jax.numpy as jnp
from jax import lax
from jax.experimental import pallas as pl
from jax.experimental.pallas import tpu as pltpu
from jax.sharding import PartitionSpec as P

smoothness = 4.0
F32, BF16, I32 = jnp.float32, jnp.bfloat16, jnp.int32
LANES = 128
WORDS = 16
BLOCK = 512
STRIDE = LANES + 8
CHUNK = 16
VMEM_LIMIT = 56 << 20
NT = (((1,), (1,)), ((), ()))


def iota(shape, axis):
    return lax.broadcasted_iota(I32, shape, axis)


def halves(x):
    hi = x.astype(BF16)
    return hi, (x - hi.astype(F32)).astype(BF16)


def dot(x, y):
    return jnp.dot(x, y, preferred_element_type=F32)


def dot_nt(x, y):
    return lax.dot_general(x, y, NT, preferred_element_type=F32)


def ones_where(mask):
    return jnp.where(mask, 1.0, 0.0).astype(BF16)


def place_product(place_ref, both):
    slots, devices, rows = place_ref.shape
    product = dot_nt(place_ref[...].reshape(slots * devices, rows), both)
    return (product[:, :LANES] + product[:, LANES:]).reshape(slots, devices, LANES)


def form_slots(owner_ref, offset_ref, taps_ref, place_ref, store_message):
    devices, rows = place_ref.shape[1:]
    hits = iota((devices, rows), 0) == owner_ref[...]
    earlier = ones_where(iota((rows, rows), 0) < iota((rows, rows), 1))
    counts = dot(ones_where(hits), earlier)
    rank = jnp.sum(jnp.where(hits, counts, 0.0), axis=0, keepdims=True)
    offset = offset_ref[...]
    row = (offset >> 9) * STRIDE + (offset & (LANES - 1))
    tail = jnp.where(iota((WORDS - 8, rows), 0) == 0, row, (offset >> 7) & 3).astype(F32)
    words = jnp.concatenate([taps_ref[...], tail], axis=0)
    both = jnp.concatenate(halves(jnp.concatenate([words] * 8, axis=0)), axis=0)
    rank = jnp.where(hits, rank, -1.0)
    for j in range(8):
        place_ref[j] = ones_where(rank == float(j))
    tall = place_product(place_ref, both)
    group = iota((devices, LANES), 1) // WORDS
    message = jnp.zeros((devices, LANES), F32)
    for j in range(8):
        message = jnp.where(group == j, tall[j], message)
    store_message(message)


def transpose_grid(stage_ref, cells_ref):
    blocks = stage_ref.shape[1] // 8

    @pl.loop(0, blocks, unroll=8)
    def _(b):
        tile = stage_ref[:, pl.ds(pl.multiple_of(b * 8, 8), 8), :].reshape(LANES, LANES)
        cells_ref[pl.ds(pl.multiple_of(b * STRIDE, 8), LANES), :] = tile.T

    quarter = (iota((8, LANES), 1) >> 1) & 3
    for b in range(blocks):
        here = cells_ref[b * STRIDE : b * STRIDE + 8, :]
        next_block = min(b + 1, blocks - 1) * STRIDE
        after = cells_ref[next_block : next_block + 8, :]
        pad = jnp.where(quarter < 3, pltpu.roll(here, LANES - 2, 1), pltpu.roll(after, 6, 1))
        cells_ref[b * STRIDE + LANES : (b + 1) * STRIDE, :] = pad


def spread_taps(words_ref, weight_ref):
    sources = words_ref.shape[0]
    tall = jnp.broadcast_to(words_ref[...].reshape(sources, 1, LANES), (sources, 8, LANES)).reshape(8 * sources, LANES)
    tall = jnp.where((iota(tall.shape, 1) & (WORDS - 1)) == (iota(tall.shape, 0) & 7), tall, 0.0)
    both = jnp.concatenate(halves(tall), axis=1)
    for pair in range(4):
        a, b = iota((2 * LANES, 2 * LANES), 0) & (LANES - 1), iota((2 * LANES, 2 * LANES), 1)
        weight = dot(both, ones_where(a // WORDS == 2 * pair + b // LANES))
        for n in range(2):
            weight_ref[2 * pair + n] = weight[:, n * LANES : (n + 1) * LANES]


def slot_quarter(words_ref, j):
    return jnp.broadcast_to(words_ref[:, j * WORDS + 9 : j * WORDS + 10], (words_ref.shape[0], LANES))


def fold_table():
    a, b = iota((2 * LANES, LANES), 0) & (LANES - 1), iota((2 * LANES, LANES), 1)
    return ones_where(((a >> 3) == (b >> 3)) & ((a & 1) == (b & 1)))


def degrid_slots(first_ref, words_ref, cells_ref, weight_ref, product_ref, store_value):
    sources = words_ref.shape[0]

    @pl.loop(0, sources, unroll=2)
    def _(s):
        at = pl.ds(pl.multiple_of(s * 8, 8), 8)
        for j in range(8):
            product_ref[j, at, :] = weight_ref[j, at, :] * cells_ref[pl.ds(first_ref[j, s], 8), :]

    fold = fold_table()
    lane_quarter = (iota((sources, LANES), 1) >> 1) & 3
    for h in range(2):
        value = jnp.zeros((sources, LANES), F32)
        for g in range(4):
            j = 4 * h + g
            total = product_ref[j, pl.ds(0, sources, stride=8), :]
            for k in range(1, 8):
                total = total + product_ref[j, pl.ds(k, sources, stride=8), :]
            total = jnp.where(slot_quarter(words_ref, j) == lane_quarter.astype(F32), total, 0.0)
            value = jnp.where(lane_quarter == g, dot(jnp.concatenate(halves(total), axis=1), fold), value)
        store_value(h, value)


def gather_degrid(load_value, place_ref, part_ref, degrid_ref):
    sources = place_ref.shape[1]
    quarter = (iota((LANES, sources), 0) >> 1) & 3
    total = None
    for h in range(2):
        turned = load_value(h).T
        for pair in range(2):
            parts = [halves(jnp.where(quarter == g, turned, 0.0)) for g in (2 * pair, 2 * pair + 1)]
            j = 4 * h + 2 * pair
            place = place_ref[j : j + 2].reshape(2 * sources, place_ref.shape[2])
            for n in range(2):
                term = dot(jnp.concatenate([parts[0][n], parts[1][n]], axis=1), place)
                total = term if total is None else total + term
    for n in range(part_ref.shape[0]):
        tile = slice(n * LANES, (n + 1) * LANES)
        part_ref[n] = total[:, tile]
        for t in range(2):
            degrid_ref[t, :, tile] = sum(part_ref[n, pl.ds(2 * g + t, 16, stride=8), :] for g in range(4))


def station_tables(pairs_ref, gather_ref, sum_ref):
    rows = pairs_ref.shape[1]
    for side in range(2):
        hits = ones_where((iota((LANES, rows), 0) & 63) == pairs_ref[side : side + 1, :])
        gather_ref[side] = hits
        for n in range(2):
            sum_ref[:, (2 * side + n) * rows : (2 * side + n + 1) * rows] = hits[:64]


def turn_gains(gains_ref, turned_ref, channels):
    for fc in range(16):
        tiles = []
        for lt in range(2):
            block = gains_ref[:, :, :, 2 * fc + lt, :].reshape(64, LANES)
            hi = block.astype(BF16).astype(F32)
            tiles.append(jnp.concatenate([hi, block - hi], axis=0).T)
        turned_ref[fc * channels : (fc + 1) * channels] = jnp.concatenate(tiles, axis=0)[:channels].astype(BF16)


def gather_gains(turned_ref, gather_ref, left_ref, right_ref, first, last):
    size = turned_ref.shape[0] // 3

    @pl.loop(first, last)
    def _(n):
        at = pl.ds(pl.multiple_of(n * size, CHUNK), size)
        gains = turned_ref[at, :]
        left_ref[at, :] = dot(gains, gather_ref[0])
        right_ref[at, :] = dot(gains, gather_ref[1])


def chunk_rows(plane, channels, chunk):
    return pl.ds(pl.multiple_of(plane * channels + chunk * CHUNK, CHUNK), CHUNK)


def channel_ramp(channels, chunk, width):
    channel = (iota((CHUNK, width), 0) + chunk * CHUNK).astype(F32)
    return 2.0 * channel / (channels - 1) - 1.0


def facet_model(degrid_ref, f, lanes, ramp):
    g = degrid_ref.shape[1] // 2 + f
    return tuple(degrid_ref[0, n : n + 1, lanes] + degrid_ref[1, n : n + 1, lanes] * ramp for n in (f, g))


def pair_step(chunk, channels, left_ref, right_ref, pair_ref, facets, width=LANES):
    for f in range(facets):
        re, im = chunk_rows(2 * f, channels, chunk), chunk_rows(2 * f + 1, channels, chunk)
        for first in range(0, left_ref.shape[1], width):
            lanes = slice(first, first + width)
            are, aim, bre, bim = left_ref[re, lanes], left_ref[im, lanes], right_ref[re, lanes], right_ref[im, lanes]
            pair_ref[re, lanes] = are * bre + aim * bim
            pair_ref[im, lanes] = aim * bre - are * bim


def error_step(
    chunk, channels, vis_ref, scale_ref, degrid_ref, pair_ref, error_ref, grad_degrid_ref, width=LANES
):
    rows = vis_ref.shape[2]
    facets = degrid_ref.shape[1] // 2
    at = chunk_rows(0, channels, chunk)
    ramp = channel_ramp(channels, chunk, width)
    for first in range(0, rows, width):
        lanes = slice(first, first + width)
        pred_re = pred_im = None
        for f in range(facets):
            re, im = chunk_rows(2 * f, channels, chunk), chunk_rows(2 * f + 1, channels, chunk)
            pre, pim = pair_ref[re, lanes], pair_ref[im, lanes]
            mre, mim = facet_model(degrid_ref, f, lanes, ramp)
            vre, vim = pre * mre - pim * mim, pre * mim + pim * mre
            pred_re = vre if pred_re is None else pred_re + vre
            pred_im = vim if pred_im is None else pred_im + vim
        ere = scale_ref[:, lanes] * (pred_re - vis_ref[0, at, lanes].astype(F32))
        eim = scale_ref[:, lanes] * (pred_im - vis_ref[1, at, lanes].astype(F32))
        error_ref[0, at, lanes] = ere
        error_ref[1, at, lanes] = eim
        for f in range(facets):
            re, im = chunk_rows(2 * f, channels, chunk), chunk_rows(2 * f + 1, channels, chunk)
            pre, pim = pair_ref[re, lanes], pair_ref[im, lanes]
            models = (ere * pre + eim * pim, eim * pre - ere * pim)
            for c in range(2):
                n = c * facets + f
                slope = models[c] * ramp
                grad_degrid_ref[0, n, :, lanes] += models[c][:8] + models[c][8:]
                grad_degrid_ref[1, n, :, lanes] += slope[:8] + slope[8:]


def gain_step(f, chunk, channels, degrid_ref, left_ref, right_ref, error_ref, grads_ref, width=LANES):
    rows = error_ref.shape[2]
    at = chunk_rows(0, channels, chunk)
    ramp = channel_ramp(channels, chunk, width)
    re, im = chunk_rows(2 * f, channels, chunk), chunk_rows(2 * f + 1, channels, chunk)
    for first in range(0, rows, width):
        lanes = slice(first, first + width)
        are, aim, bre, bim = left_ref[re, lanes], left_ref[im, lanes], right_ref[re, lanes], right_ref[im, lanes]
        mre, mim = facet_model(degrid_ref, f, lanes, ramp)
        ere, eim = error_ref[0, at, lanes], error_ref[1, at, lanes]
        qre, qim = ere * mre + eim * mim, eim * mre - ere * mim
        values = (
            (qre * bre - qim * bim, qre * bim + qim * bre),
            (qre * are + qim * aim, qre * aim - qim * are),
        )
        for side in range(2):
            for c in range(2):
                hi, lo = halves(values[side][c])
                start = 2 * side * rows + first
                grads_ref[chunk_rows(c, channels, chunk), start : start + width] = hi
                grads_ref[chunk_rows(c, channels, chunk), start + rows : start + rows + width] = lo


def place_grads(grad_degrid_ref, place_ref, store_value):
    planes = grad_degrid_ref.shape[1]
    rows = grad_degrid_ref.shape[3]
    devices = place_ref.shape[1]
    odd = (iota((8, rows), 0) & 1) == 1
    full = []
    for n in range(planes):
        level = jnp.sum(grad_degrid_ref[0, n], axis=0, keepdims=True)
        slope = jnp.sum(grad_degrid_ref[1, n], axis=0, keepdims=True)
        full.append(jnp.where(odd, slope, level))
    tall = place_product(place_ref, jnp.concatenate(halves(jnp.concatenate(full, axis=0)), axis=0))
    group = (iota((devices, LANES), 1) >> 1) & 3
    for h in range(2):
        value = tall[4 * h]
        for g in range(1, 4):
            value = jnp.where(group == g, tall[4 * h + g], value)
        store_value(h, value)


class Exchange:
    def __init__(self, send_ref, middle_ref, receive_ref, sems, time, group):
        self.send_ref, self.middle_ref, self.receive_ref, self.sems = send_ref, middle_ref, receive_ref, sems
        self.time, self.group = time, group
        self.times, self.groups = send_ref.shape[:2]

    def start(self):
        to_middle = self.middle_ref.at[:, self.time]
        pltpu.make_async_copy(self.send_ref.at[self.time], to_middle, self.sems.at[1]).start()

        @pl.loop(1, self.times)
        def _(n):
            to = lax.rem(self.time + n, self.times)
            remote(self.send_ref.at[to], to_middle, self.sems.at[0], self.sems.at[1], (to, self.group)).start()

    def pass_on(self):
        wait_bytes(self.middle_ref, self.sems.at[1])
        to_end = self.receive_ref.at[:, self.group]
        pltpu.make_async_copy(self.middle_ref.at[self.group], to_end, self.sems.at[3]).start()

        @pl.loop(1, self.groups)
        def _(n):
            to = lax.rem(self.group + n, self.groups)
            remote(self.middle_ref.at[to], to_end, self.sems.at[2], self.sems.at[3], (self.time, to)).start()

    def wait_receive(self):
        wait_bytes(self.receive_ref, self.sems.at[3])

    def wait_send(self):
        wait_bytes(self.send_ref.at[pl.ds(0, self.times - 1)], self.sems.at[0])
        wait_bytes(self.middle_ref.at[pl.ds(0, self.groups - 1)], self.sems.at[2])


def remote(source, target, send_sem, receive_sem, device):
    return pltpu.make_async_remote_copy(
        src_ref=source, dst_ref=target, send_sem=send_sem, recv_sem=receive_sem,
        device_id=device, device_id_type=pl.DeviceIdType.MESH,
    )


def wait_bytes(ref, sem):
    pltpu.make_async_copy(ref, ref, sem).wait()


def main_kernel(
    owner_ref, offset_ref, taps_ref, gain_ref, vis_ref, noise_ref, keep_ref, pairs_ref, sky_ref,
    words_ref, firsts_ref, grad_ref, data_ref,
    send_a, mid_a, got_a, send_c, mid_c, got_c, send_e, mid_e, got_e, own, gains, send_g, pair_g, sum_g, got_g, near,
    place, stage, cells, weight, product, slots, part, degrid, turned, gather, sums, scale,
    left, right, pairs, error, grads_even, grads_odd, grad_degrid,
    sky_sem, slot_sem, sem_a, sem_c, sem_e, gain_sem, pair_sem, near_sem, sum_sem,
    channels, times, groups,
):
    time, group = lax.axis_index("tm"), lax.axis_index("bl")
    devices = times * groups
    level, core = group // 2, lax.rem(group, 2)
    facets = gain_ref.shape[1]
    barrier = pltpu.get_barrier_semaphore()

    @pl.loop(1, times)
    def _(n):
        to = (lax.rem(time + n, times), group)
        pl.semaphore_signal(barrier, inc=1, device_id=to, device_id_type=pl.DeviceIdType.MESH)

    @pl.loop(1, groups)
    def _(n):
        to = (time, lax.rem(group + n, groups))
        pl.semaphore_signal(barrier, inc=1, device_id=to, device_id_type=pl.DeviceIdType.MESH)

    sky_copy = pltpu.make_async_copy(sky_ref, stage, sky_sem)
    sky_copy.start()

    def store_message(message):
        for t in range(devices):
            send_a[t // groups, t % groups] = message[t : t + 1, :]

    form_slots(owner_ref, offset_ref, taps_ref, place, store_message)
    pl.semaphore_wait(barrier, times + groups - 2)

    first = Exchange(send_a, mid_a, got_a, sem_a, time, group)
    second = Exchange(send_c, mid_c, got_c, sem_c, time, group)
    third = Exchange(send_e, mid_e, got_e, sem_e, time, group)
    first.start()

    for f in range(facets):
        for c in range(2):
            for lt in range(2):
                wide = min(LANES, channels - lt * LANES)
                block = gain_ref[:, f, c, lt * LANES : lt * LANES + wide]
                if wide < LANES:
                    block = jnp.concatenate([block, jnp.zeros((block.shape[0], LANES - wide), F32)], axis=1)
                own[:, 4 * f + 2 * c + lt, :] = block
    mine = gains.at[level, core]
    pltpu.make_async_copy(own, mine, gain_sem.at[1]).start()

    @pl.loop(1, groups // 2)
    def _(n):
        to = lax.rem(group + 2 * n, groups)
        remote(own, mine, gain_sem.at[0], gain_sem.at[1], (time, to)).start()

    def next_interval(n, step):
        to = lax.rem(time + step, times)
        return remote(own, near.at[n], near_sem.at[2 * n], near_sem.at[2 * n + 1], (to, group))

    below, above = next_interval(0, 1), next_interval(1, times - 1)
    below.start()
    above.start()

    sky_copy.wait()
    transpose_grid(stage, cells)
    first.pass_on()
    scale[...] = noise_ref[...] * keep_ref[...].astype(F32)
    station_tables(pairs_ref, gather, sums)
    grad_degrid[...] = jnp.zeros_like(grad_degrid)

    first.wait_receive()
    words_ref[...] = got_a[...].reshape(devices, LANES)
    turned_words = words_ref[...].T
    firsts = jnp.concatenate([turned_words[j * WORDS + 8 : j * WORDS + 9, :] for j in range(8)], axis=0)
    firsts_ref[...] = jnp.clip(firsts.astype(I32), 0, cells.shape[0] - 8)
    slot_copy = pltpu.make_async_copy(firsts_ref, slots, slot_sem)
    slot_copy.start()
    spread_taps(words_ref, weight)
    column = gains.at[:, core]
    pair = (time, group + 1 - 2 * core)
    wait_bytes(column, gain_sem.at[1])
    remote(column, column, pair_sem.at[0], pair_sem.at[1], pair).start()
    slot_copy.wait()

    def store_value(h, value):
        send_c[:, :, h, :] = value.reshape(times, groups, LANES)

    degrid_slots(slots, words_ref, cells, weight, product, store_value)
    second.start()
    wait_bytes(column, pair_sem.at[1])
    turn_gains(gains, turned, channels)
    gather_gains(turned, gather, left, right, 0, 2)
    second.pass_on()
    gather_gains(turned, gather, left, right, 2, 3)

    @pl.loop(0, channels // CHUNK)
    def _(chunk):
        pair_step(chunk, channels, left, right, pairs, facets, 2 * LANES)

    second.wait_receive()
    gather_degrid(lambda h: got_c[:, :, h, :].reshape(devices, LANES), place, part, degrid)

    @pl.loop(0, channels // CHUNK)
    def _(chunk):
        error_step(chunk, channels, vis_ref, scale, degrid, pairs, error, grad_degrid, 2 * LANES)

    def store_grad(h, value):
        send_e[:, :, h, :] = value.reshape(times, groups, LANES)

    place_grads(grad_degrid, place, store_grad)
    third.start()

    batch = 2

    def these(b):
        return pl.ds(b * batch, batch)

    def combine(b):
        wait_bytes(pair_g.at[these(b)], sum_sem.at[2 + b])
        for fc in range(b * batch, (b + 1) * batch):
            sum_g[:, fc] = send_g[core, fc] + pair_g[fc]
        to_end = got_g.at[level, these(b)]
        pltpu.make_async_copy(sum_g.at[level, these(b)], to_end, sum_sem.at[2 + facets + b]).start()

        @pl.loop(1, groups // 2)
        def _(n):
            to = lax.rem(level + n, groups // 2)
            remote(sum_g.at[to, these(b)], to_end, sum_sem.at[1], sum_sem.at[2 + facets + b], (time, 2 * to + core)).start()

    def finish(f):
        wait_bytes(got_g.at[:, these(f)], sum_sem.at[2 + facets + f])
        for c in range(2):
            fc = 2 * f + c
            total = got_g[0, fc]
            for n in range(1, groups // 2):
                total = total + got_g[n, fc]
            smooth = []
            for lt in range(2):
                here = own[:, 2 * fc + lt, :]
                down = jnp.where(time > 0, here - near[0, :, 2 * fc + lt, :], 0.0)
                up = jnp.where(time < times - 1, near[1, :, 2 * fc + lt, :] - here, 0.0)
                smooth.append(down - up)
            total = total + smoothness * jnp.concatenate(smooth, axis=1)
            data_ref[:, f, c, :] = total[:, :channels]

    below.wait()
    above.wait()
    for f in range(facets):
        grads = grads_even if f % 2 == 0 else grads_odd

        @pl.loop(0, channels // CHUNK, unroll=5)
        def _(chunk):
            gain_step(f, chunk, channels, degrid, left, right, error, grads, 2 * LANES)

        for c in range(2):
            value = dot_nt(sums[...], grads[c * channels : (c + 1) * channels, :])
            value = jnp.concatenate([value, jnp.zeros((64, 2 * LANES - channels), F32)], axis=1)
            value = value.reshape(groups // 2, 2, 8, 2 * LANES)
            for k in range(2):
                send_g[k, 2 * f + c] = value[:, k]
        remote(send_g.at[1 - core, these(f)], pair_g.at[these(f)], sum_sem.at[0], sum_sem.at[2 + f], pair).start()
        if f > 0:
            combine(f - 1)
        if f > 4:
            finish(f - 5)
        if f == 3:
            third.pass_on()
    combine(facets - 1)
    for f in range(facets - 5, facets - 1):
        finish(f)
    third.wait_receive()
    grad_ref[...] = got_e[...].reshape(devices, 2, LANES)
    finish(facets - 1)

    first.wait_send()
    second.wait_send()
    third.wait_send()
    wait_bytes(gains.at[pl.ds(0, groups // 2 - 1), 0], gain_sem.at[0])
    wait_bytes(column, pair_sem.at[0])
    wait_bytes(pair_g, sum_sem.at[0])
    wait_bytes(got_g.at[pl.ds(0, groups // 2 - 1)], sum_sem.at[1])


def scatter_kernel(first_ref, words_ref, grad_ref, sky_ref, weight_ref, spread, cells, stage, sem):
    sources = grad_ref.shape[0]
    blocks = stage.shape[1] // 8
    for b in range(blocks):
        cells[b * STRIDE : (b + 1) * STRIDE, :] = jnp.zeros((STRIDE, LANES), F32)
    spread_taps(words_ref, weight_ref)
    fold = fold_table()
    lane_quarter = (iota((sources, LANES), 1) >> 1) & 3
    for h in range(2):
        block = grad_ref[:, h, :]
        for g in range(4):
            j = 4 * h + g
            part = jnp.concatenate(halves(jnp.where(lane_quarter == g, block, 0.0)), axis=1)
            spread[j] = jnp.where(slot_quarter(words_ref, j) == lane_quarter.astype(F32), dot(part, fold), 0.0)

    @pl.loop(0, sources, unroll=2)
    def _(s):
        at = pl.ds(pl.multiple_of(s * 8, 8), 8)
        for j in range(8):
            cells[pl.ds(first_ref[j, s], 8), :] += weight_ref[j, at, :] * spread[j, pl.ds(s, 1), :]

    quarter = (iota((8, LANES), 1) >> 1) & 3
    last = jnp.zeros((8, LANES), F32)
    for b in range(blocks):
        pads = cells[b * STRIDE + LANES : (b + 1) * STRIDE, :]
        head = slice(b * STRIDE, b * STRIDE + 8)
        cells[head, :] = cells[head, :] + jnp.where(quarter > 0, pltpu.roll(pads, 2, 1), last)
        last = pltpu.roll(pads, LANES - 6, 1)

    pieces = 4
    length = blocks // pieces

    def copy(n):
        at = pl.ds(n * length * 8, length * 8)
        return pltpu.make_async_copy(stage.at[:, at, :], sky_ref.at[:, at, :], sem.at[n])

    for n in range(pieces):

        @pl.loop(n * length, (n + 1) * length, unroll=8)
        def _(b):
            turned = cells[pl.ds(pl.multiple_of(b * STRIDE, 8), LANES), :].T
            stage[:, pl.ds(pl.multiple_of(b * 8, 8), 8), :] = turned.reshape(16, 8, LANES)

        copy(n).start()
    for n in range(pieces):
        copy(n).wait()


def vmem(count):
    return [pl.BlockSpec(memory_space=pltpu.VMEM)] * count


def shape(dims, dtype=F32):
    return jax.ShapeDtypeStruct(dims, dtype)


def params():
    return pltpu.CompilerParams(vmem_limit_bytes=VMEM_LIMIT)


def body(
    visibilities, noise_weight, keep_flag, station_pairs, tile_owner, tile_offset, kernel_taps, gain_field, sky_grid
):
    rows = visibilities.shape[0]
    channels = visibilities.shape[2]
    devices = lax.axis_size("tm") * lax.axis_size("bl")
    parts, facets, terms, cells = sky_grid.shape
    lines = cells // LANES
    sky = sky_grid.reshape(parts, facets, terms, lines, LANES).transpose(0, 1, 3, 2, 4)
    sky = sky.reshape(parts * facets, lines * terms, LANES)

    times, groups = lax.axis_size("tm"), lax.axis_size("bl")
    singles, doubles = pltpu.VMEM((times, groups, 1, LANES), F32), pltpu.VMEM((times, groups, 2, LANES), F32)
    middle_singles = pltpu.VMEM((groups, times, 1, LANES), F32)
    middle_doubles = pltpu.VMEM((groups, times, 2, LANES), F32)
    tiles = facets * 4
    words, firsts, grad, data = pl.pallas_call(
        functools.partial(
            main_kernel, channels=channels, times=times, groups=groups
        ),
        out_shape=(
            shape((devices, LANES)), shape((8, devices), I32), shape((devices, 2, LANES)),
            shape(gain_field.shape[1:]),
        ),
        in_specs=vmem(8) + [pl.BlockSpec(memory_space=pl.ANY)],
        out_specs=tuple(vmem(4)),
        scratch_shapes=[
            singles, middle_singles, singles,
            doubles, middle_doubles, doubles,
            doubles, middle_doubles, doubles,
            pltpu.VMEM((8, tiles, LANES), F32),
            pltpu.VMEM((groups // 2, 2, 8, tiles, LANES), F32),
            pltpu.VMEM((2, 2 * facets, groups // 2, 8, 2 * LANES), F32),
            pltpu.VMEM((2 * facets, groups // 2, 8, 2 * LANES), F32),
            pltpu.VMEM((groups // 2, 2 * facets, 8, 2 * LANES), F32),
            pltpu.VMEM((groups // 2, 2 * facets, 8, 2 * LANES), F32),
            pltpu.VMEM((2, 8, tiles, LANES), F32),
            pltpu.VMEM((8, devices, rows), BF16),
            pltpu.VMEM(sky.shape, F32),
            pltpu.VMEM((cells // BLOCK * STRIDE, LANES), F32),
            pltpu.VMEM((8, devices * 8, LANES), F32),
            pltpu.VMEM((8, devices * 8, LANES), F32),
            pltpu.SMEM((8, devices), I32),
            pltpu.VMEM((rows // LANES, LANES, LANES), F32),
            pltpu.VMEM((2, 16, rows), F32),
            pltpu.VMEM((2 * facets * channels, LANES), BF16),
            pltpu.VMEM((2, LANES, rows), BF16),
            pltpu.VMEM((64, 4 * rows), BF16),
            pltpu.VMEM((1, rows), F32),
            pltpu.VMEM((2 * facets * channels, rows), F32),
            pltpu.VMEM((2 * facets * channels, rows), F32),
            pltpu.VMEM((2 * facets * channels, rows), F32),
            pltpu.VMEM((2, channels, rows), F32),
            pltpu.VMEM((2 * channels, 4 * rows), BF16),
            pltpu.VMEM((2 * channels, 4 * rows), BF16),
            pltpu.VMEM((2, 2 * facets, 8, rows), F32),
            pltpu.SemaphoreType.DMA,
            pltpu.SemaphoreType.DMA,
            pltpu.SemaphoreType.DMA((4,)),
            pltpu.SemaphoreType.DMA((4,)),
            pltpu.SemaphoreType.DMA((4,)),
            pltpu.SemaphoreType.DMA((2,)),
            pltpu.SemaphoreType.DMA((2,)),
            pltpu.SemaphoreType.DMA((4,)),
            pltpu.SemaphoreType.DMA((2 + 2 * facets,)),
        ],
        compiler_params=pltpu.CompilerParams(
            vmem_limit_bytes=62 << 20, collective_id=0, has_side_effects=True
        ),
        name="main",
    )(
        tile_owner.reshape(1, rows), tile_offset.reshape(1, rows), kernel_taps, gain_field[0],
        visibilities.transpose(1, 2, 0), noise_weight.reshape(1, rows), keep_flag.reshape(1, rows),
        station_pairs, sky,
    )

    out_grid = pl.pallas_call(
        scatter_kernel,
        out_shape=shape(sky.shape),
        in_specs=[pl.BlockSpec(memory_space=pltpu.SMEM)] + vmem(2),
        out_specs=pl.BlockSpec(memory_space=pl.ANY),
        scratch_shapes=[
            pltpu.VMEM((8, devices * 8, LANES), F32),
            pltpu.VMEM((8, devices, LANES), F32),
            pltpu.VMEM((cells // BLOCK * STRIDE, LANES), F32),
            pltpu.VMEM(sky.shape, F32),
            pltpu.SemaphoreType.DMA((4,)),
        ],
        compiler_params=params(),
        name="scatter",
    )(firsts, words, grad)
    grid_gradient = out_grid.reshape(parts, facets, lines, terms, LANES).transpose(0, 1, 3, 2, 4)
    grid_gradient = grid_gradient.reshape(sky_grid.shape)

    return (data[None], grid_gradient)


def solution(mesh):
    split = ("tm", "bl")
    return jax.shard_map(
        body,
        mesh=mesh,
        in_specs=(
            P(split, None, None),
            P(split),
            P(split),
            P(None, split),
            P(split, None),
            P(split),
            P(None, split),
            P("tm", "bl", None, None, None),
            P(None, None, None, split),
        ),
        out_specs=(P("tm", "bl", None, None, None), P(None, None, None, split)),
        check_vma=False,
    )
```

```python
import functools

import jax
import jax.numpy as jnp
from jax import lax
from jax.experimental import pallas as pl
from jax.experimental.pallas import tpu as pltpu
from jax.sharding import PartitionSpec as P

smoothness = 4.0
F32, BF16, I32 = jnp.float32, jnp.bfloat16, jnp.int32
LANES = 128
WORDS = 16
BLOCK = 512
STRIDE = LANES + 8
CHUNK = 16
VMEM_LIMIT = 56 << 20
NT = (((1,), (1,)), ((), ()))


def iota(shape, axis):
    return lax.broadcasted_iota(I32, shape, axis)


def halves(x):
    hi = x.astype(BF16)
    return hi, (x - hi.astype(F32)).astype(BF16)


def dot(x, y):
    return jnp.dot(x, y, preferred_element_type=F32)


def dot_nt(x, y):
    return lax.dot_general(x, y, NT, preferred_element_type=F32)


def ones_where(mask):
    return jnp.where(mask, 1.0, 0.0).astype(BF16)


def place_product(place_ref, both):
    slots, devices, rows = place_ref.shape
    product = dot_nt(place_ref[...].reshape(slots * devices, rows), both)
    return (product[:, :LANES] + product[:, LANES:]).reshape(slots, devices, LANES)


def form_slots(owner_ref, offset_ref, taps_ref, place_ref, store_message):
    devices, rows = place_ref.shape[1:]
    hits = iota((devices, rows), 0) == owner_ref[...]
    earlier = ones_where(iota((rows, rows), 0) < iota((rows, rows), 1))
    counts = dot(ones_where(hits), earlier)
    rank = jnp.sum(jnp.where(hits, counts, 0.0), axis=0, keepdims=True)
    offset = offset_ref[...]
    row = (offset >> 9) * STRIDE + (offset & (LANES - 1))
    tail = jnp.where(iota((WORDS - 8, rows), 0) == 0, row, (offset >> 7) & 3).astype(F32)
    words = jnp.concatenate([taps_ref[...], tail], axis=0)
    both = jnp.concatenate(halves(jnp.concatenate([words] * 8, axis=0)), axis=0)
    rank = jnp.where(hits, rank, -1.0)
    for j in range(8):
        place_ref[j] = ones_where(rank == float(j))
    tall = place_product(place_ref, both)
    group = iota((devices, LANES), 1) // WORDS
    message = jnp.zeros((devices, LANES), F32)
    for j in range(8):
        message = jnp.where(group == j, tall[j], message)
    store_message(message)


def transpose_grid(stage_ref, cells_ref):
    blocks = stage_ref.shape[1] // 8

    @pl.loop(0, blocks, unroll=8)
    def _(b):
        tile = stage_ref[:, pl.ds(pl.multiple_of(b * 8, 8), 8), :].reshape(LANES, LANES)
        cells_ref[pl.ds(pl.multiple_of(b * STRIDE, 8), LANES), :] = tile.T

    quarter = (iota((8, LANES), 1) >> 1) & 3
    for b in range(blocks):
        here = cells_ref[b * STRIDE : b * STRIDE + 8, :]
        next_block = min(b + 1, blocks - 1) * STRIDE
        after = cells_ref[next_block : next_block + 8, :]
        pad = jnp.where(quarter < 3, pltpu.roll(here, LANES - 2, 1), pltpu.roll(after, 6, 1))
        cells_ref[b * STRIDE + LANES : (b + 1) * STRIDE, :] = pad


def spread_taps(words_ref, weight_ref):
    sources = words_ref.shape[0]
    tall = jnp.broadcast_to(words_ref[...].reshape(sources, 1, LANES), (sources, 8, LANES)).reshape(8 * sources, LANES)
    tall = jnp.where((iota(tall.shape, 1) & (WORDS - 1)) == (iota(tall.shape, 0) & 7), tall, 0.0)
    both = jnp.concatenate(halves(tall), axis=1)
    for pair in range(4):
        a, b = iota((2 * LANES, 2 * LANES), 0) & (LANES - 1), iota((2 * LANES, 2 * LANES), 1)
        weight = dot(both, ones_where(a // WORDS == 2 * pair + b // LANES))
        for n in range(2):
            weight_ref[2 * pair + n] = weight[:, n * LANES : (n + 1) * LANES]


def slot_quarter(words_ref, j):
    return jnp.broadcast_to(words_ref[:, j * WORDS + 9 : j * WORDS + 10], (words_ref.shape[0], LANES))


def fold_table():
    a, b = iota((2 * LANES, LANES), 0) & (LANES - 1), iota((2 * LANES, LANES), 1)
    return ones_where(((a >> 3) == (b >> 3)) & ((a & 1) == (b & 1)))


def degrid_slots(first_ref, words_ref, cells_ref, weight_ref, product_ref, store_value):
    sources = words_ref.shape[0]

    @pl.loop(0, sources, unroll=2)
    def _(s):
        at = pl.ds(pl.multiple_of(s * 8, 8), 8)
        for j in range(8):
            product_ref[j, at, :] = weight_ref[j, at, :] * cells_ref[pl.ds(first_ref[j, s], 8), :]

    fold = fold_table()
    lane_quarter = (iota((sources, LANES), 1) >> 1) & 3
    for h in range(2):
        value = jnp.zeros((sources, LANES), F32)
        for g in range(4):
            j = 4 * h + g
            total = product_ref[j, pl.ds(0, sources, stride=8), :]
            for k in range(1, 8):
                total = total + product_ref[j, pl.ds(k, sources, stride=8), :]
            total = jnp.where(slot_quarter(words_ref, j) == lane_quarter.astype(F32), total, 0.0)
            value = jnp.where(lane_quarter == g, dot(jnp.concatenate(halves(total), axis=1), fold), value)
        store_value(h, value)


def gather_degrid(load_value, place_ref, part_ref, degrid_ref):
    sources = place_ref.shape[1]
    quarter = (iota((LANES, sources), 0) >> 1) & 3
    total = None
    for h in range(2):
        turned = load_value(h).T
        for pair in range(2):
            parts = [halves(jnp.where(quarter == g, turned, 0.0)) for g in (2 * pair, 2 * pair + 1)]
            j = 4 * h + 2 * pair
            place = place_ref[j : j + 2].reshape(2 * sources, place_ref.shape[2])
            for n in range(2):
                term = dot(jnp.concatenate([parts[0][n], parts[1][n]], axis=1), place)
                total = term if total is None else total + term
    for n in range(part_ref.shape[0]):
        tile = slice(n * LANES, (n + 1) * LANES)
        part_ref[n] = total[:, tile]
        for t in range(2):
            degrid_ref[t, :, tile] = sum(part_ref[n, pl.ds(2 * g + t, 16, stride=8), :] for g in range(4))


def station_tables(pairs_ref, gather_ref, sum_ref):
    rows = pairs_ref.shape[1]
    for side in range(2):
        hits = ones_where((iota((LANES, rows), 0) & 63) == pairs_ref[side : side + 1, :])
        gather_ref[side] = hits
        for n in range(2):
            sum_ref[:, (2 * side + n) * rows : (2 * side + n + 1) * rows] = hits[:64]


def turn_gains(gains_ref, turned_ref, channels):
    for fc in range(16):
        tiles = []
        for lt in range(2):
            block = gains_ref[:, :, :, 2 * fc + lt, :].reshape(64, LANES)
            hi = block.astype(BF16).astype(F32)
            tiles.append(jnp.concatenate([hi, block - hi], axis=0).T)
        turned_ref[fc * channels : (fc + 1) * channels] = jnp.concatenate(tiles, axis=0)[:channels].astype(BF16)


def gather_gains(turned_ref, gather_ref, left_ref, right_ref, first, last):
    size = turned_ref.shape[0] // 3

    @pl.loop(first, last)
    def _(n):
        at = pl.ds(pl.multiple_of(n * size, CHUNK), size)
        gains = turned_ref[at, :]
        left_ref[at, :] = dot(gains, gather_ref[0])
        right_ref[at, :] = dot(gains, gather_ref[1])


def chunk_rows(plane, channels, chunk):
    if isinstance(chunk, int):
        return pl.ds(plane * channels + chunk * CHUNK, CHUNK)
    return pl.ds(pl.multiple_of(plane * channels + chunk * CHUNK, CHUNK), CHUNK)


def channel_ramp(channels, chunk, width):
    channel = (iota((CHUNK, width), 0) + chunk * CHUNK).astype(F32)
    return 2.0 * channel / (channels - 1) - 1.0


def facet_model(degrid_ref, f, lanes, ramp):
    g = degrid_ref.shape[1] // 2 + f
    return tuple(degrid_ref[0, n : n + 1, lanes] + degrid_ref[1, n : n + 1, lanes] * ramp for n in (f, g))


def pair_step(chunk, channels, left_ref, right_ref, pair_ref, facets, width=LANES):
    for f in range(facets):
        re, im = chunk_rows(2 * f, channels, chunk), chunk_rows(2 * f + 1, channels, chunk)
        for first in range(0, left_ref.shape[1], width):
            lanes = slice(first, first + width)
            are, aim, bre, bim = left_ref[re, lanes], left_ref[im, lanes], right_ref[re, lanes], right_ref[im, lanes]
            pair_ref[re, lanes] = are * bre + aim * bim
            pair_ref[im, lanes] = aim * bre - are * bim


def error_step(
    chunk, channels, vis_ref, scale_ref, degrid_ref, pair_ref, error_ref, grad_degrid_ref, width=LANES
):
    rows = vis_ref.shape[2]
    facets = degrid_ref.shape[1] // 2
    at = chunk_rows(0, channels, chunk)
    ramp = channel_ramp(channels, chunk, width)
    for first in range(0, rows, width):
        lanes = slice(first, first + width)
        pred_re = pred_im = None
        for f in range(facets):
            re, im = chunk_rows(2 * f, channels, chunk), chunk_rows(2 * f + 1, channels, chunk)
            pre, pim = pair_ref[re, lanes], pair_ref[im, lanes]
            mre, mim = facet_model(degrid_ref, f, lanes, ramp)
            vre, vim = pre * mre - pim * mim, pre * mim + pim * mre
            pred_re = vre if pred_re is None else pred_re + vre
            pred_im = vim if pred_im is None else pred_im + vim
        ere = scale_ref[:, lanes] * (pred_re - vis_ref[0, at, lanes].astype(F32))
        eim = scale_ref[:, lanes] * (pred_im - vis_ref[1, at, lanes].astype(F32))
        error_ref[0, at, lanes] = ere
        error_ref[1, at, lanes] = eim
        for f in range(facets):
            re, im = chunk_rows(2 * f, channels, chunk), chunk_rows(2 * f + 1, channels, chunk)
            pre, pim = pair_ref[re, lanes], pair_ref[im, lanes]
            models = (ere * pre + eim * pim, eim * pre - ere * pim)
            for c in range(2):
                n = c * facets + f
                slope = models[c] * ramp
                grad_degrid_ref[0, n, :, lanes] += models[c][:8] + models[c][8:]
                grad_degrid_ref[1, n, :, lanes] += slope[:8] + slope[8:]


def gain_step(f, chunk, channels, degrid_ref, left_ref, right_ref, error_ref, grads_ref, width=LANES):
    rows = error_ref.shape[2]
    at = chunk_rows(0, channels, chunk)
    ramp = channel_ramp(channels, chunk, width)
    re, im = chunk_rows(2 * f, channels, chunk), chunk_rows(2 * f + 1, channels, chunk)
    for first in range(0, rows, width):
        lanes = slice(first, first + width)
        are, aim, bre, bim = left_ref[re, lanes], left_ref[im, lanes], right_ref[re, lanes], right_ref[im, lanes]
        mre, mim = facet_model(degrid_ref, f, lanes, ramp)
        ere, eim = error_ref[0, at, lanes], error_ref[1, at, lanes]
        qre, qim = ere * mre + eim * mim, eim * mre - ere * mim
        values = (
            (qre * bre - qim * bim, qre * bim + qim * bre),
            (qre * are + qim * aim, qre * aim - qim * are),
        )
        for side in range(2):
            for c in range(2):
                hi, lo = halves(values[side][c])
                start = 2 * side * rows + first
                grads_ref[chunk_rows(c, channels, chunk), start : start + width] = hi
                grads_ref[chunk_rows(c, channels, chunk), start + rows : start + rows + width] = lo


def place_grads(grad_degrid_ref, place_ref, store_value):
    planes = grad_degrid_ref.shape[1]
    rows = grad_degrid_ref.shape[3]
    devices = place_ref.shape[1]
    odd = (iota((8, rows), 0) & 1) == 1
    full = []
    for n in range(planes):
        level = jnp.sum(grad_degrid_ref[0, n], axis=0, keepdims=True)
        slope = jnp.sum(grad_degrid_ref[1, n], axis=0, keepdims=True)
        full.append(jnp.where(odd, slope, level))
    tall = place_product(place_ref, jnp.concatenate(halves(jnp.concatenate(full, axis=0)), axis=0))
    group = (iota((devices, LANES), 1) >> 1) & 3
    for h in range(2):
        value = tall[4 * h]
        for g in range(1, 4):
            value = jnp.where(group == g, tall[4 * h + g], value)
        store_value(h, value)


class Exchange:
    def __init__(self, send_ref, middle_ref, receive_ref, sems, time, group):
        self.send_ref, self.middle_ref, self.receive_ref, self.sems = send_ref, middle_ref, receive_ref, sems
        self.time, self.group = time, group
        self.times, self.groups = send_ref.shape[:2]

    def start(self):
        to_middle = self.middle_ref.at[:, self.time]
        pltpu.make_async_copy(self.send_ref.at[self.time], to_middle, self.sems.at[1]).start()

        @pl.loop(1, self.times)
        def _(n):
            to = lax.rem(self.time + n, self.times)
            remote(self.send_ref.at[to], to_middle, self.sems.at[0], self.sems.at[1], (to, self.group)).start()

    def pass_on(self):
        wait_bytes(self.middle_ref, self.sems.at[1])
        to_end = self.receive_ref.at[:, self.group]
        pltpu.make_async_copy(self.middle_ref.at[self.group], to_end, self.sems.at[3]).start()

        @pl.loop(1, self.groups)
        def _(n):
            to = lax.rem(self.group + n, self.groups)
            remote(self.middle_ref.at[to], to_end, self.sems.at[2], self.sems.at[3], (self.time, to)).start()

    def wait_receive(self):
        wait_bytes(self.receive_ref, self.sems.at[3])

    def wait_send(self):
        wait_bytes(self.send_ref.at[pl.ds(0, self.times - 1)], self.sems.at[0])
        wait_bytes(self.middle_ref.at[pl.ds(0, self.groups - 1)], self.sems.at[2])


def remote(source, target, send_sem, receive_sem, device):
    return pltpu.make_async_remote_copy(
        src_ref=source, dst_ref=target, send_sem=send_sem, recv_sem=receive_sem,
        device_id=device, device_id_type=pl.DeviceIdType.MESH,
    )


def wait_bytes(ref, sem):
    pltpu.make_async_copy(ref, ref, sem).wait()


def main_kernel(
    owner_ref, offset_ref, taps_ref, gain_ref, vis_ref, noise_ref, keep_ref, pairs_ref, sky_ref,
    words_ref, firsts_ref, grad_ref, data_ref,
    send_a, mid_a, got_a, send_c, mid_c, got_c, send_e, mid_e, got_e, own, gains, send_g, pair_g, sum_g, got_g, near,
    place, stage, cells, weight, product, slots, part, degrid, turned, gather, sums, scale,
    left, right, pairs, error, grads_even, grads_odd, grad_degrid,
    sky_sem, slot_sem, sem_a, sem_c, sem_e, gain_sem, pair_sem, near_sem, sum_sem,
    channels, times, groups,
):
    time, group = lax.axis_index("tm"), lax.axis_index("bl")
    devices = times * groups
    level, core = group // 2, lax.rem(group, 2)
    facets = gain_ref.shape[1]
    barrier = pltpu.get_barrier_semaphore()

    @pl.loop(1, times)
    def _(n):
        to = (lax.rem(time + n, times), group)
        pl.semaphore_signal(barrier, inc=1, device_id=to, device_id_type=pl.DeviceIdType.MESH)

    @pl.loop(1, groups)
    def _(n):
        to = (time, lax.rem(group + n, groups))
        pl.semaphore_signal(barrier, inc=1, device_id=to, device_id_type=pl.DeviceIdType.MESH)

    sky_copy = pltpu.make_async_copy(sky_ref, stage, sky_sem)
    sky_copy.start()

    def store_message(message):
        for t in range(devices):
            send_a[t // groups, t % groups] = message[t : t + 1, :]

    form_slots(owner_ref, offset_ref, taps_ref, place, store_message)
    pl.semaphore_wait(barrier, times + groups - 2)

    first = Exchange(send_a, mid_a, got_a, sem_a, time, group)
    second = Exchange(send_c, mid_c, got_c, sem_c, time, group)
    third = Exchange(send_e, mid_e, got_e, sem_e, time, group)
    first.start()

    for f in range(facets):
        for c in range(2):
            for lt in range(2):
                wide = min(LANES, channels - lt * LANES)
                block = gain_ref[:, f, c, lt * LANES : lt * LANES + wide]
                if wide < LANES:
                    block = jnp.concatenate([block, jnp.zeros((block.shape[0], LANES - wide), F32)], axis=1)
                own[:, 4 * f + 2 * c + lt, :] = block
    mine = gains.at[level, core]
    pltpu.make_async_copy(own, mine, gain_sem.at[1]).start()

    @pl.loop(1, groups // 2)
    def _(n):
        to = lax.rem(group + 2 * n, groups)
        remote(own, mine, gain_sem.at[0], gain_sem.at[1], (time, to)).start()

    def next_interval(n, step):
        to = lax.rem(time + step, times)
        return remote(own, near.at[n], near_sem.at[2 * n], near_sem.at[2 * n + 1], (to, group))

    below, above = next_interval(0, 1), next_interval(1, times - 1)
    below.start()
    above.start()

    sky_copy.wait()
    transpose_grid(stage, cells)
    first.pass_on()
    scale[...] = noise_ref[...] * keep_ref[...].astype(F32)
    station_tables(pairs_ref, gather, sums)
    grad_degrid[...] = jnp.zeros_like(grad_degrid)

    first.wait_receive()
    words_ref[...] = got_a[...].reshape(devices, LANES)
    turned_words = words_ref[...].T
    firsts = jnp.concatenate([turned_words[j * WORDS + 8 : j * WORDS + 9, :] for j in range(8)], axis=0)
    firsts_ref[...] = jnp.clip(firsts.astype(I32), 0, cells.shape[0] - 8)
    slot_copy = pltpu.make_async_copy(firsts_ref, slots, slot_sem)
    slot_copy.start()
    spread_taps(words_ref, weight)
    column = gains.at[:, core]
    pair = (time, group + 1 - 2 * core)
    wait_bytes(column, gain_sem.at[1])
    remote(column, column, pair_sem.at[0], pair_sem.at[1], pair).start()
    slot_copy.wait()

    def store_value(h, value):
        send_c[:, :, h, :] = value.reshape(times, groups, LANES)

    degrid_slots(slots, words_ref, cells, weight, product, store_value)
    second.start()
    wait_bytes(column, pair_sem.at[1])
    turn_gains(gains, turned, channels)
    gather_gains(turned, gather, left, right, 0, 2)
    second.pass_on()
    gather_gains(turned, gather, left, right, 2, 3)

    @pl.loop(0, channels // CHUNK)
    def _(chunk):
        pair_step(chunk, channels, left, right, pairs, facets, 2 * LANES)

    second.wait_receive()
    gather_degrid(lambda h: got_c[:, :, h, :].reshape(devices, LANES), place, part, degrid)

    @pl.loop(0, channels // CHUNK, unroll=3)
    def _(chunk):
        error_step(chunk, channels, vis_ref, scale, degrid, pairs, error, grad_degrid, 2 * LANES)

    def store_grad(h, value):
        send_e[:, :, h, :] = value.reshape(times, groups, LANES)

    place_grads(grad_degrid, place, store_grad)
    third.start()

    batch = 2

    def these(b):
        return pl.ds(b * batch, batch)

    def combine(b):
        wait_bytes(pair_g.at[these(b)], sum_sem.at[2 + b])
        for fc in range(b * batch, (b + 1) * batch):
            sum_g[:, fc] = send_g[core, fc] + pair_g[fc]
        to_end = got_g.at[level, these(b)]
        pltpu.make_async_copy(sum_g.at[level, these(b)], to_end, sum_sem.at[2 + facets + b]).start()

        for n in range(1, groups // 2):
            to = lax.rem(level + n, groups // 2)
            remote(
                sum_g.at[to, these(b)], to_end, sum_sem.at[1], sum_sem.at[2 + facets + b], (time, 2 * to + core)
            ).start()

    def finish(f):
        wait_bytes(got_g.at[:, these(f)], sum_sem.at[2 + facets + f])
        for c in range(2):
            fc = 2 * f + c
            total = got_g[0, fc]
            for n in range(1, groups // 2):
                total = total + got_g[n, fc]
            smooth = []
            for lt in range(2):
                here = own[:, 2 * fc + lt, :]
                down = jnp.where(time > 0, here - near[0, :, 2 * fc + lt, :], 0.0)
                up = jnp.where(time < times - 1, near[1, :, 2 * fc + lt, :] - here, 0.0)
                smooth.append(down - up)
            total = total + smoothness * jnp.concatenate(smooth, axis=1)
            data_ref[:, f, c, :] = total[:, :channels]

    below.wait()
    above.wait()
    def grads_of(f):
        return grads_even if f % 2 == 0 else grads_odd

    def sum_stations(f):
        for c in range(2):
            value = dot_nt(sums[...], grads_of(f)[c * channels : (c + 1) * channels, :])
            value = jnp.concatenate([value, jnp.zeros((64, 2 * LANES - channels), F32)], axis=1)
            value = value.reshape(groups // 2, 2, 8, 2 * LANES)
            for k in range(2):
                send_g[k, 2 * f + c] = value[:, k]

    for f in range(facets + 1):
        if f > 0:
            sum_stations(f - 1)
        if f < facets:
            for chunk in range(channels // CHUNK):
                gain_step(f, chunk, channels, degrid, left, right, error, grads_of(f), 2 * LANES)
        if f > 0:
            b = f - 1
            remote(send_g.at[1 - core, these(b)], pair_g.at[these(b)], sum_sem.at[0], sum_sem.at[2 + b], pair).start()
        if f > 1:
            combine(f - 2)
        if f > 6:
            finish(f - 7)
        if f == 6:
            third.pass_on()
    combine(facets - 1)
    for f in range(facets - 6, facets - 1):
        finish(f)
    third.wait_receive()
    grad_ref[...] = got_e[...].reshape(devices, 2, LANES)
    finish(facets - 1)

    first.wait_send()
    second.wait_send()
    third.wait_send()
    wait_bytes(gains.at[pl.ds(0, groups // 2 - 1), 0], gain_sem.at[0])
    wait_bytes(column, pair_sem.at[0])
    wait_bytes(pair_g, sum_sem.at[0])
    wait_bytes(got_g.at[pl.ds(0, groups // 2 - 1)], sum_sem.at[1])


def scatter_kernel(first_ref, words_ref, grad_ref, sky_ref, weight_ref, spread, cells, stage, sem):
    sources = grad_ref.shape[0]
    blocks = stage.shape[1] // 8
    for b in range(blocks):
        cells[b * STRIDE : (b + 1) * STRIDE, :] = jnp.zeros((STRIDE, LANES), F32)
    spread_taps(words_ref, weight_ref)
    fold = fold_table()
    lane_quarter = (iota((sources, LANES), 1) >> 1) & 3
    for h in range(2):
        block = grad_ref[:, h, :]
        for g in range(4):
            j = 4 * h + g
            part = jnp.concatenate(halves(jnp.where(lane_quarter == g, block, 0.0)), axis=1)
            spread[j] = jnp.where(slot_quarter(words_ref, j) == lane_quarter.astype(F32), dot(part, fold), 0.0)

    @pl.loop(0, sources, unroll=2)
    def _(s):
        at = pl.ds(pl.multiple_of(s * 8, 8), 8)
        for j in range(8):
            cells[pl.ds(first_ref[j, s], 8), :] += weight_ref[j, at, :] * spread[j, pl.ds(s, 1), :]

    quarter = (iota((8, LANES), 1) >> 1) & 3
    last = jnp.zeros((8, LANES), F32)
    for b in range(blocks):
        pads = cells[b * STRIDE + LANES : (b + 1) * STRIDE, :]
        head = slice(b * STRIDE, b * STRIDE + 8)
        cells[head, :] = cells[head, :] + jnp.where(quarter > 0, pltpu.roll(pads, 2, 1), last)
        last = pltpu.roll(pads, LANES - 6, 1)

    pieces = 4
    length = blocks // pieces

    def copy(n):
        at = pl.ds(n * length * 8, length * 8)
        return pltpu.make_async_copy(stage.at[:, at, :], sky_ref.at[:, at, :], sem.at[n])

    for n in range(pieces):

        @pl.loop(n * length, (n + 1) * length, unroll=8)
        def _(b):
            turned = cells[pl.ds(pl.multiple_of(b * STRIDE, 8), LANES), :].T
            stage[:, pl.ds(pl.multiple_of(b * 8, 8), 8), :] = turned.reshape(16, 8, LANES)

        copy(n).start()
    for n in range(pieces):
        copy(n).wait()


def vmem(count):
    return [pl.BlockSpec(memory_space=pltpu.VMEM)] * count


def shape(dims, dtype=F32):
    return jax.ShapeDtypeStruct(dims, dtype)


def params():
    return pltpu.CompilerParams(vmem_limit_bytes=VMEM_LIMIT)


def body(
    visibilities, noise_weight, keep_flag, station_pairs, tile_owner, tile_offset, kernel_taps, gain_field, sky_grid
):
    rows = visibilities.shape[0]
    channels = visibilities.shape[2]
    devices = lax.axis_size("tm") * lax.axis_size("bl")
    parts, facets, terms, cells = sky_grid.shape
    lines = cells // LANES
    sky = sky_grid.reshape(parts, facets, terms, lines, LANES).transpose(0, 1, 3, 2, 4)
    sky = sky.reshape(parts * facets, lines * terms, LANES)

    times, groups = lax.axis_size("tm"), lax.axis_size("bl")
    singles, doubles = pltpu.VMEM((times, groups, 1, LANES), F32), pltpu.VMEM((times, groups, 2, LANES), F32)
    middle_singles = pltpu.VMEM((groups, times, 1, LANES), F32)
    middle_doubles = pltpu.VMEM((groups, times, 2, LANES), F32)
    tiles = facets * 4
    words, firsts, grad, data = pl.pallas_call(
        functools.partial(
            main_kernel, channels=channels, times=times, groups=groups
        ),
        out_shape=(
            shape((devices, LANES)), shape((8, devices), I32), shape((devices, 2, LANES)),
            shape(gain_field.shape[1:]),
        ),
        in_specs=vmem(8) + [pl.BlockSpec(memory_space=pl.ANY)],
        out_specs=tuple(vmem(4)),
        scratch_shapes=[
            singles, middle_singles, singles,
            doubles, middle_doubles, doubles,
            doubles, middle_doubles, doubles,
            pltpu.VMEM((8, tiles, LANES), F32),
            pltpu.VMEM((groups // 2, 2, 8, tiles, LANES), F32),
            pltpu.VMEM((2, 2 * facets, groups // 2, 8, 2 * LANES), F32),
            pltpu.VMEM((2 * facets, groups // 2, 8, 2 * LANES), F32),
            pltpu.VMEM((groups // 2, 2 * facets, 8, 2 * LANES), F32),
            pltpu.VMEM((groups // 2, 2 * facets, 8, 2 * LANES), F32),
            pltpu.VMEM((2, 8, tiles, LANES), F32),
            pltpu.VMEM((8, devices, rows), BF16),
            pltpu.VMEM(sky.shape, F32),
            pltpu.VMEM((cells // BLOCK * STRIDE, LANES), F32),
            pltpu.VMEM((8, devices * 8, LANES), F32),
            pltpu.VMEM((8, devices * 8, LANES), F32),
            pltpu.SMEM((8, devices), I32),
            pltpu.VMEM((rows // LANES, LANES, LANES), F32),
            pltpu.VMEM((2, 16, rows), F32),
            pltpu.VMEM((2 * facets * channels, LANES), BF16),
            pltpu.VMEM((2, LANES, rows), BF16),
            pltpu.VMEM((64, 4 * rows), BF16),
            pltpu.VMEM((1, rows), F32),
            pltpu.VMEM((2 * facets * channels, rows), F32),
            pltpu.VMEM((2 * facets * channels, rows), F32),
            pltpu.VMEM((2 * facets * channels, rows), F32),
            pltpu.VMEM((2, channels, rows), F32),
            pltpu.VMEM((2 * channels, 4 * rows), BF16),
            pltpu.VMEM((2 * channels, 4 * rows), BF16),
            pltpu.VMEM((2, 2 * facets, 8, rows), F32),
            pltpu.SemaphoreType.DMA,
            pltpu.SemaphoreType.DMA,
            pltpu.SemaphoreType.DMA((4,)),
            pltpu.SemaphoreType.DMA((4,)),
            pltpu.SemaphoreType.DMA((4,)),
            pltpu.SemaphoreType.DMA((2,)),
            pltpu.SemaphoreType.DMA((2,)),
            pltpu.SemaphoreType.DMA((4,)),
            pltpu.SemaphoreType.DMA((2 + 2 * facets,)),
        ],
        compiler_params=pltpu.CompilerParams(
            vmem_limit_bytes=62 << 20, collective_id=0, has_side_effects=True
        ),
        name="main",
    )(
        tile_owner.reshape(1, rows), tile_offset.reshape(1, rows), kernel_taps, gain_field[0],
        visibilities.transpose(1, 2, 0), noise_weight.reshape(1, rows), keep_flag.reshape(1, rows),
        station_pairs, sky,
    )

    out_grid = pl.pallas_call(
        scatter_kernel,
        out_shape=shape(sky.shape),
        in_specs=[pl.BlockSpec(memory_space=pltpu.SMEM)] + vmem(2),
        out_specs=pl.BlockSpec(memory_space=pl.ANY),
        scratch_shapes=[
            pltpu.VMEM((8, devices * 8, LANES), F32),
            pltpu.VMEM((8, devices, LANES), F32),
            pltpu.VMEM((cells // BLOCK * STRIDE, LANES), F32),
            pltpu.VMEM(sky.shape, F32),
            pltpu.SemaphoreType.DMA((4,)),
        ],
        compiler_params=params(),
        name="scatter",
    )(firsts, words, grad)
    grid_gradient = out_grid.reshape(parts, facets, lines, terms, LANES).transpose(0, 1, 3, 2, 4)
    grid_gradient = grid_gradient.reshape(sky_grid.shape)

    return (data[None], grid_gradient)


def solution(mesh):
    split = ("tm", "bl")
    return jax.shard_map(
        body,
        mesh=mesh,
        in_specs=(
            P(split, None, None),
            P(split),
            P(split),
            P(None, split),
            P(split, None),
            P(split),
            P(None, split),
            P("tm", "bl", None, None, None),
            P(None, None, None, split),
        ),
        out_specs=(P("tm", "bl", None, None, None), P(None, None, None, split)),
        check_vma=False,
    )
```

```python
import functools

import jax
import jax.numpy as jnp
from jax import lax
from jax.experimental import pallas as pl
from jax.experimental.pallas import tpu as pltpu
from jax.sharding import PartitionSpec as P

smoothness = 4.0
F32, BF16, I32 = jnp.float32, jnp.bfloat16, jnp.int32
LANES = 128
WORDS = 16
BLOCK = 512
STRIDE = LANES + 8
CHUNK = 16
VMEM_LIMIT = 56 << 20
NT = (((1,), (1,)), ((), ()))


def iota(shape, axis):
    return lax.broadcasted_iota(I32, shape, axis)


def halves(x):
    hi = x.astype(BF16)
    return hi, (x - hi.astype(F32)).astype(BF16)


def dot(x, y):
    return jnp.dot(x, y, preferred_element_type=F32)


def dot_nt(x, y):
    return lax.dot_general(x, y, NT, preferred_element_type=F32)


def ones_where(mask):
    return jnp.where(mask, 1.0, 0.0).astype(BF16)


def place_product(place_ref, both):
    slots, devices, rows = place_ref.shape
    product = dot_nt(place_ref[...].reshape(slots * devices, rows), both)
    return (product[:, :LANES] + product[:, LANES:]).reshape(slots, devices, LANES)


def form_slots(owner_ref, offset_ref, taps_ref, place_ref, store_message):
    devices, rows = place_ref.shape[1:]
    hits = iota((devices, rows), 0) == owner_ref[...]
    earlier = ones_where(iota((rows, rows), 0) < iota((rows, rows), 1))
    counts = dot(ones_where(hits), earlier)
    rank = jnp.sum(jnp.where(hits, counts, 0.0), axis=0, keepdims=True)
    offset = offset_ref[...]
    row = (offset >> 9) * STRIDE + (offset & (LANES - 1))
    tail = jnp.where(iota((WORDS - 8, rows), 0) == 0, row, (offset >> 7) & 3).astype(F32)
    words = jnp.concatenate([taps_ref[...], tail], axis=0)
    both = jnp.concatenate(halves(jnp.concatenate([words] * 8, axis=0)), axis=0)
    rank = jnp.where(hits, rank, -1.0)
    for j in range(8):
        place_ref[j] = ones_where(rank == float(j))
    tall = place_product(place_ref, both)
    group = iota((devices, LANES), 1) // WORDS
    message = jnp.zeros((devices, LANES), F32)
    for j in range(8):
        message = jnp.where(group == j, tall[j], message)
    store_message(message)


def transpose_grid(stage_ref, cells_ref):
    blocks = stage_ref.shape[1] // 8

    @pl.loop(0, blocks, unroll=8)
    def _(b):
        tile = stage_ref[:, pl.ds(pl.multiple_of(b * 8, 8), 8), :].reshape(LANES, LANES)
        cells_ref[pl.ds(pl.multiple_of(b * STRIDE, 8), LANES), :] = tile.T

    quarter = (iota((8, LANES), 1) >> 1) & 3
    for b in range(blocks):
        here = cells_ref[b * STRIDE : b * STRIDE + 8, :]
        next_block = min(b + 1, blocks - 1) * STRIDE
        after = cells_ref[next_block : next_block + 8, :]
        pad = jnp.where(quarter < 3, pltpu.roll(here, LANES - 2, 1), pltpu.roll(after, 6, 1))
        cells_ref[b * STRIDE + LANES : (b + 1) * STRIDE, :] = pad


def spread_taps(words_ref, weight_ref):
    sources = words_ref.shape[0]
    tall = jnp.broadcast_to(words_ref[...].reshape(sources, 1, LANES), (sources, 8, LANES)).reshape(8 * sources, LANES)
    tall = jnp.where((iota(tall.shape, 1) & (WORDS - 1)) == (iota(tall.shape, 0) & 7), tall, 0.0)
    both = jnp.concatenate(halves(tall), axis=1)
    for pair in range(4):
        a, b = iota((2 * LANES, 2 * LANES), 0) & (LANES - 1), iota((2 * LANES, 2 * LANES), 1)
        weight = dot(both, ones_where(a // WORDS == 2 * pair + b // LANES))
        for n in range(2):
            weight_ref[2 * pair + n] = weight[:, n * LANES : (n + 1) * LANES]


def slot_quarter(words_ref, j):
    return jnp.broadcast_to(words_ref[:, j * WORDS + 9 : j * WORDS + 10], (words_ref.shape[0], LANES))


def fold_table():
    a, b = iota((2 * LANES, LANES), 0) & (LANES - 1), iota((2 * LANES, LANES), 1)
    return ones_where(((a >> 3) == (b >> 3)) & ((a & 1) == (b & 1)))


def degrid_slots(first_ref, words_ref, cells_ref, weight_ref, product_ref, store_value):
    sources = words_ref.shape[0]

    @pl.loop(0, sources, unroll=8)
    def _(s):
        at = pl.ds(pl.multiple_of(s * 8, 8), 8)
        for j in range(8):
            product_ref[j, at, :] = weight_ref[j, at, :] * cells_ref[pl.ds(first_ref[j, s], 8), :]

    fold = fold_table()
    lane_quarter = (iota((sources, LANES), 1) >> 1) & 3
    for h in range(2):
        value = jnp.zeros((sources, LANES), F32)
        for g in range(4):
            j = 4 * h + g
            total = product_ref[j, pl.ds(0, sources, stride=8), :]
            for k in range(1, 8):
                total = total + product_ref[j, pl.ds(k, sources, stride=8), :]
            total = jnp.where(slot_quarter(words_ref, j) == lane_quarter.astype(F32), total, 0.0)
            value = jnp.where(lane_quarter == g, dot(jnp.concatenate(halves(total), axis=1), fold), value)
        store_value(h, value)


def gather_degrid(load_value, place_ref, part_ref, degrid_ref):
    sources = place_ref.shape[1]
    quarter = (iota((LANES, sources), 0) >> 1) & 3
    total = None
    for h in range(2):
        turned = load_value(h).T
        for pair in range(2):
            parts = [halves(jnp.where(quarter == g, turned, 0.0)) for g in (2 * pair, 2 * pair + 1)]
            j = 4 * h + 2 * pair
            place = place_ref[j : j + 2].reshape(2 * sources, place_ref.shape[2])
            for n in range(2):
                term = dot(jnp.concatenate([parts[0][n], parts[1][n]], axis=1), place)
                total = term if total is None else total + term
    for n in range(part_ref.shape[0]):
        tile = slice(n * LANES, (n + 1) * LANES)
        part_ref[n] = total[:, tile]
        for t in range(2):
            degrid_ref[t, :, tile] = sum(part_ref[n, pl.ds(2 * g + t, 16, stride=8), :] for g in range(4))


def station_tables(pairs_ref, gather_ref, sum_ref):
    rows = pairs_ref.shape[1]
    for side in range(2):
        hits = ones_where((iota((LANES, rows), 0) & 63) == pairs_ref[side : side + 1, :])
        gather_ref[side] = hits
        for n in range(2):
            sum_ref[:, (2 * side + n) * rows : (2 * side + n + 1) * rows] = hits[:64]


def turn_gains(gains_ref, turned_ref, channels):
    for fc in range(16):
        tiles = []
        for lt in range(2):
            block = gains_ref[:, :, :, 2 * fc + lt, :].reshape(64, LANES)
            hi = block.astype(BF16).astype(F32)
            tiles.append(jnp.concatenate([hi, block - hi], axis=0).T)
        turned_ref[fc * channels : (fc + 1) * channels] = jnp.concatenate(tiles, axis=0)[:channels].astype(BF16)


def gather_gains(turned_ref, gather_ref, left_ref, right_ref, first, last):
    size = turned_ref.shape[0] // 3

    @pl.loop(first, last)
    def _(n):
        at = pl.ds(pl.multiple_of(n * size, CHUNK), size)
        gains = turned_ref[at, :]
        left_ref[at, :] = dot(gains, gather_ref[0])
        right_ref[at, :] = dot(gains, gather_ref[1])


def chunk_rows(plane, channels, chunk):
    if isinstance(chunk, int):
        return pl.ds(plane * channels + chunk * CHUNK, CHUNK)
    return pl.ds(pl.multiple_of(plane * channels + chunk * CHUNK, CHUNK), CHUNK)


def channel_ramp(channels, chunk, width):
    channel = (iota((CHUNK, width), 0) + chunk * CHUNK).astype(F32)
    return 2.0 * channel / (channels - 1) - 1.0


def facet_model(degrid_ref, f, lanes, ramp):
    g = degrid_ref.shape[1] // 2 + f
    return tuple(degrid_ref[0, n : n + 1, lanes] + degrid_ref[1, n : n + 1, lanes] * ramp for n in (f, g))


def pair_step(chunk, channels, left_ref, right_ref, pair_ref, facets, width=LANES):
    for f in range(facets):
        re, im = chunk_rows(2 * f, channels, chunk), chunk_rows(2 * f + 1, channels, chunk)
        for first in range(0, left_ref.shape[1], width):
            lanes = slice(first, first + width)
            are, aim, bre, bim = left_ref[re, lanes], left_ref[im, lanes], right_ref[re, lanes], right_ref[im, lanes]
            pair_ref[re, lanes] = are * bre + aim * bim
            pair_ref[im, lanes] = aim * bre - are * bim


def error_step(
    chunk, channels, vis_ref, scale_ref, degrid_ref, pair_ref, error_ref, grad_degrid_ref, width=LANES
):
    rows = vis_ref.shape[2]
    facets = degrid_ref.shape[1] // 2
    at = chunk_rows(0, channels, chunk)
    ramp = channel_ramp(channels, chunk, width)
    for first in range(0, rows, width):
        lanes = slice(first, first + width)
        pred_re = pred_im = None
        for f in range(facets):
            re, im = chunk_rows(2 * f, channels, chunk), chunk_rows(2 * f + 1, channels, chunk)
            pre, pim = pair_ref[re, lanes], pair_ref[im, lanes]
            mre, mim = facet_model(degrid_ref, f, lanes, ramp)
            vre, vim = pre * mre - pim * mim, pre * mim + pim * mre
            pred_re = vre if pred_re is None else pred_re + vre
            pred_im = vim if pred_im is None else pred_im + vim
        ere = scale_ref[:, lanes] * (pred_re - vis_ref[0, at, lanes].astype(F32))
        eim = scale_ref[:, lanes] * (pred_im - vis_ref[1, at, lanes].astype(F32))
        error_ref[0, at, lanes] = ere
        error_ref[1, at, lanes] = eim
        for f in range(facets):
            re, im = chunk_rows(2 * f, channels, chunk), chunk_rows(2 * f + 1, channels, chunk)
            pre, pim = pair_ref[re, lanes], pair_ref[im, lanes]
            models = (ere * pre + eim * pim, eim * pre - ere * pim)
            for c in range(2):
                n = c * facets + f
                slope = models[c] * ramp
                grad_degrid_ref[0, n, :, lanes] += models[c][:8] + models[c][8:]
                grad_degrid_ref[1, n, :, lanes] += slope[:8] + slope[8:]


def gain_step(f, chunk, channels, degrid_ref, left_ref, right_ref, error_ref, grads_ref, width=LANES):
    rows = error_ref.shape[2]
    at = chunk_rows(0, channels, chunk)
    ramp = channel_ramp(channels, chunk, width)
    re, im = chunk_rows(2 * f, channels, chunk), chunk_rows(2 * f + 1, channels, chunk)
    for first in range(0, rows, width):
        lanes = slice(first, first + width)
        are, aim, bre, bim = left_ref[re, lanes], left_ref[im, lanes], right_ref[re, lanes], right_ref[im, lanes]
        mre, mim = facet_model(degrid_ref, f, lanes, ramp)
        ere, eim = error_ref[0, at, lanes], error_ref[1, at, lanes]
        qre, qim = ere * mre + eim * mim, eim * mre - ere * mim
        values = (
            (qre * bre - qim * bim, qre * bim + qim * bre),
            (qre * are + qim * aim, qre * aim - qim * are),
        )
        for side in range(2):
            for c in range(2):
                hi, lo = halves(values[side][c])
                start = 2 * side * rows + first
                grads_ref[chunk_rows(c, channels, chunk), start : start + width] = hi
                grads_ref[chunk_rows(c, channels, chunk), start + rows : start + rows + width] = lo


def place_grads(grad_degrid_ref, place_ref, store_value):
    planes = grad_degrid_ref.shape[1]
    rows = grad_degrid_ref.shape[3]
    devices = place_ref.shape[1]
    odd = (iota((8, rows), 0) & 1) == 1
    full = []
    for n in range(planes):
        level = jnp.sum(grad_degrid_ref[0, n], axis=0, keepdims=True)
        slope = jnp.sum(grad_degrid_ref[1, n], axis=0, keepdims=True)
        full.append(jnp.where(odd, slope, level))
    tall = place_product(place_ref, jnp.concatenate(halves(jnp.concatenate(full, axis=0)), axis=0))
    group = (iota((devices, LANES), 1) >> 1) & 3
    for h in range(2):
        value = tall[4 * h]
        for g in range(1, 4):
            value = jnp.where(group == g, tall[4 * h + g], value)
        store_value(h, value)


class Exchange:
    def __init__(self, send_ref, middle_ref, receive_ref, sems, time, group):
        self.send_ref, self.middle_ref, self.receive_ref, self.sems = send_ref, middle_ref, receive_ref, sems
        self.time, self.group = time, group
        self.times, self.groups = send_ref.shape[:2]

    def start(self):
        to_middle = self.middle_ref.at[:, self.time]
        pltpu.make_async_copy(self.send_ref.at[self.time], to_middle, self.sems.at[1]).start()

        @pl.loop(1, self.times)
        def _(n):
            to = lax.rem(self.time + n, self.times)
            remote(self.send_ref.at[to], to_middle, self.sems.at[0], self.sems.at[1], (to, self.group)).start()

    def pass_on(self):
        wait_bytes(self.middle_ref, self.sems.at[1])
        to_end = self.receive_ref.at[:, self.group]
        pltpu.make_async_copy(self.middle_ref.at[self.group], to_end, self.sems.at[3]).start()

        @pl.loop(1, self.groups)
        def _(n):
            to = lax.rem(self.group + n, self.groups)
            remote(self.middle_ref.at[to], to_end, self.sems.at[2], self.sems.at[3], (self.time, to)).start()

    def wait_receive(self):
        wait_bytes(self.receive_ref, self.sems.at[3])

    def wait_send(self):
        wait_bytes(self.send_ref.at[pl.ds(0, self.times - 1)], self.sems.at[0])
        wait_bytes(self.middle_ref.at[pl.ds(0, self.groups - 1)], self.sems.at[2])


def remote(source, target, send_sem, receive_sem, device):
    return pltpu.make_async_remote_copy(
        src_ref=source, dst_ref=target, send_sem=send_sem, recv_sem=receive_sem,
        device_id=device, device_id_type=pl.DeviceIdType.MESH,
    )


def wait_bytes(ref, sem):
    pltpu.make_async_copy(ref, ref, sem).wait()


def main_kernel(
    owner_ref, offset_ref, taps_ref, gain_ref, vis_ref, noise_ref, keep_ref, pairs_ref, sky_ref,
    words_ref, firsts_ref, grad_ref, data_ref,
    send_a, mid_a, got_a, send_c, mid_c, got_c, send_e, mid_e, got_e, own, gains, send_g, pair_g, sum_g, got_g, near,
    place, stage, cells, weight, product, slots, part, degrid, turned, gather, sums, scale,
    left, right, pairs, error, grads_even, grads_odd, grad_degrid,
    sky_sem, slot_sem, sem_a, sem_c, sem_e, gain_sem, pair_sem, near_sem, sum_sem,
    channels, times, groups,
):
    time, group = lax.axis_index("tm"), lax.axis_index("bl")
    devices = times * groups
    level, core = group // 2, lax.rem(group, 2)
    facets = gain_ref.shape[1]
    barrier = pltpu.get_barrier_semaphore()

    @pl.loop(1, times)
    def _(n):
        to = (lax.rem(time + n, times), group)
        pl.semaphore_signal(barrier, inc=1, device_id=to, device_id_type=pl.DeviceIdType.MESH)

    @pl.loop(1, groups)
    def _(n):
        to = (time, lax.rem(group + n, groups))
        pl.semaphore_signal(barrier, inc=1, device_id=to, device_id_type=pl.DeviceIdType.MESH)

    sky_copy = pltpu.make_async_copy(sky_ref, stage, sky_sem)
    sky_copy.start()

    def store_message(message):
        for t in range(devices):
            send_a[t // groups, t % groups] = message[t : t + 1, :]

    form_slots(owner_ref, offset_ref, taps_ref, place, store_message)
    pl.semaphore_wait(barrier, times + groups - 2)

    first = Exchange(send_a, mid_a, got_a, sem_a, time, group)
    second = Exchange(send_c, mid_c, got_c, sem_c, time, group)
    third = Exchange(send_e, mid_e, got_e, sem_e, time, group)
    first.start()

    for f in range(facets):
        for c in range(2):
            for lt in range(2):
                wide = min(LANES, channels - lt * LANES)
                block = gain_ref[:, f, c, lt * LANES : lt * LANES + wide]
                if wide < LANES:
                    block = jnp.concatenate([block, jnp.zeros((block.shape[0], LANES - wide), F32)], axis=1)
                own[:, 4 * f + 2 * c + lt, :] = block
    mine = gains.at[level, core]
    pltpu.make_async_copy(own, mine, gain_sem.at[1]).start()

    @pl.loop(1, groups // 2)
    def _(n):
        to = lax.rem(group + 2 * n, groups)
        remote(own, mine, gain_sem.at[0], gain_sem.at[1], (time, to)).start()

    def next_interval(n, step):
        to = lax.rem(time + step, times)
        return remote(own, near.at[n], near_sem.at[2 * n], near_sem.at[2 * n + 1], (to, group))

    below, above = next_interval(0, 1), next_interval(1, times - 1)
    below.start()
    above.start()

    sky_copy.wait()
    transpose_grid(stage, cells)
    first.pass_on()
    scale[...] = noise_ref[...] * keep_ref[...].astype(F32)
    station_tables(pairs_ref, gather, sums)
    grad_degrid[...] = jnp.zeros_like(grad_degrid)

    first.wait_receive()
    words_ref[...] = got_a[...].reshape(devices, LANES)
    turned_words = words_ref[...].T
    firsts = jnp.concatenate([turned_words[j * WORDS + 8 : j * WORDS + 9, :] for j in range(8)], axis=0)
    firsts_ref[...] = jnp.clip(firsts.astype(I32), 0, cells.shape[0] - 8)
    slot_copy = pltpu.make_async_copy(firsts_ref, slots, slot_sem)
    slot_copy.start()
    spread_taps(words_ref, weight)
    column = gains.at[:, core]
    pair = (time, group + 1 - 2 * core)
    wait_bytes(column, gain_sem.at[1])
    remote(column, column, pair_sem.at[0], pair_sem.at[1], pair).start()
    slot_copy.wait()

    def store_value(h, value):
        send_c[:, :, h, :] = value.reshape(times, groups, LANES)

    degrid_slots(slots, words_ref, cells, weight, product, store_value)
    second.start()
    wait_bytes(column, pair_sem.at[1])
    turn_gains(gains, turned, channels)
    gather_gains(turned, gather, left, right, 0, 2)
    second.pass_on()
    gather_gains(turned, gather, left, right, 2, 3)

    @pl.loop(0, channels // CHUNK)
    def _(chunk):
        pair_step(chunk, channels, left, right, pairs, facets, 2 * LANES)

    second.wait_receive()
    gather_degrid(lambda h: got_c[:, :, h, :].reshape(devices, LANES), place, part, degrid)

    @pl.loop(0, channels // CHUNK, unroll=3)
    def _(chunk):
        error_step(chunk, channels, vis_ref, scale, degrid, pairs, error, grad_degrid, 2 * LANES)

    def store_grad(h, value):
        send_e[:, :, h, :] = value.reshape(times, groups, LANES)

    place_grads(grad_degrid, place, store_grad)
    third.start()

    batch = 2

    def these(b):
        return pl.ds(b * batch, batch)

    def combine(b):
        wait_bytes(pair_g.at[these(b)], sum_sem.at[2 + b])
        for fc in range(b * batch, (b + 1) * batch):
            sum_g[:, fc] = send_g[core, fc] + pair_g[fc]
        to_end = got_g.at[level, these(b)]
        pltpu.make_async_copy(sum_g.at[level, these(b)], to_end, sum_sem.at[2 + facets + b]).start()

        for n in range(1, groups // 2):
            to = lax.rem(level + n, groups // 2)
            remote(
                sum_g.at[to, these(b)], to_end, sum_sem.at[1], sum_sem.at[2 + facets + b], (time, 2 * to + core)
            ).start()

    def finish(f):
        wait_bytes(got_g.at[:, these(f)], sum_sem.at[2 + facets + f])
        for c in range(2):
            fc = 2 * f + c
            total = got_g[0, fc]
            for n in range(1, groups // 2):
                total = total + got_g[n, fc]
            smooth = []
            for lt in range(2):
                here = own[:, 2 * fc + lt, :]
                down = jnp.where(time > 0, here - near[0, :, 2 * fc + lt, :], 0.0)
                up = jnp.where(time < times - 1, near[1, :, 2 * fc + lt, :] - here, 0.0)
                smooth.append(down - up)
            total = total + smoothness * jnp.concatenate(smooth, axis=1)
            data_ref[:, f, c, :] = total[:, :channels]

    below.wait()
    above.wait()
    def grads_of(f):
        return grads_even if f % 2 == 0 else grads_odd

    def sum_stations(f):
        for c in range(2):
            value = dot_nt(sums[...], grads_of(f)[c * channels : (c + 1) * channels, :])
            value = jnp.concatenate([value, jnp.zeros((64, 2 * LANES - channels), F32)], axis=1)
            value = value.reshape(groups // 2, 2, 8, 2 * LANES)
            for k in range(2):
                send_g[k, 2 * f + c] = value[:, k]

    for f in range(facets + 1):
        if f > 0:
            sum_stations(f - 1)
        if f < facets:
            for chunk in range(channels // CHUNK):
                gain_step(f, chunk, channels, degrid, left, right, error, grads_of(f), 2 * LANES)
        if f > 0:
            b = f - 1
            remote(send_g.at[1 - core, these(b)], pair_g.at[these(b)], sum_sem.at[0], sum_sem.at[2 + b], pair).start()
        if f > 1:
            combine(f - 2)
        if f > 6:
            finish(f - 7)
        if f == 5:
            third.pass_on()
    combine(facets - 1)
    for f in range(facets - 6, facets - 1):
        finish(f)
    third.wait_receive()
    grad_ref[...] = got_e[...].reshape(devices, 2, LANES)
    finish(facets - 1)

    first.wait_send()
    second.wait_send()
    third.wait_send()
    wait_bytes(gains.at[pl.ds(0, groups // 2 - 1), 0], gain_sem.at[0])
    wait_bytes(column, pair_sem.at[0])
    wait_bytes(pair_g, sum_sem.at[0])
    wait_bytes(got_g.at[pl.ds(0, groups // 2 - 1)], sum_sem.at[1])


def scatter_kernel(
    first_ref, words_ref, grad_ref, data_ref, sky_ref, data_out_ref, weight_ref, spread, cells, stage, sem, data_sem
):
    data_copy = pltpu.make_async_copy(data_ref, data_out_ref, data_sem)
    data_copy.start()
    sources = grad_ref.shape[0]
    blocks = stage.shape[1] // 8
    for b in range(blocks):
        cells[b * STRIDE : (b + 1) * STRIDE, :] = jnp.zeros((STRIDE, LANES), F32)
    spread_taps(words_ref, weight_ref)
    fold = fold_table()
    lane_quarter = (iota((sources, LANES), 1) >> 1) & 3
    for h in range(2):
        block = grad_ref[:, h, :]
        for g in range(4):
            j = 4 * h + g
            part = jnp.concatenate(halves(jnp.where(lane_quarter == g, block, 0.0)), axis=1)
            spread[j] = jnp.where(slot_quarter(words_ref, j) == lane_quarter.astype(F32), dot(part, fold), 0.0)

    @pl.loop(0, sources)
    def _(s):
        at = pl.ds(pl.multiple_of(s * 8, 8), 8)
        for j in range(8):
            cells[pl.ds(first_ref[j, s], 8), :] += weight_ref[j, at, :] * spread[j, pl.ds(s, 1), :]

    quarter = (iota((8, LANES), 1) >> 1) & 3
    last = jnp.zeros((8, LANES), F32)
    for b in range(blocks):
        pads = cells[b * STRIDE + LANES : (b + 1) * STRIDE, :]
        head = slice(b * STRIDE, b * STRIDE + 8)
        cells[head, :] = cells[head, :] + jnp.where(quarter > 0, pltpu.roll(pads, 2, 1), last)
        last = pltpu.roll(pads, LANES - 6, 1)

    pieces = sem.shape[0]
    length = blocks // pieces

    def copy(n):
        at = pl.ds(n * length * 8, length * 8)
        return pltpu.make_async_copy(stage.at[:, at, :], sky_ref.at[:, at, :], sem.at[n])

    for n in range(pieces):

        @pl.loop(n * length, (n + 1) * length, unroll=8)
        def _(b):
            turned = cells[pl.ds(pl.multiple_of(b * STRIDE, 8), LANES), :].T
            stage[:, pl.ds(pl.multiple_of(b * 8, 8), 8), :] = turned.reshape(16, 8, LANES)

        copy(n).start()
    for n in range(pieces):
        copy(n).wait()
    data_copy.wait()


def vmem(count):
    return [pl.BlockSpec(memory_space=pltpu.VMEM)] * count


def shape(dims, dtype=F32):
    return jax.ShapeDtypeStruct(dims, dtype)


def params():
    return pltpu.CompilerParams(vmem_limit_bytes=VMEM_LIMIT)


def body(
    visibilities, noise_weight, keep_flag, station_pairs, tile_owner, tile_offset, kernel_taps, gain_field, sky_grid
):
    rows = visibilities.shape[0]
    channels = visibilities.shape[2]
    devices = lax.axis_size("tm") * lax.axis_size("bl")
    parts, facets, terms, cells = sky_grid.shape
    lines = cells // LANES
    sky = sky_grid.reshape(parts, facets, terms, lines, LANES).transpose(0, 1, 3, 2, 4)
    sky = sky.reshape(parts * facets, lines * terms, LANES)

    times, groups = lax.axis_size("tm"), lax.axis_size("bl")
    singles, doubles = pltpu.VMEM((times, groups, 1, LANES), F32), pltpu.VMEM((times, groups, 2, LANES), F32)
    middle_singles = pltpu.VMEM((groups, times, 1, LANES), F32)
    middle_doubles = pltpu.VMEM((groups, times, 2, LANES), F32)
    tiles = facets * 4
    words, firsts, grad, data = pl.pallas_call(
        functools.partial(
            main_kernel, channels=channels, times=times, groups=groups
        ),
        out_shape=(
            shape((devices, LANES)), shape((8, devices), I32), shape((devices, 2, LANES)),
            shape(gain_field.shape[1:]),
        ),
        in_specs=vmem(8) + [pl.BlockSpec(memory_space=pl.ANY)],
        out_specs=tuple(vmem(4)),
        scratch_shapes=[
            singles, middle_singles, singles,
            doubles, middle_doubles, doubles,
            doubles, middle_doubles, doubles,
            pltpu.VMEM((8, tiles, LANES), F32),
            pltpu.VMEM((groups // 2, 2, 8, tiles, LANES), F32),
            pltpu.VMEM((2, 2 * facets, groups // 2, 8, 2 * LANES), F32),
            pltpu.VMEM((2 * facets, groups // 2, 8, 2 * LANES), F32),
            pltpu.VMEM((groups // 2, 2 * facets, 8, 2 * LANES), F32),
            pltpu.VMEM((groups // 2, 2 * facets, 8, 2 * LANES), F32),
            pltpu.VMEM((2, 8, tiles, LANES), F32),
            pltpu.VMEM((8, devices, rows), BF16),
            pltpu.VMEM(sky.shape, F32),
            pltpu.VMEM((cells // BLOCK * STRIDE, LANES), F32),
            pltpu.VMEM((8, devices * 8, LANES), F32),
            pltpu.VMEM((8, devices * 8, LANES), F32),
            pltpu.SMEM((8, devices), I32),
            pltpu.VMEM((rows // LANES, LANES, LANES), F32),
            pltpu.VMEM((2, 16, rows), F32),
            pltpu.VMEM((2 * facets * channels, LANES), BF16),
            pltpu.VMEM((2, LANES, rows), BF16),
            pltpu.VMEM((64, 4 * rows), BF16),
            pltpu.VMEM((1, rows), F32),
            pltpu.VMEM((2 * facets * channels, rows), F32),
            pltpu.VMEM((2 * facets * channels, rows), F32),
            pltpu.VMEM((2 * facets * channels, rows), F32),
            pltpu.VMEM((2, channels, rows), F32),
            pltpu.VMEM((2 * channels, 4 * rows), BF16),
            pltpu.VMEM((2 * channels, 4 * rows), BF16),
            pltpu.VMEM((2, 2 * facets, 8, rows), F32),
            pltpu.SemaphoreType.DMA,
            pltpu.SemaphoreType.DMA,
            pltpu.SemaphoreType.DMA((4,)),
            pltpu.SemaphoreType.DMA((4,)),
            pltpu.SemaphoreType.DMA((4,)),
            pltpu.SemaphoreType.DMA((2,)),
            pltpu.SemaphoreType.DMA((2,)),
            pltpu.SemaphoreType.DMA((4,)),
            pltpu.SemaphoreType.DMA((2 + 2 * facets,)),
        ],
        compiler_params=pltpu.CompilerParams(
            vmem_limit_bytes=62 << 20, collective_id=0, has_side_effects=True
        ),
        name="main",
    )(
        tile_owner.reshape(1, rows), tile_offset.reshape(1, rows), kernel_taps, gain_field[0],
        visibilities.transpose(1, 2, 0), noise_weight.reshape(1, rows), keep_flag.reshape(1, rows),
        station_pairs, sky,
    )

    out_grid, data = pl.pallas_call(
        scatter_kernel,
        out_shape=(shape(sky.shape), shape(data.shape)),
        in_specs=[pl.BlockSpec(memory_space=pltpu.SMEM)] + vmem(2) + [pl.BlockSpec(memory_space=pl.ANY)],
        out_specs=(pl.BlockSpec(memory_space=pl.ANY), pl.BlockSpec(memory_space=pl.ANY)),
        scratch_shapes=[
            pltpu.VMEM((8, devices * 8, LANES), F32),
            pltpu.VMEM((8, devices, LANES), F32),
            pltpu.VMEM((cells // BLOCK * STRIDE, LANES), F32),
            pltpu.VMEM(sky.shape, F32),
            pltpu.SemaphoreType.DMA((8,)),
            pltpu.SemaphoreType.DMA,
        ],
        compiler_params=params(),
        name="scatter",
    )(firsts, words, grad, data)
    grid_gradient = out_grid.reshape(parts, facets, lines, terms, LANES).transpose(0, 1, 3, 2, 4)
    grid_gradient = grid_gradient.reshape(sky_grid.shape)

    return (data[None], grid_gradient)


def solution(mesh):
    split = ("tm", "bl")
    return jax.shard_map(
        body,
        mesh=mesh,
        in_specs=(
            P(split, None, None),
            P(split),
            P(split),
            P(None, split),
            P(split, None),
            P(split),
            P(None, split),
            P("tm", "bl", None, None, None),
            P(None, None, None, split),
        ),
        out_specs=(P("tm", "bl", None, None, None), P(None, None, None, split)),
        check_vma=False,
    )
```

```python
import functools

import jax
import jax.numpy as jnp
from jax import lax
from jax.experimental import pallas as pl
from jax.experimental.pallas import tpu as pltpu
from jax.sharding import PartitionSpec as P

smoothness = 4.0
F32, BF16, I32 = jnp.float32, jnp.bfloat16, jnp.int32
LANES = 128
WORDS = 16
BLOCK = 512
STRIDE = LANES + 8
CHUNK = 16
VMEM_LIMIT = 56 << 20
NT = (((1,), (1,)), ((), ()))


def iota(shape, axis):
    return lax.broadcasted_iota(I32, shape, axis)


def halves(x):
    hi = x.astype(BF16)
    return hi, (x - hi.astype(F32)).astype(BF16)


def dot(x, y):
    return jnp.dot(x, y, preferred_element_type=F32)


def dot_nt(x, y):
    return lax.dot_general(x, y, NT, preferred_element_type=F32)


def ones_where(mask):
    return jnp.where(mask, 1.0, 0.0).astype(BF16)


def place_product(place_ref, both):
    slots, devices, rows = place_ref.shape
    product = dot_nt(place_ref[...].reshape(slots * devices, rows), both)
    return (product[:, :LANES] + product[:, LANES:]).reshape(slots, devices, LANES)


def form_slots(owner_ref, offset_ref, taps_ref, place_ref, store_message):
    devices, rows = place_ref.shape[1:]
    hits = iota((devices, rows), 0) == owner_ref[...]
    earlier = ones_where(iota((rows, rows), 0) < iota((rows, rows), 1))
    counts = dot(ones_where(hits), earlier)
    rank = jnp.sum(jnp.where(hits, counts, 0.0), axis=0, keepdims=True)
    offset = offset_ref[...]
    row = (offset >> 9) * STRIDE + (offset & (LANES - 1))
    tail = jnp.where(iota((WORDS - 8, rows), 0) == 0, row, (offset >> 7) & 3).astype(F32)
    words = jnp.concatenate([taps_ref[...], tail], axis=0)
    both = jnp.concatenate(halves(jnp.concatenate([words] * 8, axis=0)), axis=0)
    rank = jnp.where(hits, rank, -1.0)
    for j in range(8):
        place_ref[j] = ones_where(rank == float(j))
    tall = place_product(place_ref, both)
    group = iota((devices, LANES), 1) // WORDS
    message = jnp.zeros((devices, LANES), F32)
    for j in range(8):
        message = jnp.where(group == j, tall[j], message)
    store_message(message)


def transpose_grid(stage_ref, cells_ref):
    blocks = stage_ref.shape[1] // 8

    @pl.loop(0, blocks, unroll=8)
    def _(b):
        tile = stage_ref[:, pl.ds(pl.multiple_of(b * 8, 8), 8), :].reshape(LANES, LANES)
        cells_ref[pl.ds(pl.multiple_of(b * STRIDE, 8), LANES), :] = tile.T

    quarter = (iota((8, LANES), 1) >> 1) & 3
    for b in range(blocks):
        here = cells_ref[b * STRIDE : b * STRIDE + 8, :]
        next_block = min(b + 1, blocks - 1) * STRIDE
        after = cells_ref[next_block : next_block + 8, :]
        pad = jnp.where(quarter < 3, pltpu.roll(here, LANES - 2, 1), pltpu.roll(after, 6, 1))
        cells_ref[b * STRIDE + LANES : (b + 1) * STRIDE, :] = pad


def spread_taps(words_ref, weight_ref):
    sources = words_ref.shape[0]
    tall = jnp.broadcast_to(words_ref[...].reshape(sources, 1, LANES), (sources, 8, LANES)).reshape(8 * sources, LANES)
    tall = jnp.where((iota(tall.shape, 1) & (WORDS - 1)) == (iota(tall.shape, 0) & 7), tall, 0.0)
    both = jnp.concatenate(halves(tall), axis=1)
    for pair in range(4):
        a, b = iota((2 * LANES, 2 * LANES), 0) & (LANES - 1), iota((2 * LANES, 2 * LANES), 1)
        weight = dot(both, ones_where(a // WORDS == 2 * pair + b // LANES))
        for n in range(2):
            weight_ref[2 * pair + n] = weight[:, n * LANES : (n + 1) * LANES]


def slot_quarter(words_ref, j):
    return jnp.broadcast_to(words_ref[:, j * WORDS + 9 : j * WORDS + 10], (words_ref.shape[0], LANES))


def fold_table():
    a, b = iota((2 * LANES, LANES), 0) & (LANES - 1), iota((2 * LANES, LANES), 1)
    return ones_where(((a >> 3) == (b >> 3)) & ((a & 1) == (b & 1)))


def degrid_slots(first_ref, words_ref, cells_ref, weight_ref, product_ref, store_value):
    sources = words_ref.shape[0]

    @pl.loop(0, sources, unroll=8)
    def _(s):
        at = pl.ds(pl.multiple_of(s * 8, 8), 8)
        for j in range(8):
            product_ref[j, at, :] = weight_ref[j, at, :] * cells_ref[pl.ds(first_ref[j, s], 8), :]

    fold = fold_table()
    lane_quarter = (iota((sources, LANES), 1) >> 1) & 3
    for h in range(2):
        value = jnp.zeros((sources, LANES), F32)
        for g in range(4):
            j = 4 * h + g
            total = product_ref[j, pl.ds(0, sources, stride=8), :]
            for k in range(1, 8):
                total = total + product_ref[j, pl.ds(k, sources, stride=8), :]
            total = jnp.where(slot_quarter(words_ref, j) == lane_quarter.astype(F32), total, 0.0)
            value = jnp.where(lane_quarter == g, dot(jnp.concatenate(halves(total), axis=1), fold), value)
        store_value(h, value)


def gather_degrid(load_value, place_ref, part_ref, degrid_ref):
    sources = place_ref.shape[1]
    quarter = (iota((LANES, sources), 0) >> 1) & 3
    total = None
    for h in range(2):
        turned = load_value(h).T
        for pair in range(2):
            parts = [halves(jnp.where(quarter == g, turned, 0.0)) for g in (2 * pair, 2 * pair + 1)]
            j = 4 * h + 2 * pair
            place = place_ref[j : j + 2].reshape(2 * sources, place_ref.shape[2])
            for n in range(2):
                term = dot(jnp.concatenate([parts[0][n], parts[1][n]], axis=1), place)
                total = term if total is None else total + term
    for n in range(part_ref.shape[0]):
        tile = slice(n * LANES, (n + 1) * LANES)
        part_ref[n] = total[:, tile]
        for t in range(2):
            degrid_ref[t, :, tile] = sum(part_ref[n, pl.ds(2 * g + t, 16, stride=8), :] for g in range(4))


def station_tables(pairs_ref, gather_ref, sum_ref):
    rows = pairs_ref.shape[1]
    for side in range(2):
        hits = ones_where((iota((LANES, rows), 0) & 63) == pairs_ref[side : side + 1, :])
        gather_ref[side] = hits
        for n in range(2):
            sum_ref[:, (2 * side + n) * rows : (2 * side + n + 1) * rows] = hits[:64]


def turn_gains(gains_ref, turned_ref, channels):
    for fc in range(16):
        tiles = []
        for lt in range(2):
            block = gains_ref[:, :, :, 2 * fc + lt, :].reshape(64, LANES)
            hi = block.astype(BF16).astype(F32)
            tiles.append(jnp.concatenate([hi, block - hi], axis=0).T)
        turned_ref[fc * channels : (fc + 1) * channels] = jnp.concatenate(tiles, axis=0)[:channels].astype(BF16)


def gather_gains(turned_ref, gather_ref, left_ref, right_ref, first, last):
    size = turned_ref.shape[0] // 3

    @pl.loop(first, last)
    def _(n):
        at = pl.ds(pl.multiple_of(n * size, CHUNK), size)
        gains = turned_ref[at, :]
        left_ref[at, :] = dot(gains, gather_ref[0])
        right_ref[at, :] = dot(gains, gather_ref[1])


def chunk_rows(plane, channels, chunk):
    if isinstance(chunk, int):
        return pl.ds(plane * channels + chunk * CHUNK, CHUNK)
    return pl.ds(pl.multiple_of(plane * channels + chunk * CHUNK, CHUNK), CHUNK)


def channel_ramp(channels, chunk, width):
    channel = (iota((CHUNK, width), 0) + chunk * CHUNK).astype(F32)
    return 2.0 * channel / (channels - 1) - 1.0


def facet_model(degrid_ref, f, lanes, ramp):
    g = degrid_ref.shape[1] // 2 + f
    return tuple(degrid_ref[0, n : n + 1, lanes] + degrid_ref[1, n : n + 1, lanes] * ramp for n in (f, g))


def pair_step(chunk, channels, left_ref, right_ref, pair_ref, facets, width=LANES):
    for f in range(facets):
        re, im = chunk_rows(2 * f, channels, chunk), chunk_rows(2 * f + 1, channels, chunk)
        for first in range(0, left_ref.shape[1], width):
            lanes = slice(first, first + width)
            are, aim, bre, bim = left_ref[re, lanes], left_ref[im, lanes], right_ref[re, lanes], right_ref[im, lanes]
            pair_ref[re, lanes] = are * bre + aim * bim
            pair_ref[im, lanes] = aim * bre - are * bim


def error_step(
    chunk, channels, vis_ref, scale_ref, degrid_ref, pair_ref, error_ref, grad_degrid_ref, width=LANES
):
    rows = vis_ref.shape[2]
    facets = degrid_ref.shape[1] // 2
    at = chunk_rows(0, channels, chunk)
    ramp = channel_ramp(channels, chunk, width)
    for first in range(0, rows, width):
        lanes = slice(first, first + width)
        pred_re = pred_im = None
        for f in range(facets):
            re, im = chunk_rows(2 * f, channels, chunk), chunk_rows(2 * f + 1, channels, chunk)
            pre, pim = pair_ref[re, lanes], pair_ref[im, lanes]
            mre, mim = facet_model(degrid_ref, f, lanes, ramp)
            vre, vim = pre * mre - pim * mim, pre * mim + pim * mre
            pred_re = vre if pred_re is None else pred_re + vre
            pred_im = vim if pred_im is None else pred_im + vim
        ere = scale_ref[:, lanes] * (pred_re - vis_ref[0, at, lanes].astype(F32))
        eim = scale_ref[:, lanes] * (pred_im - vis_ref[1, at, lanes].astype(F32))
        error_ref[0, at, lanes] = ere
        error_ref[1, at, lanes] = eim
        for f in range(facets):
            re, im = chunk_rows(2 * f, channels, chunk), chunk_rows(2 * f + 1, channels, chunk)
            pre, pim = pair_ref[re, lanes], pair_ref[im, lanes]
            models = (ere * pre + eim * pim, eim * pre - ere * pim)
            for c in range(2):
                n = c * facets + f
                slope = models[c] * ramp
                grad_degrid_ref[0, n, :, lanes] += models[c][:8] + models[c][8:]
                grad_degrid_ref[1, n, :, lanes] += slope[:8] + slope[8:]


def gain_step(f, chunk, channels, degrid_ref, left_ref, right_ref, error_ref, grads_ref, width=LANES):
    rows = error_ref.shape[2]
    at = chunk_rows(0, channels, chunk)
    ramp = channel_ramp(channels, chunk, width)
    re, im = chunk_rows(2 * f, channels, chunk), chunk_rows(2 * f + 1, channels, chunk)
    for first in range(0, rows, width):
        lanes = slice(first, first + width)
        are, aim, bre, bim = left_ref[re, lanes], left_ref[im, lanes], right_ref[re, lanes], right_ref[im, lanes]
        mre, mim = facet_model(degrid_ref, f, lanes, ramp)
        ere, eim = error_ref[0, at, lanes], error_ref[1, at, lanes]
        qre, qim = ere * mre + eim * mim, eim * mre - ere * mim
        values = (
            (qre * bre - qim * bim, qre * bim + qim * bre),
            (qre * are + qim * aim, qre * aim - qim * are),
        )
        for side in range(2):
            for c in range(2):
                hi, lo = halves(values[side][c])
                start = 2 * side * rows + first
                grads_ref[chunk_rows(c, channels, chunk), start : start + width] = hi
                grads_ref[chunk_rows(c, channels, chunk), start + rows : start + rows + width] = lo


def place_grads(grad_degrid_ref, place_ref, store_value):
    planes = grad_degrid_ref.shape[1]
    rows = grad_degrid_ref.shape[3]
    devices = place_ref.shape[1]
    odd = (iota((8, rows), 0) & 1) == 1
    full = []
    for n in range(planes):
        level = jnp.sum(grad_degrid_ref[0, n], axis=0, keepdims=True)
        slope = jnp.sum(grad_degrid_ref[1, n], axis=0, keepdims=True)
        full.append(jnp.where(odd, slope, level))
    tall = place_product(place_ref, jnp.concatenate(halves(jnp.concatenate(full, axis=0)), axis=0))
    group = (iota((devices, LANES), 1) >> 1) & 3
    for h in range(2):
        value = tall[4 * h]
        for g in range(1, 4):
            value = jnp.where(group == g, tall[4 * h + g], value)
        store_value(h, value)


class Exchange:
    def __init__(self, send_ref, middle_ref, receive_ref, sems, time, group):
        self.send_ref, self.middle_ref, self.receive_ref, self.sems = send_ref, middle_ref, receive_ref, sems
        self.time, self.group = time, group
        self.times, self.groups = send_ref.shape[:2]

    def start(self):
        to_middle = self.middle_ref.at[:, self.time]
        pltpu.make_async_copy(self.send_ref.at[self.time], to_middle, self.sems.at[1]).start()

        @pl.loop(1, self.times)
        def _(n):
            to = lax.rem(self.time + n, self.times)
            remote(self.send_ref.at[to], to_middle, self.sems.at[0], self.sems.at[1], (to, self.group)).start()

    def pass_on(self):
        wait_bytes(self.middle_ref, self.sems.at[1])
        to_end = self.receive_ref.at[:, self.group]
        pltpu.make_async_copy(self.middle_ref.at[self.group], to_end, self.sems.at[3]).start()

        @pl.loop(1, self.groups)
        def _(n):
            to = lax.rem(self.group + n, self.groups)
            remote(self.middle_ref.at[to], to_end, self.sems.at[2], self.sems.at[3], (self.time, to)).start()

    def wait_receive(self):
        wait_bytes(self.receive_ref, self.sems.at[3])

    def wait_send(self):
        wait_bytes(self.send_ref.at[pl.ds(0, self.times - 1)], self.sems.at[0])
        wait_bytes(self.middle_ref.at[pl.ds(0, self.groups - 1)], self.sems.at[2])


def remote(source, target, send_sem, receive_sem, device):
    return pltpu.make_async_remote_copy(
        src_ref=source, dst_ref=target, send_sem=send_sem, recv_sem=receive_sem,
        device_id=device, device_id_type=pl.DeviceIdType.MESH,
    )


def wait_bytes(ref, sem):
    pltpu.make_async_copy(ref, ref, sem).wait()


def main_kernel(
    owner_ref, offset_ref, taps_ref, gain_ref, vis_ref, noise_ref, keep_ref, pairs_ref, sky_ref,
    words_ref, firsts_ref, grad_ref, data_ref,
    send_a, mid_a, got_a, send_c, mid_c, got_c, send_e, mid_e, got_e, own, gains, send_g, pair_g, sum_g, got_g, near,
    place, stage, cells, weight, product, slots, part, degrid, turned, gather, sums, scale,
    left, right, pairs, error, grads_even, grads_odd, grad_degrid,
    sky_sem, slot_sem, sem_a, sem_c, sem_e, gain_sem, pair_sem, near_sem, sum_sem,
    channels, times, groups,
):
    time, group = lax.axis_index("tm"), lax.axis_index("bl")
    devices = times * groups
    level, core = group // 2, lax.rem(group, 2)
    facets = gain_ref.shape[1]
    barrier = pltpu.get_barrier_semaphore()

    @pl.loop(1, times)
    def _(n):
        to = (lax.rem(time + n, times), group)
        pl.semaphore_signal(barrier, inc=1, device_id=to, device_id_type=pl.DeviceIdType.MESH)

    @pl.loop(1, groups)
    def _(n):
        to = (time, lax.rem(group + n, groups))
        pl.semaphore_signal(barrier, inc=1, device_id=to, device_id_type=pl.DeviceIdType.MESH)

    sky_copy = pltpu.make_async_copy(sky_ref, stage, sky_sem)
    sky_copy.start()

    def store_message(message):
        for t in range(devices):
            send_a[t // groups, t % groups] = message[t : t + 1, :]

    form_slots(owner_ref, offset_ref, taps_ref, place, store_message)
    pl.semaphore_wait(barrier, times + groups - 2)

    first = Exchange(send_a, mid_a, got_a, sem_a, time, group)
    second = Exchange(send_c, mid_c, got_c, sem_c, time, group)
    third = Exchange(send_e, mid_e, got_e, sem_e, time, group)
    first.start()

    for f in range(facets):
        for c in range(2):
            for lt in range(2):
                wide = min(LANES, channels - lt * LANES)
                block = gain_ref[:, f, c, lt * LANES : lt * LANES + wide]
                if wide < LANES:
                    block = jnp.concatenate([block, jnp.zeros((block.shape[0], LANES - wide), F32)], axis=1)
                own[:, 4 * f + 2 * c + lt, :] = block
    mine = gains.at[level, core]
    pltpu.make_async_copy(own, mine, gain_sem.at[1]).start()

    @pl.loop(1, groups // 2)
    def _(n):
        to = lax.rem(group + 2 * n, groups)
        remote(own, mine, gain_sem.at[0], gain_sem.at[1], (time, to)).start()

    sky_copy.wait()
    transpose_grid(stage, cells)
    first.pass_on()
    scale[...] = noise_ref[...] * keep_ref[...].astype(F32)
    station_tables(pairs_ref, gather, sums)
    grad_degrid[...] = jnp.zeros_like(grad_degrid)

    first.wait_receive()
    words_ref[...] = got_a[...].reshape(devices, LANES)
    turned_words = words_ref[...].T
    firsts = jnp.concatenate([turned_words[j * WORDS + 8 : j * WORDS + 9, :] for j in range(8)], axis=0)
    firsts_ref[...] = jnp.clip(firsts.astype(I32), 0, cells.shape[0] - 8)
    slot_copy = pltpu.make_async_copy(firsts_ref, slots, slot_sem)
    slot_copy.start()
    spread_taps(words_ref, weight)
    column = gains.at[:, core]
    pair = (time, group + 1 - 2 * core)
    wait_bytes(column, gain_sem.at[1])
    remote(column, column, pair_sem.at[0], pair_sem.at[1], pair).start()
    slot_copy.wait()

    def store_value(h, value):
        send_c[:, :, h, :] = value.reshape(times, groups, LANES)

    degrid_slots(slots, words_ref, cells, weight, product, store_value)
    second.start()
    wait_bytes(column, pair_sem.at[1])
    turn_gains(gains, turned, channels)
    gather_gains(turned, gather, left, right, 0, 2)
    second.pass_on()
    def next_interval(n, step):
        to = lax.rem(time + step, times)
        return remote(own, near.at[n], near_sem.at[2 * n], near_sem.at[2 * n + 1], (to, group))

    below, above = next_interval(0, 1), next_interval(1, times - 1)
    below.start()
    above.start()
    gather_gains(turned, gather, left, right, 2, 3)

    @pl.loop(0, channels // CHUNK)
    def _(chunk):
        pair_step(chunk, channels, left, right, pairs, facets, 2 * LANES)

    second.wait_receive()
    gather_degrid(lambda h: got_c[:, :, h, :].reshape(devices, LANES), place, part, degrid)

    @pl.loop(0, channels // CHUNK, unroll=3)
    def _(chunk):
        error_step(chunk, channels, vis_ref, scale, degrid, pairs, error, grad_degrid, 2 * LANES)

    def store_grad(h, value):
        send_e[:, :, h, :] = value.reshape(times, groups, LANES)

    place_grads(grad_degrid, place, store_grad)
    third.start()

    batch = 2

    def these(b):
        return pl.ds(b * batch, batch)

    def combine(b):
        wait_bytes(pair_g.at[these(b)], sum_sem.at[2 + b])
        for fc in range(b * batch, (b + 1) * batch):
            sum_g[:, fc] = send_g[core, fc] + pair_g[fc]
        to_end = got_g.at[level, these(b)]
        pltpu.make_async_copy(sum_g.at[level, these(b)], to_end, sum_sem.at[2 + facets + b]).start()

        for n in range(1, groups // 2):
            to = lax.rem(level + n, groups // 2)
            remote(
                sum_g.at[to, these(b)], to_end, sum_sem.at[1], sum_sem.at[2 + facets + b], (time, 2 * to + core)
            ).start()

    def finish(f):
        wait_bytes(got_g.at[:, these(f)], sum_sem.at[2 + facets + f])
        for c in range(2):
            fc = 2 * f + c
            total = got_g[0, fc]
            for n in range(1, groups // 2):
                total = total + got_g[n, fc]
            smooth = []
            for lt in range(2):
                here = own[:, 2 * fc + lt, :]
                down = jnp.where(time > 0, here - near[0, :, 2 * fc + lt, :], 0.0)
                up = jnp.where(time < times - 1, near[1, :, 2 * fc + lt, :] - here, 0.0)
                smooth.append(down - up)
            total = total + smoothness * jnp.concatenate(smooth, axis=1)
            data_ref[:, f, c, :] = total[:, :channels]

    below.wait()
    above.wait()
    def grads_of(f):
        return grads_even if f % 2 == 0 else grads_odd

    def sum_stations(f):
        for c in range(2):
            value = dot_nt(sums[...], grads_of(f)[c * channels : (c + 1) * channels, :])
            value = jnp.concatenate([value, jnp.zeros((64, 2 * LANES - channels), F32)], axis=1)
            value = value.reshape(groups // 2, 2, 8, 2 * LANES)
            for k in range(2):
                send_g[k, 2 * f + c] = value[:, k]

    for f in range(facets + 1):
        if f > 0:
            sum_stations(f - 1)
        if f < facets:
            for chunk in range(channels // CHUNK):
                gain_step(f, chunk, channels, degrid, left, right, error, grads_of(f), 2 * LANES)
        if f > 0:
            b = f - 1
            remote(send_g.at[1 - core, these(b)], pair_g.at[these(b)], sum_sem.at[0], sum_sem.at[2 + b], pair).start()
        if f > 1:
            combine(f - 2)
        if f > 6:
            finish(f - 7)
        if f == 5:
            third.pass_on()
    combine(facets - 1)
    for f in range(facets - 6, facets - 1):
        finish(f)
    third.wait_receive()
    grad_ref[...] = got_e[...].reshape(devices, 2, LANES)
    finish(facets - 1)

    first.wait_send()
    second.wait_send()
    third.wait_send()
    wait_bytes(gains.at[pl.ds(0, groups // 2 - 1), 0], gain_sem.at[0])
    wait_bytes(column, pair_sem.at[0])
    wait_bytes(pair_g, sum_sem.at[0])
    wait_bytes(got_g.at[pl.ds(0, groups // 2 - 1)], sum_sem.at[1])


def scatter_kernel(
    first_ref, words_ref, grad_ref, data_ref, sky_ref, data_out_ref, weight_ref, spread, cells, stage, sem, data_sem
):
    data_copy = pltpu.make_async_copy(data_ref, data_out_ref, data_sem)
    data_copy.start()
    sources = grad_ref.shape[0]
    blocks = stage.shape[1] // 8
    for b in range(blocks):
        cells[b * STRIDE : (b + 1) * STRIDE, :] = jnp.zeros((STRIDE, LANES), F32)
    spread_taps(words_ref, weight_ref)
    fold = fold_table()
    lane_quarter = (iota((sources, LANES), 1) >> 1) & 3
    for h in range(2):
        block = grad_ref[:, h, :]
        for g in range(4):
            j = 4 * h + g
            part = jnp.concatenate(halves(jnp.where(lane_quarter == g, block, 0.0)), axis=1)
            spread[j] = jnp.where(slot_quarter(words_ref, j) == lane_quarter.astype(F32), dot(part, fold), 0.0)

    @pl.loop(0, sources)
    def _(s):
        at = pl.ds(pl.multiple_of(s * 8, 8), 8)
        for j in range(8):
            cells[pl.ds(first_ref[j, s], 8), :] += weight_ref[j, at, :] * spread[j, pl.ds(s, 1), :]

    quarter = (iota((8, LANES), 1) >> 1) & 3
    last = jnp.zeros((8, LANES), F32)
    for b in range(blocks):
        pads = cells[b * STRIDE + LANES : (b + 1) * STRIDE, :]
        head = slice(b * STRIDE, b * STRIDE + 8)
        cells[head, :] = cells[head, :] + jnp.where(quarter > 0, pltpu.roll(pads, 2, 1), last)
        last = pltpu.roll(pads, LANES - 6, 1)

    pieces = sem.shape[0]
    length = blocks // pieces

    def copy(n):
        at = pl.ds(n * length * 8, length * 8)
        return pltpu.make_async_copy(stage.at[:, at, :], sky_ref.at[:, at, :], sem.at[n])

    for n in range(pieces):

        @pl.loop(n * length, (n + 1) * length, unroll=8)
        def _(b):
            turned = cells[pl.ds(pl.multiple_of(b * STRIDE, 8), LANES), :].T
            stage[:, pl.ds(pl.multiple_of(b * 8, 8), 8), :] = turned.reshape(16, 8, LANES)

        copy(n).start()
    for n in range(pieces):
        copy(n).wait()
    data_copy.wait()


def vmem(count):
    return [pl.BlockSpec(memory_space=pltpu.VMEM)] * count


def shape(dims, dtype=F32):
    return jax.ShapeDtypeStruct(dims, dtype)


def params():
    return pltpu.CompilerParams(vmem_limit_bytes=VMEM_LIMIT)


def body(
    visibilities, noise_weight, keep_flag, station_pairs, tile_owner, tile_offset, kernel_taps, gain_field, sky_grid
):
    rows = visibilities.shape[0]
    channels = visibilities.shape[2]
    devices = lax.axis_size("tm") * lax.axis_size("bl")
    parts, facets, terms, cells = sky_grid.shape
    lines = cells // LANES
    sky = sky_grid.reshape(parts, facets, terms, lines, LANES).transpose(0, 1, 3, 2, 4)
    sky = sky.reshape(parts * facets, lines * terms, LANES)

    times, groups = lax.axis_size("tm"), lax.axis_size("bl")
    singles, doubles = pltpu.VMEM((times, groups, 1, LANES), F32), pltpu.VMEM((times, groups, 2, LANES), F32)
    middle_singles = pltpu.VMEM((groups, times, 1, LANES), F32)
    middle_doubles = pltpu.VMEM((groups, times, 2, LANES), F32)
    tiles = facets * 4
    words, firsts, grad, data = pl.pallas_call(
        functools.partial(
            main_kernel, channels=channels, times=times, groups=groups
        ),
        out_shape=(
            shape((devices, LANES)), shape((8, devices), I32), shape((devices, 2, LANES)),
            shape(gain_field.shape[1:]),
        ),
        in_specs=vmem(8) + [pl.BlockSpec(memory_space=pl.ANY)],
        out_specs=tuple(vmem(4)),
        scratch_shapes=[
            singles, middle_singles, singles,
            doubles, middle_doubles, doubles,
            doubles, middle_doubles, doubles,
            pltpu.VMEM((8, tiles, LANES), F32),
            pltpu.VMEM((groups // 2, 2, 8, tiles, LANES), F32),
            pltpu.VMEM((2, 2 * facets, groups // 2, 8, 2 * LANES), F32),
            pltpu.VMEM((2 * facets, groups // 2, 8, 2 * LANES), F32),
            pltpu.VMEM((groups // 2, 2 * facets, 8, 2 * LANES), F32),
            pltpu.VMEM((groups // 2, 2 * facets, 8, 2 * LANES), F32),
            pltpu.VMEM((2, 8, tiles, LANES), F32),
            pltpu.VMEM((8, devices, rows), BF16),
            pltpu.VMEM(sky.shape, F32),
            pltpu.VMEM((cells // BLOCK * STRIDE, LANES), F32),
            pltpu.VMEM((8, devices * 8, LANES), F32),
            pltpu.VMEM((8, devices * 8, LANES), F32),
            pltpu.SMEM((8, devices), I32),
            pltpu.VMEM((rows // LANES, LANES, LANES), F32),
            pltpu.VMEM((2, 16, rows), F32),
            pltpu.VMEM((2 * facets * channels, LANES), BF16),
            pltpu.VMEM((2, LANES, rows), BF16),
            pltpu.VMEM((64, 4 * rows), BF16),
            pltpu.VMEM((1, rows), F32),
            pltpu.VMEM((2 * facets * channels, rows), F32),
            pltpu.VMEM((2 * facets * channels, rows), F32),
            pltpu.VMEM((2 * facets * channels, rows), F32),
            pltpu.VMEM((2, channels, rows), F32),
            pltpu.VMEM((2 * channels, 4 * rows), BF16),
            pltpu.VMEM((2 * channels, 4 * rows), BF16),
            pltpu.VMEM((2, 2 * facets, 8, rows), F32),
            pltpu.SemaphoreType.DMA,
            pltpu.SemaphoreType.DMA,
            pltpu.SemaphoreType.DMA((4,)),
            pltpu.SemaphoreType.DMA((4,)),
            pltpu.SemaphoreType.DMA((4,)),
            pltpu.SemaphoreType.DMA((2,)),
            pltpu.SemaphoreType.DMA((2,)),
            pltpu.SemaphoreType.DMA((4,)),
            pltpu.SemaphoreType.DMA((2 + 2 * facets,)),
        ],
        compiler_params=pltpu.CompilerParams(
            vmem_limit_bytes=62 << 20, collective_id=0, has_side_effects=True
        ),
        name="main",
    )(
        tile_owner.reshape(1, rows), tile_offset.reshape(1, rows), kernel_taps, gain_field[0],
        visibilities.transpose(1, 2, 0), noise_weight.reshape(1, rows), keep_flag.reshape(1, rows),
        station_pairs, sky,
    )

    out_grid, data = pl.pallas_call(
        scatter_kernel,
        out_shape=(shape(sky.shape), shape(data.shape)),
        in_specs=[pl.BlockSpec(memory_space=pltpu.SMEM)] + vmem(2) + [pl.BlockSpec(memory_space=pl.ANY)],
        out_specs=(pl.BlockSpec(memory_space=pl.ANY), pl.BlockSpec(memory_space=pl.ANY)),
        scratch_shapes=[
            pltpu.VMEM((8, devices * 8, LANES), F32),
            pltpu.VMEM((8, devices, LANES), F32),
            pltpu.VMEM((cells // BLOCK * STRIDE, LANES), F32),
            pltpu.VMEM(sky.shape, F32),
            pltpu.SemaphoreType.DMA((8,)),
            pltpu.SemaphoreType.DMA,
        ],
        compiler_params=params(),
        name="scatter",
    )(firsts, words, grad, data)
    grid_gradient = out_grid.reshape(parts, facets, lines, terms, LANES).transpose(0, 1, 3, 2, 4)
    grid_gradient = grid_gradient.reshape(sky_grid.shape)

    return (data[None], grid_gradient)


def solution(mesh):
    split = ("tm", "bl")
    return jax.shard_map(
        body,
        mesh=mesh,
        in_specs=(
            P(split, None, None),
            P(split),
            P(split),
            P(None, split),
            P(split, None),
            P(split),
            P(None, split),
            P("tm", "bl", None, None, None),
            P(None, None, None, split),
        ),
        out_specs=(P("tm", "bl", None, None, None), P(None, None, None, split)),
        check_vma=False,
    )
```
